32 devices in a mesh: rows: 8 (over z, x), wide: 4 (over y, core).
Axes of the slice: x: 2, y: 2, z: 4, core: 2. Of those that a mesh axis runs over, the one named last changes fastest.
Arguments:
- hidden_in: bfloat16 [1024, 16, 1024], P('wide', 'rows'), may hold values from -6 to 6
- segments: int32 [16, 1024], P('rows'), may hold values from 0 to 3, never falling along the last dimension, each value on 1 to 768 neighbouring positions
- prefix_vis: int32 [16, 64], P('rows'), may hold values 0 or 1
- prefix_key: bfloat16 [64, 1024], replicated, may hold values from -6 to 6
- prefix_value: bfloat16 [64, 1024], replicated, may hold values from -6 to 6
- w_query: bfloat16 [1024, 1024], replicated, may hold values from -0.375 to 0.375
- w_key: bfloat16 [1024, 1024], replicated, may hold values from -0.1875 to 0.1875
- w_value: bfloat16 [1024, 1024], replicated, may hold values from -0.1875 to 0.1875
- w_out: bfloat16 [1024, 1024], replicated, may hold values from -4 to 4
- norm1_gain: float32 [1024], replicated, may hold values from 0.1 to 1.9
- norm1_bias: float32 [1024], replicated, may hold values from -3 to 3
- w_up: bfloat16 [1024, 4096], P(None, 'wide'), may hold values from -0.1875 to 0.1875
- w_down: bfloat16 [4096, 1024], P('wide'), may hold values from -0.09375 to 0.09375
- norm2_gain: float32 [1024], replicated, may hold values from 0.1 to 1.9
- norm2_bias: float32 [1024], replicated, may hold values from -3 to 3
- out_grad: float32 [1024, 16, 1024], P('wide', 'rows'), may hold values from -6 to 6
Outputs:
- block_out: bfloat16 [1024, 16, 1024], P('wide', 'rows')
- input_grad: float32 [1024, 16, 1024], P('wide', 'rows')
- prefix_key_grad: float32 [64, 1024], replicated
- prefix_value_grad: float32 [64, 1024], replicated
The draws below stay inside these ranges and needn't reach their ends.
Inputs may be any that keep to these rules, and one draw needn't show every extreme that they name: `segments`: in each row the segment ids never fall, and a segment holds at most 768 positions.
All inputs are finite; a program needn't handle non-finite values. No bound on the sum of `prefix_vis` on one device may be relied on, other than what follows from the above.
Results may differ from the reference program's by a relative error of at most 0.014.
The reference program's roundings to bfloat16 on the way count: a program that leaves them out, or rounds other values in their place, can miss the bound.
Values may be sent and summed in bfloat16 or wider, within the bound.
A program may use at most 256 MiB of HBM per device.

```python
import math
import jax
import jax.numpy as jnp
import numpy as np
from jax import lax

D = 1024
H = 16
E = 64
FF = 4096
P_SIZE = 64
LEN = 1024
ROWS = 16


def set_ends(array, rng, smallest, largest):
    index_at = [jax.random.randint(jax.random.fold_in(rng, axis), (), 0, length) for axis, length in enumerate(array.shape)]
    main_axis = array.shape.index(max(array.shape))
    beside = index_at[:main_axis] + [(index_at[main_axis] + 1) % array.shape[main_axis]] + index_at[main_axis + 1:]
    return array.at[tuple(index_at)].set(smallest).at[tuple(beside)].set(largest)


def shard_levels(rng, extent, cuts, least, largest):
    level, own = 1.0, jax.random.fold_in(rng, 6)
    for dim, shards_of in cuts:
        draws = jnp.exp(jax.random.uniform(jax.random.fold_in(own, dim), (shards_of,), jnp.float32, least / len(cuts), largest / len(cuts)))
        level = level * jnp.repeat(draws, extent[dim] // shards_of).reshape([-1 if axis == dim else 1 for axis in range(len(extent))])
    return level


def length_profile(amount, total, bound, lean):
    weights = [(1 << 20) // math.isqrt(standing ** lean) + 1 for standing in range(2, amount + 1)]
    rest, holding = total - bound - (amount - 1), [1] * (amount - 1)
    while rest > 0:
        free = [i for i in range(amount - 1) if holding[i] < bound]
        whole, left = sum([weights[i] for i in free]), rest
        for i in free:
            addition = min(bound - holding[i], max(1, left * weights[i] // whole), rest)
            holding[i] = holding[i] + addition
            rest = rest - addition
    return np.array([bound] + holding)


def uneven(stream_key, amount, total, most, skew):
    if amount == 2:
        one = jax.random.randint(stream_key, (), max(1, total - most), min(most, total - 1) + 1)
        return jnp.stack([one, total - one])
    sizes = jnp.asarray(length_profile(amount, total, most, skew), jnp.int32)
    couples = (amount - 1) // 2
    source_of, receiver = sizes[1:1 + 2 * couples:2], sizes[2:2 + 2 * couples:2]
    room = jnp.minimum(source_of - 1, most - receiver)
    passed = jax.random.randint(jax.random.fold_in(stream_key, 1), (couples,), 0, 1 << 20) % (room + 1)
    sizes = sizes.at[1:1 + 2 * couples:2].set(source_of - passed).at[2:2 + 2 * couples:2].set(receiver + passed)
    return sizes[jax.random.permutation(jax.random.fold_in(stream_key, 2), amount)]


def bell_draw(stream_key, dims, spread, limit, shards=(), dtype=jnp.bfloat16):
    values = jax.random.normal(stream_key, dims, jnp.float32) * spread
    if len(shards) > 0:
        values = shard_levels(stream_key, dims, shards, -0.22, 0.18) * values
    return jnp.clip(values, min=-limit, max=limit).astype(dtype)


def setup_inputs(seed: int = 0) -> dict:
    splits = jax.random.split(jax.random.key(seed), 17)
    hidden_in = bell_draw(splits[0], (LEN, ROWS, D), 1.0, 6.0, ((0, 4), (1, 8)))
    segments = jax.vmap(lambda own: jnp.searchsorted(jnp.cumsum(uneven(own, 4, LEN, 3 * LEN // 4, 0)), jnp.arange(LEN), side="right"))(jax.random.split(splits[1], ROWS)).reshape((ROWS, LEN)).astype(jnp.int32)
    prefix_vis = set_ends((jax.random.randint(splits[2], (ROWS, P_SIZE), 0, 4) < 3).astype(jnp.int32), jax.random.fold_in(splits[2], 1), 0, 1)
    prefix_key = bell_draw(splits[3], (P_SIZE, D), 1.0, 6.0)
    prefix_value = bell_draw(splits[4], (P_SIZE, D), 1.0, 6.0)
    w_query = bell_draw(splits[5], (D, D), (D // 4) ** -0.5, 0.375)
    w_key = bell_draw(splits[6], (D, D), D ** -0.5, 0.1875)
    w_value = bell_draw(splits[7], (D, D), D ** -0.5, 0.1875)
    w_out = bell_draw(splits[8], (D, D), (max(1, 2 * D // LEN)) ** -0.5, 4.0)
    norm1_gain = jnp.clip(1.0 + 0.18 * jax.random.normal(splits[9], (D,), jnp.float32), 0.1, 1.9)
    norm1_bias = bell_draw(splits[10], (D,), 0.5, 3.0, (), jnp.float32)
    w_up = bell_draw(splits[11], (D, FF), D ** -0.5, 0.1875, ((1, 4),))
    w_down = bell_draw(splits[12], (FF, D), FF ** -0.5, 0.09375, ((0, 4),))
    norm2_gain = jnp.clip(1.0 + 0.18 * jax.random.normal(splits[13], (D,), jnp.float32), 0.1, 1.9)
    norm2_bias = bell_draw(splits[14], (D,), 0.5, 3.0, (), jnp.float32)
    out_grad = bell_draw(splits[15], (LEN, ROWS, D), 1.0, 6.0, ((0, 4), (1, 8)), jnp.float32)
    return {"hidden_in": hidden_in, "segments": segments, "prefix_vis": prefix_vis, "prefix_key": prefix_key, "prefix_value": prefix_value, "w_query": w_query, "w_key": w_key, "w_value": w_value, "w_out": w_out, "norm1_gain": norm1_gain, "norm1_bias": norm1_bias, "w_up": w_up, "w_down": w_down, "norm2_gain": norm2_gain, "norm2_bias": norm2_bias, "out_grad": out_grad}


@jax.custom_vjp
def low(v):
    return lax.optimization_barrier(v.astype(jnp.bfloat16)).astype(jnp.float32)

@jax.custom_vjp
def low_back(v):
    return v

def low_keep(v):
    return (low(v), None)

def low_pass(kept, grad):
    return (grad,)

def back_keep(v):
    return (v, None)

def back_low(kept, grad):
    return (low(grad),)
low.defvjp(low_keep, low_pass)
low_back.defvjp(back_keep, back_low)
norm_eps = 1e-05
neg_large = -1e+30
highest = lax.Precision.HIGHEST

def layer_norm(summed, norm_gain, norm_bias):
    average = lax.optimization_barrier(jnp.mean(summed, axis=-1, keepdims=True))
    centred = summed - average
    variance = lax.optimization_barrier(jnp.mean(centred * centred, axis=-1, keepdims=True))
    return centred * lax.rsqrt(variance + norm_eps) * norm_gain + norm_bias

def row_forward(weights, row_in, row_seg, row_vis, prefix_keys, prefix_vals):
    w_query, w_key, w_value, w_out, gain_one, bias_one, w_up, w_down, gain_two, bias_two = weights
    seq_len = row_in.shape[0]
    queries = low(low_back(jnp.dot(row_in, w_query, precision=highest) * 0.125)).reshape(seq_len, H, E)
    seq_keys = low(low_back(jnp.dot(row_in, w_key, precision=highest))).reshape(seq_len, H, E)
    seq_values = low(low_back(jnp.dot(row_in, w_value, precision=highest))).reshape(seq_len, H, E)
    all_keys = jnp.concatenate([prefix_keys.reshape(P_SIZE, H, E), seq_keys], axis=0)
    all_values = jnp.concatenate([prefix_vals.reshape(P_SIZE, H, E), seq_values], axis=0)
    scores = low_back(jnp.einsum('qhe,khe->hqk', queries, all_keys, precision=highest))
    prefix_ok = jnp.broadcast_to(row_vis[None, :] > 0, (seq_len, P_SIZE))
    same_seg = row_seg[:, None] == row_seg[None, :]
    allowed = jnp.concatenate([prefix_ok, same_seg], axis=1)
    scores = jnp.where(allowed[None], scores, neg_large)
    row_max = lax.optimization_barrier(jnp.max(scores, axis=-1, keepdims=True))
    exp_scores = jnp.exp(scores - row_max)
    attn_prob = low(exp_scores / lax.optimization_barrier(jnp.sum(exp_scores, axis=-1, keepdims=True)))
    mixture = jnp.einsum('hqk,khe->qhe', attn_prob, all_values, precision=highest).reshape(seq_len, D)
    mixture = low(low_back(mixture))
    attn_out = low_back(jnp.dot(mixture, w_out, precision=highest))
    normed_one = layer_norm(row_in + attn_out, gain_one, bias_one)
    hidden_pre = low_back(jnp.dot(low(normed_one), w_up, precision=highest))
    hidden_act = low(jax.nn.gelu(hidden_pre, approximate=False))
    ffn_out = low_back(jnp.dot(hidden_act, w_down, precision=highest))
    return layer_norm(normed_one + ffn_out, gain_two, bias_two)

def reference(hidden_in, segments, prefix_vis, prefix_key, prefix_value, w_query, w_key, w_value, w_out, norm1_gain, norm1_bias, w_up, w_down, norm2_gain, norm2_bias, out_grad):
    weights = tuple((w.astype(jnp.float32) for w in (w_query, w_key, w_value, w_out, norm1_gain, norm1_bias, w_up, w_down, norm2_gain, norm2_bias)))
    rows_in = jnp.transpose(hidden_in.astype(jnp.float32), (1, 0, 2))

    def whole_pass(rows_arg, prefix_keys, prefix_vals):

        def row_step(packed):
            return row_forward(weights, packed[0], packed[1], packed[2], prefix_keys, prefix_vals)
        return lax.map(jax.checkpoint(row_step), (rows_arg, segments, prefix_vis))
    outputs, pullback = jax.vjp(whole_pass, rows_in, prefix_key.astype(jnp.float32), prefix_value.astype(jnp.float32))
    grad_rows, key_grad, value_grad = pullback(jnp.transpose(out_grad.astype(jnp.float32), (1, 0, 2)))
    block_out = jnp.transpose(outputs, (1, 0, 2)).astype(jnp.bfloat16)
    input_grad = jnp.transpose(grad_rows, (1, 0, 2))
    return (block_out, input_grad, key_grad, value_grad)
```

```python
import functools

import jax
import jax.numpy as jnp
from jax import lax
from jax.experimental import pallas as pl
from jax.experimental.pallas import tpu as pltpu
from jax.sharding import PartitionSpec as P

E = 64
P_SIZE = 64
SEGS = 4
PAIR = 2 * E
BIG = 1e30
norm_eps = 1e-05
root_half = 0.7071067811865476
inv_root_tau = 0.3989422804014327

BF = jnp.bfloat16
F32 = jnp.float32
MESH = pl.DeviceIdType.MESH
ANY = pl.BlockSpec(memory_space=pl.ANY)
VM = pl.BlockSpec(memory_space=pltpu.VMEM)
NN = (((1,), (0,)), ((), ()))
NT = (((1,), (1,)), ((), ()))
VMEM_LIMIT = 66 * 1024 * 1000


def dot(a, b, dims=NN):
    return lax.dot_general(a, b, dims, preferred_element_type=F32)


def lanes():
    return lax.broadcasted_iota(jnp.int32, (1, PAIR), 1)


def place():
    row, wide = lax.axis_index("rows"), lax.axis_index("wide")
    return row, wide, lax.rem(wide, 2), lax.div(wide, 2)


def greet(devices):
    barrier = pltpu.get_barrier_semaphore()
    for dev in devices:
        pl.semaphore_signal(barrier, inc=1, device_id=dev, device_id_type=MESH)
    pl.semaphore_wait(barrier, len(devices))


def remote(src, dst, send, recv, dev):
    return pltpu.make_async_remote_copy(
        src_ref=src, dst_ref=dst, send_sem=send, recv_sem=recv, device_id=dev, device_id_type=MESH
    )


def ring_pos(row, rows):
    half = rows // 2
    z, x = lax.div(row, 2), lax.rem(row, 2)
    return z + x * (2 * half - 1 - 2 * z)


def ring_row(pos, rows):
    pos = lax.rem(pos + 2 * rows, rows)
    upper = lax.div(pos, rows // 2)
    return 2 * pos + upper * (2 * rows - 1 - 4 * pos)


def forward_kernel(
    rows, chips,
    x_own, wq, wk, wv, pkey, pval, qext, kext_a, kext_b, w_up, w_dn,
    q_o, ka_o, va_o, kb_o, vb_o, pa_o, pb_o, ra_o, rb_o, mix_o, mixtok_o, wupp_o, wdnp_o, wupr_o, wdnr_o,
    xbuf, wqkv, pks, pvs, q_s, ka, va, kb, vb, s0, s1, s2, s3, oa, la, ma, mix_s, pst_a, pst_b,
    load_sem, out_sem, p_sem, x_send, x_recv, y_send, y_recv, d_send, d_recv, f_send, f_recv,
    mx_send, mx_recv, g_send, g_recv, sh_send, sh_recv, r_send, r_recv, k_send, k_recv,
):
    batch, per = x_own.shape[0], x_own.shape[1]
    tpc = 2 * per
    rem = (chips - 1) * tpc
    half = wqkv.shape[1] // 3
    pairs = half // PAIR
    row, wide, core, chip = place()
    partner = (row, wide + 1 - 2 * core)
    pos = ring_pos(row, rows)
    nxt = (ring_row(pos + 1, rows), wide)
    prv = (ring_row(pos - 1, rows), wide)
    peers = [(row, 2 * lax.rem(chip - d + chips, chips) + core) for d in range(1, chips)]
    back = [(row, 2 * lax.rem(chip + d, chips) + core) for d in range(1, chips)]
    steps = rows // 2
    mats = ((w_up, wupp_o, wupr_o), (w_dn, wdnp_o, wdnr_o))

    col = pl.multiple_of(core * half, half)
    loads = [
        pltpu.make_async_copy(x_own, xbuf.at[:, 0, core], load_sem.at[0]),
        pltpu.make_async_copy(wq.at[:, pl.ds(col, half)], wqkv.at[:, 0:half], load_sem.at[1]),
        pltpu.make_async_copy(wk.at[:, pl.ds(col, half)], wqkv.at[:, half : 2 * half], load_sem.at[2]),
        pltpu.make_async_copy(wv.at[:, pl.ds(col, half)], wqkv.at[:, 2 * half : 3 * half], load_sem.at[3]),
        pltpu.make_async_copy(pkey.at[:, pl.ds(col, half)], pks, load_sem.at[4]),
        pltpu.make_async_copy(pval.at[:, pl.ds(col, half)], pvs, load_sem.at[5]),
    ]
    for copy in loads:
        copy.start()

    greet([partner, nxt, prv] + peers)

    x_pair = remote(x_own, xbuf.at[:, 0, core], x_send, x_recv, partner)
    x_pair.start()

    def x_cross(r):
        return [
            remote(x_own.at[r], xbuf.at[r, d, core], y_send.at[r, d - 1], y_recv.at[r, d - 1], peers[d - 1])
            for d in range(1, chips)
        ]

    def piece(ref, row_at):
        size = ref.shape[-2] // rows
        return pl.ds(pl.multiple_of(row_at * size, size), size)

    def w_cross(m):
        src, _, dst = mats[m]
        at = piece(src, row)
        return [
            remote(src.at[at], dst.at[core, d - 1, at], g_send.at[m, d - 1], g_recv.at[m, d - 1], peers[d - 1])
            for d in range(1, chips)
        ]

    cross = [x_cross(r) for r in range(batch)]
    wcross = [w_cross(0), w_cross(1)]
    for group in (wcross[0], cross[0], wcross[1]) + tuple(cross[1:]):
        for copy in group:
            copy.start()
    shards = [
        remote(mats[m][0], mats[m][1], sh_send.at[m], sh_recv.at[m], partner) for m in range(2)
    ]
    for copy in shards:
        copy.start()

    def ring_copy(m, s, way):
        _, _, buf = mats[m]
        at = piece(buf, ring_row(pos - (s - 1) if way == 0 else pos + (s - 1), rows))
        ref = buf.at[core, :, at]
        return remote(ref, ref, r_send.at[m, s, way], r_recv.at[m, s, way], nxt if way == 0 else prv)

    def hand_over(m, row_at, s, way):
        _, _, buf = mats[m]
        ref = buf.at[core, :, piece(buf, row_at)]
        return remote(ref, ref, k_send.at[m, s, way], k_recv.at[m, s, way], partner)

    def ring_step(m, s):
        if s == 1:
            for copy in wcross[m]:
                copy.wait_recv()
            hand_over(m, row, 0, 0).start()
        else:
            for way in range(2):
                ring_copy(m, s - 1, way).wait_recv()
                hand_over(m, ring_row(pos - (s - 1) if way == 0 else pos + (s - 1), rows), s - 1, way).start()
        if s <= steps:
            ring_copy(m, s, 0).start()
            if s < steps:
                ring_copy(m, s, 1).start()

    def ring_last(m):
        ring_copy(m, steps, 0).wait_recv()
        hand_over(m, ring_row(pos - steps, rows), steps, 0).start()

    def ring_end(m):
        for copy in wcross[m]:
            copy.wait_send()
        hand_over(m, row, 0, 0).wait()
        for s in range(1, steps + 1):
            for way in range(2 if s < steps else 1):
                ring_copy(m, s, way).wait_send()
                hand_over(m, row, s, way).wait()

    def project(r, d, cb, with_q):
        x = xbuf[r, d, cb]
        if with_q:
            q = (dot(x, wqkv[:, 0:half]) * 0.125).astype(BF)
            for p in range(pairs):
                q_s[r, p, pl.ds(pl.multiple_of(cb * per, per), per), :] = q[:, p * PAIR : (p + 1) * PAIR]
        for ref_a, ref_b, at in ((ka, kb, 1), (va, vb, 2)):
            y = dot(x, wqkv[:, at * half : (at + 1) * half]).astype(BF)
            for p in range(pairs):
                val = y[:, p * PAIR : (p + 1) * PAIR]
                if with_q:
                    ref_a[r, p, pl.ds(pl.multiple_of(cb * per, per), per), :] = val
                else:
                    ref_b[r, p, pl.ds(pl.multiple_of((d - 1) * tpc + cb * per, per), per), :] = val

    for copy in loads:
        copy.wait()
    for r in range(batch):
        for p in range(pairs):
            kb[r, p, rem:, :] = pks[:, p * PAIR : (p + 1) * PAIR]
            vb[r, p, rem:, :] = pvs[:, p * PAIR : (p + 1) * PAIR]

    @pl.loop(0, batch)
    def _(r):
        project(r, 0, core, True)

    x_pair.wait_recv()

    @pl.loop(0, batch)
    def _(r):
        project(r, 0, 1 - core, True)

    outs = [
        pltpu.make_async_copy(src, dst, out_sem.at[i])
        for i, (src, dst) in enumerate(((q_s, q_o), (ka, ka_o), (va, va_o)))
    ]
    for copy in outs:
        copy.start()
    ring_step(0, 1)

    bufs = (s0, s1, s2, s3)

    def score(r, p, h, k_s, kext, buf):
        keys = k_s.shape[2]
        mine = lanes() < E if h == 0 else lanes() >= E
        q = jnp.where(mine, q_s[r, p], qext[r])
        k = jnp.where(mine, k_s[r, p], kext[r])
        buf[:, 0:keys] = dot(q, k, NT)

    def unit(r, p, after, u, k_s, v_s, kext, pst, p_hbm, finish, wait_slot):
        keys = k_s.shape[2]
        copy = pltpu.make_async_copy(pst.at[u], p_hbm.at[r, p], p_sem.at[u])
        pl.when(wait_slot)(copy.wait)
        outs, tops = [], []
        for h in range(2):
            score(after[0], after[1], h, k_s, kext, bufs[2 * (1 - u) + h])
            s = bufs[2 * u + h][:, 0:keys]
            top = jnp.max(s, axis=1, keepdims=True)
            prob = jnp.exp(s - top).astype(BF)
            pst[u, h] = prob
            mine = lanes() < E if h == 0 else lanes() >= E
            v = jnp.where(mine, v_s[r, p], jnp.ones((1, PAIR), BF))
            outs.append(dot(prob, v))
            tops.append(top)
        copy.start()
        low = lanes() < E
        finish(
            r,
            p,
            jnp.where(low, outs[0], outs[1]),
            pltpu.roll(jnp.where(low, outs[1], outs[0]), E, 1),
            jnp.where(low, tops[0], tops[1]),
        )

    def finish_a(r, p, o, l, m):
        oa[r, p], la[r, p], ma[r, p] = o, l, m

    def finish_b(r, p, o, l, m):
        top = jnp.maximum(ma[r, p], m)
        w_a, w_b = jnp.exp(ma[r, p] - top), jnp.exp(m - top)
        inv = 1.0 / (w_a * la[r, p] + w_b * l)
        r_a, r_b = w_a * inv, w_b * inv
        mix_s[r, p] = (oa[r, p] * r_a + o * r_b).astype(BF)
        la[r, p], ma[r, p] = r_a, r_b

    def drain(pst, p_hbm):
        for u in range(2):
            pltpu.make_async_copy(pst.at[u], p_hbm.at[0, 0], p_sem.at[u]).wait()

    args_a = (ka, va, kext_a, pst_a, pa_o, finish_a)
    for h in range(2):
        score(0, 0, h, ka, kext_a, bufs[h])
    for r in range(batch):

        @pl.loop(0, pairs // 2)
        def _(i, r=r):
            for u in range(2):
                p = 2 * i + u
                flat = jnp.minimum(r * pairs + p + 1, batch * pairs - 1)
                unit(
                    r, p, (lax.div(flat, pairs), lax.rem(flat, pairs)), u, *args_a,
                    jnp.logical_or(i > 0, r > 0),
                )

        if r + 2 <= steps:
            ring_step(0, r + 2)
    drain(pst_a, pa_o)
    done = [batch + 1, 0]

    def advance(count):
        for _ in range(count):
            for m in range(2):
                if done[m] < steps + 1:
                    done[m] += 1
                    if done[m] <= steps:
                        ring_step(m, done[m])
                    else:
                        ring_last(m)
                    break

    args_b = (kb, vb, kext_b, pst_b, pb_o, finish_b)
    for r in range(batch):
        for copy in cross[r]:
            copy.wait_recv()
        forward = remote(
            xbuf.at[r, 1:, core], xbuf.at[r, 1:, core], d_send.at[r], d_recv.at[r], partner
        )
        forward.start()

        @pl.loop(0, chips - 1)
        def _(d, r=r):
            project(r, d + 1, core, False)

        forward.wait_recv()

        @pl.loop(0, chips - 1)
        def _(d, r=r):
            project(r, d + 1, 1 - core, False)

        if r == batch - 1:
            for i, (src, dst) in enumerate(((kb, kb_o), (vb, vb_o))):
                copy = pltpu.make_async_copy(src, dst, out_sem.at[3 + i])
                copy.start()
                outs.append(copy)
        for h in range(2):
            score(r, 0, h, kb, kext_b, bufs[h])

        @pl.loop(0, pairs // 2)
        def _(i, r=r):
            for u in range(2):
                p = 2 * i + u
                unit(r, p, (r, jnp.minimum(p + 1, pairs - 1)), u, *args_b, i > 0)

        drain(pst_b, pb_o)
        advance(2)
        mine, other = pl.multiple_of(core * per, per), pl.multiple_of((1 - core) * per, per)
        for p in range(pairs):
            cols = pl.ds(pl.multiple_of(core * half + p * PAIR, PAIR), PAIR)
            copy = remote(
                mix_s.at[r, p, pl.ds(other, per)], mixtok_o.at[r, :, cols],
                mx_send.at[r, p], mx_recv.at[r, p], partner,
            )
            copy.start()
            outs.append(copy)
            copy = pltpu.make_async_copy(
                mix_s.at[r, p, pl.ds(mine, per)], mixtok_o.at[r, :, cols], f_send.at[r, p]
            )
            copy.start()
            outs.append(copy)
        for i, (src, dst) in enumerate(((mix_s, mix_o), (la, ra_o), (ma, rb_o))):
            copy = pltpu.make_async_copy(src.at[r], dst.at[r], f_recv.at[r, i])
            copy.start()
            outs.append(copy)
        forward.wait_send()

    advance(2 * (steps + 1))
    for m in range(2):
        ring_end(m)
    x_pair.wait_send()
    for group in cross:
        for copy in group:
            copy.wait_send()
    for copy in shards + outs:
        copy.wait()


def forward_call(rows, chips, x, wq, wk, wv, pkey, pval, qext, kext_a, kext_b, w_up, w_dn):
    batch, per, width = x.shape
    tpc, half = 2 * per, width // 2
    keys_a, keys_b = tpc, (chips - 1) * tpc + P_SIZE
    pairs = half // PAIR
    steps = rows // 2
    out = lambda dt, *s: jax.ShapeDtypeStruct(s, dt)
    shapes = (
        out(BF, batch, pairs, tpc, PAIR),
        out(BF, batch, pairs, keys_a, PAIR),
        out(BF, batch, pairs, keys_a, PAIR),
        out(BF, batch, pairs, keys_b, PAIR),
        out(BF, batch, pairs, keys_b, PAIR),
        out(BF, batch, pairs, 2, tpc, keys_a),
        out(BF, batch, pairs, 2, tpc, keys_b),
        out(F32, batch, pairs, tpc, PAIR),
        out(F32, batch, pairs, tpc, PAIR),
        out(BF, batch, pairs, tpc, PAIR),
        out(BF, batch, per, width),
        out(BF, *w_up.shape),
        out(BF, *w_dn.shape),
        out(BF, 2, chips - 1, *w_up.shape),
        out(BF, 2, chips - 1, *w_dn.shape),
    )
    dma = pltpu.SemaphoreType.DMA
    scratch = [
        pltpu.VMEM((batch, chips, 2, per, width), BF),
        pltpu.VMEM((width, 3 * half), BF),
        pltpu.VMEM((P_SIZE, half), BF),
        pltpu.VMEM((P_SIZE, half), BF),
        pltpu.VMEM((batch, pairs, tpc, PAIR), BF),
        pltpu.VMEM((batch, pairs, keys_a, PAIR), BF),
        pltpu.VMEM((batch, pairs, keys_a, PAIR), BF),
        pltpu.VMEM((batch, pairs, keys_b, PAIR), BF),
        pltpu.VMEM((batch, pairs, keys_b, PAIR), BF),
        *([pltpu.VMEM((tpc, max(keys_a, keys_b)), F32)] * 4),
        *([pltpu.VMEM((batch, pairs, tpc, PAIR), F32)] * 3),
        pltpu.VMEM((batch, pairs, tpc, PAIR), BF),
        pltpu.VMEM((2, 2, tpc, keys_a), BF),
        pltpu.VMEM((2, 2, tpc, keys_b), BF),
        dma((6,)), dma((5,)), dma((2,)), dma, dma,
        dma((batch, chips - 1)), dma((batch, chips - 1)),
        dma((batch,)), dma((batch,)),
        dma((batch, pairs)), dma((batch, 3)),
        dma((batch, pairs)), dma((batch, pairs)),
        dma((2, chips - 1)), dma((2, chips - 1)),
        dma((2,)), dma((2,)),
        dma((2, steps + 1, 2)), dma((2, steps + 1, 2)),
        dma((2, steps + 1, 2)), dma((2, steps + 1, 2)),
    ]
    return pl.pallas_call(
        functools.partial(forward_kernel, rows, chips),
        out_shape=shapes,
        in_specs=[ANY] * 6 + [VM] * 3 + [ANY] * 2,
        out_specs=[ANY] * len(shapes),
        scratch_shapes=scratch,
        compiler_params=pltpu.CompilerParams(
            collective_id=0, has_side_effects=True, vmem_limit_bytes=VMEM_LIMIT
        ),
        name="attention_forward",
    )(x, wq, wk, wv, pkey, pval, qext, kext_a, kext_b, w_up, w_dn)


def mean_of(value):
    return jnp.mean(value, axis=-1, keepdims=True)


def ffn_kernel(
    mixtok, x_own, og, w_out, g1, b1, g2, b2, w_up, wup_p, wup_r, w_dn, wdn_p, wdn_r,
    block_o, gsum_o, gatt_o,
    mix, x, ogs, wo, up, dn, n1, n1l, sc1, inv1, acc, slope, pre0, pre1, gt, gtl, act, bst, gst,
    load_sem, w_sem, o_sem, d_send, d_recv,
):
    batch, per, width = mixtok.shape
    tokens = batch * per
    shards, hidden = up.shape[0], up.shape[2]
    tile = 256
    tiles = hidden // tile
    half = width // 2
    pairs = half // PAIR
    row, wide, core, chip = place()
    partner = (row, wide + 1 - 2 * core)
    chips_less = shards // 2 - 1

    loads = [pltpu.make_async_copy(w_out, wo, load_sem.at[0])]
    for r in range(batch):
        at = slice(r * per, (r + 1) * per)
        loads.append(pltpu.make_async_copy(mixtok.at[r], mix.at[at], load_sem.at[1 + 3 * r]))
        loads.append(pltpu.make_async_copy(x_own.at[r], x.at[at], load_sem.at[2 + 3 * r]))
        loads.append(pltpu.make_async_copy(og.at[r], ogs.at[at], load_sem.at[3 + 3 * r]))
    weights = []
    for s in range(shards):
        for m, (own, pair, far, buf) in enumerate(((w_up, wup_p, wup_r, up), (w_dn, wdn_p, wdn_r, dn))):
            if s < 2:
                src = (own, pair)[s]
            else:
                c, d = (s - 2) // chips_less, (s - 2) % chips_less
                src = far.at[c, d]
            weights.append(pltpu.make_async_copy(src, buf.at[s], w_sem.at[m, s]))
    for copy in loads + weights:
        copy.start()
    greet([partner])
    for copy in loads:
        copy.wait()

    @pl.loop(0, width // tile)
    def _(j):
        at = pl.ds(pl.multiple_of(j * tile, tile), tile)
        acc[:, at] = dot(mix[...], wo[:, at]) + x[:, at].astype(F32)

    chunk = 64

    def by_rows(body):
        @pl.loop(0, tokens // chunk)
        def _(i):
            body(pl.ds(pl.multiple_of(i * chunk, chunk), chunk))

    def norm_one(at):
        z = acc[at]
        c = z - mean_of(z)
        inv = lax.rsqrt(mean_of(c * c) + norm_eps)
        s = c * inv
        n = s * g1[...] + b1[...]
        n1[at], n1l[at], sc1[at], inv1[at] = n, n.astype(BF), s, inv
        acc[at] = jnp.zeros_like(z)

    by_rows(norm_one)
    for copy in weights:
        copy.wait()
    total = shards * tiles

    def split(j):
        return lax.div(j, tiles), pl.ds(pl.multiple_of(lax.rem(j, tiles) * tile, tile), tile)

    def up_tile(j, buf):
        s, at = split(j)
        buf[...] = dot(n1l[...], up[s, :, at])

    pres = (pre0, pre1)
    up_tile(0, pre0)

    @pl.loop(0, total // 2)
    def _(i):
        for u in range(2):
            j = 2 * i + u
            up_tile(jnp.minimum(j + 1, total - 1), pres[1 - u])
            v = pres[u][...]
            cdf = 0.5 * (1.0 + lax.erf(v * root_half))
            a = (v * cdf).astype(BF)
            s, at = split(j)
            slope[j] = cdf + v * jnp.exp(-0.5 * v * v) * inv_root_tau
            acc[...] += dot(a, dn[s, at, :])

    def norm_two(at):
        z = n1[at] + acc[at]
        c = z - mean_of(z)
        inv = lax.rsqrt(mean_of(c * c) + norm_eps)
        s = c * inv
        bst[at] = (s * g2[...] + b2[...]).astype(BF)
        t = ogs[at] * g2[...]
        g = inv * (t - mean_of(t) - s * mean_of(t * s))
        gt[at], gtl[at] = g, g.astype(BF)
        acc[at] = jnp.zeros_like(z)

    by_rows(norm_two)
    outs = []
    for r in range(batch):
        outs.append(pltpu.make_async_copy(bst.at[r * per : (r + 1) * per], block_o.at[r], o_sem.at[0, r]))

    for copy in outs:
        copy.start()

    def down_back(j, buf):
        s, at = split(j)
        buf[...] = dot(gtl[...], dn[s, at, :], NT)

    down_back(0, pre0)

    @pl.loop(0, total // 2)
    def _(i):
        for u in range(2):
            j = 2 * i + u
            down_back(jnp.minimum(j + 1, total - 1), pres[1 - u])
            g = (pres[u][...] * slope[j]).astype(BF)
            s, at = split(j)
            acc[...] += dot(g, up[s, :, at], NT)

    def norm_back(at):
        t = (gt[at] + acc[at]) * g1[...]
        s = sc1[at]
        g = inv1[at] * (t - mean_of(t) - s * mean_of(t * s))
        gt[at], gtl[at] = g, g.astype(BF)

    by_rows(norm_back)
    for r in range(batch):
        copy = pltpu.make_async_copy(gt.at[r * per : (r + 1) * per], gsum_o.at[r], o_sem.at[1, r])
        copy.start()
        outs.append(copy)

    mine = pl.ds(pl.multiple_of(core * per, per), per)
    for side in range(2):
        base = (1 - core) * half if side == 0 else core * half
        g = dot(gtl[...], wo[pl.ds(pl.multiple_of(base, half), half), :], NT).astype(BF)
        for p in range(pairs):
            gst[side, p] = g[:, p * PAIR : (p + 1) * PAIR]
        for p in range(pairs):
            for r in range(batch):
                src, dst = gst.at[side, p, r * per : (r + 1) * per], gatt_o.at[r, p, mine]
                if side == 0:
                    copy = remote(src, dst, d_send.at[r, p], d_recv.at[r, p], partner)
                else:
                    copy = pltpu.make_async_copy(src, dst, o_sem.at[2 + p, r])
                copy.start()
                outs.append(copy)
    for copy in outs:
        copy.wait()


def ffn_call(mixtok, x, og, w_out, g1, b1, g2, b2, w_up, wup_p, wup_r, w_dn, wdn_p, wdn_r):
    batch, per, width = mixtok.shape
    tokens = batch * per
    shards = 2 + 2 * wup_r.shape[1]
    hidden = w_up.shape[1]
    tile = 256
    pairs = width // 2 // PAIR
    out = lambda dt, *s: jax.ShapeDtypeStruct(s, dt)
    dma = pltpu.SemaphoreType.DMA
    vm = pltpu.VMEM
    return pl.pallas_call(
        ffn_kernel,
        out_shape=(
            out(BF, batch, per, width),
            out(F32, batch, per, width),
            out(BF, batch, pairs, 2 * per, PAIR),
        ),
        in_specs=[ANY] * 4 + [VM] * 4 + [ANY] * 6,
        out_specs=[ANY] * 3,
        scratch_shapes=[
            vm((tokens, width), BF),
            vm((tokens, width), BF),
            vm((tokens, width), F32),
            vm((width, width), BF),
            vm((shards, width, hidden), BF),
            vm((shards, hidden, width), BF),
            vm((tokens, width), F32),
            vm((tokens, width), BF),
            vm((tokens, width), F32),
            vm((tokens, 1), F32),
            vm((tokens, width), F32),
            vm((shards * hidden // tile, tokens, tile), F32),
            vm((tokens, tile), F32),
            vm((tokens, tile), F32),
            vm((tokens, width), F32),
            vm((tokens, width), BF),
            vm((8, 128), BF),
            vm((tokens, width), BF),
            vm((2, pairs, tokens, PAIR), BF),
            dma((1 + 3 * batch,)), dma((2, shards)), dma((2 + pairs, batch)), dma((batch, pairs)), dma((batch, pairs)),
        ],
        compiler_params=pltpu.CompilerParams(
            collective_id=1, has_side_effects=True, vmem_limit_bytes=VMEM_LIMIT
        ),
        name="feed_forward",
    )(mixtok, x, og, w_out, g1, b1, g2, b2, w_up, wup_p, wup_r, w_dn, wdn_p, wdn_r)


def backward_kernel(
    rows, chips,
    g_i, mix_i, ra_i, rb_i, q_i, ka_i, va_i, kb_i, vb_i, pa_i, pb_i, wq, wk, wv, gs_i,
    ig_o, pk_o, pv_o,
    g_s, mix_s, ra, rb, q_s, ka, va, kb, vb, w_s, gs, pin_a, pin_b, s0, s1, s2, s3, do0, do1,
    dq, dks, dvs, psum, half_b, send_b, got_b, y_out, y_in, half_a, send_a, got_a,
    pr_in, pr_y, p_full,
    load_sem, p_sem, o_sem, db_send, db_recv, y_send, y_recv, da_send, da_recv,
    p1_send, p1_recv, p2_send, p2_recv, p3_send, p3_recv, p4_send, p4_recv,
):
    batch, pairs, tpc = q_s.shape[0], q_s.shape[1], q_s.shape[2]
    per = tpc // 2
    rem = (chips - 1) * tpc
    width, half = w_s.shape[1], w_s.shape[2]
    row, wide, core, chip = place()
    partner = (row, wide + 1 - 2 * core)
    peers = [(row, 2 * lax.rem(chip - d + chips, chips) + core) for d in range(1, chips)]
    back = [(row, 2 * lax.rem(chip + d, chips) + core) for d in range(1, chips)]
    plane = [(lax.rem(row + t, rows), wide) for t in range(1, rows)]

    col = pl.multiple_of(core * half, half)
    pairs_of = (
        (g_i, g_s), (mix_i, mix_s), (rb_i, rb), (kb_i, kb), (vb_i, vb), (q_i, q_s),
        (wk.at[:, pl.ds(col, half)], w_s.at[1]), (wv.at[:, pl.ds(col, half)], w_s.at[2]),
        (ra_i, ra), (ka_i, ka), (va_i, va), (wq.at[:, pl.ds(col, half)], w_s.at[0]), (gs_i, gs),
    )
    loads = [pltpu.make_async_copy(src, dst, load_sem.at[i]) for i, (src, dst) in enumerate(pairs_of)]

    def fetch(pin, p_hbm, r, p, u):
        return pltpu.make_async_copy(p_hbm.at[r, p], pin.at[u], p_sem.at[u])

    for copy in loads[:6]:
        copy.start()
    for u in range(2):
        fetch(pin_b, pb_i, 0, u, u).start()
    for copy in loads[6:]:
        copy.start()
    greet([partner] + peers + plane)
    for copy in loads[:6]:
        copy.wait()

    bufs, dos = (s0, s1, s2, s3), (do0, do1)

    def first(r, p, u, v_s, scale):
        keys = v_s.shape[2]
        g = g_s[r, p].astype(F32) * scale[r, p]
        do = g.astype(BF)
        dos[u][...] = do
        t = g * mix_s[r, p].astype(F32)
        lane = lanes()
        for h in range(2):
            mine = lane < E if h == 0 else lane >= E
            delta = jnp.sum(jnp.where(mine, t, 0.0), axis=1, keepdims=True)
            hi = delta.astype(BF)
            left = delta - hi.astype(F32)
            mid = left.astype(BF)
            low = (left - mid.astype(F32)).astype(BF)
            at = E if h == 0 else 0
            ext = jnp.where(
                lane == at, -hi, jnp.where(lane == at + 1, -mid, jnp.where(lane == at + 2, -low, jnp.zeros((1, PAIR), BF)))
            )
            one = jnp.where(jnp.logical_and(lane >= at, lane < at + 3), 1.0, 0.0).astype(BF)
            bufs[2 * u + h][:, 0:keys] = dot(
                jnp.where(mine, do, ext), jnp.where(mine, v_s[r, p], one), NT
            )

    def second(r, p, u, k_s, pin, start_dq, prefix):
        keys = k_s.shape[2]
        q2, k2, do = q_s[r, p], k_s[r, p], dos[u][...]
        do_t, q_t = do.T, q2.T
        gq, gk, gv = [], [], []
        for h in range(2):
            prob = pin[u, h]
            ds = (prob.astype(F32) * bufs[2 * u + h][:, 0:keys]).astype(BF)
            at = slice(h * E, (h + 1) * E)
            gv.append(dot(do_t[at], prob))
            gk.append(dot(q_t[at], ds))
            gq.append(dot(ds, k2))
        low = lanes() < E
        grad = jnp.where(low, gq[0], gq[1])
        dq[r, p] = grad if start_dq else dq[r, p] + grad
        cols = pl.ds(pl.multiple_of(p * PAIR, PAIR), PAIR)
        for ref, parts, k in ((dks, gk, 0), (dvs, gv, 1)):
            val = jnp.concatenate(parts, axis=0).T
            if prefix:
                ref[0:rem, cols] = val[:rem].astype(BF)
                psum[k * P_SIZE : (k + 1) * P_SIZE, cols] += val[rem:]
            else:
                ref[0:tpc, cols] = val.astype(BF)

    def group(r, k_s, v_s, scale, pin, p_hbm, start_dq, prefix):
        first(r, 0, 0, v_s, scale)

        @pl.loop(0, pairs // 2)
        def _(i):
            for u in range(2):
                p = 2 * i + u
                fetch(pin, p_hbm, r, p, u).wait()
                first(r, jnp.minimum(p + 1, pairs - 1), 1 - u, v_s, scale)
                second(r, p, u, k_s, pin, start_dq, prefix)

                @pl.when(i < pairs // 2 - 1)
                def _():
                    fetch(pin, p_hbm, r, p + 2, u).start()

    def to_inputs(at):
        keys = dot(dks[at], w_s[1], NT)
        return keys + dot(dvs[at], w_s[2], NT)

    psum[...] = jnp.zeros_like(psum)
    tails = []
    y_copies = []
    b_copies = []

    def chip_sum(r):
        for copy in b_copies[r]:
            copy.wait_recv()
        for d in range(1, chips):
            y_out[r, d - 1] = (half_b[r, d - 1] + got_b[r, d - 1]).astype(BF)
        copies = [
            remote(
                y_out.at[r, d - 1], y_in.at[r, d - 1], y_send.at[r, d - 1], y_recv.at[r, d - 1], back[d - 1]
            )
            for d in range(1, chips)
        ]
        for copy in copies:
            copy.start()
        y_copies.append(copies)

    for r in range(batch):
        group(r, kb, vb, rb, pin_b, pb_i, True, True)
        if r + 1 < batch:
            for u in range(2):
                fetch(pin_b, pb_i, r + 1, u, u).start()
        else:
            for u in range(2):
                fetch(pin_a, pa_i, 0, u, u).start()
        if r == 0:
            for copy in loads[6:]:
                copy.wait()
        copies = []
        for d in range(1, chips):
            at = pl.ds(pl.multiple_of((d - 1) * tpc + (1 - core) * per, per), per)
            send_b[r, d - 1] = to_inputs(at)
            copy = remote(
                send_b.at[r, d - 1], got_b.at[r, d - 1], db_send.at[r, d - 1], db_recv.at[r, d - 1], partner
            )
            copy.start()
            copies.append(copy)
        b_copies.append(copies)
        for d in range(1, chips):
            at = pl.ds(pl.multiple_of((d - 1) * tpc + core * per, per), per)
            half_b[r, d - 1] = to_inputs(at)
        chip_sum(r)

    size = 2 * P_SIZE // rows

    def part(at):
        return pl.ds(pl.multiple_of(at * size, size), size)

    p_one = [
        remote(psum.at[part(plane[t - 1][0])], pr_in.at[t - 1], p1_send.at[t - 1], p1_recv.at[t - 1], plane[t - 1])
        for t in range(1, rows)
    ]
    for copy in p_one:
        copy.start()

    for r in range(batch):
        group(r, ka, va, ra, pin_a, pa_i, False, False)
        if r + 1 < batch:
            for u in range(2):
                fetch(pin_a, pa_i, r + 1, u, u).start()
        for side in range(2):
            block = pl.multiple_of(((1 - core) if side == 0 else core) * per, per)
            at = pl.ds(block, per)
            part_in = to_inputs(at)
            for p in range(pairs):
                dvs[at, p * PAIR : (p + 1) * PAIR] = (dq[r, p, at, :]).astype(BF)
            val = part_in + 0.125 * dot(dvs[at], w_s[0], NT)
            if side == 0:
                send_a[r] = val
                copy = remote(send_a.at[r], got_a.at[r], da_send.at[r], da_recv.at[r], partner)
                copy.start()
                tails.append(copy)
            else:
                half_a[r] = gs[r] + val
        if r == 0:
            for copy in p_one:
                copy.wait_recv()
            total = psum[part(row)]
            for t in range(1, rows):
                total = total + pr_in[t - 1]
            pr_y[0] = total
            p_two = [
                remote(pr_y.at[0], pr_y.at[d], p2_send.at[d - 1], p2_recv.at[d - 1], peers[d - 1])
                for d in range(1, chips)
            ]
            for copy in p_two:
                copy.start()
        if r == batch - 1:
            for copy in p_two:
                copy.wait()
            whole = jnp.zeros((size, half), F32)
            for c in range(chips):
                whole = whole + pr_y[lax.rem(c - chip + chips, chips)]
            p_full[part(row)] = whole
            p_three = [
                remote(p_full.at[part(row)], p_full.at[part(row)], p3_send.at[t - 1], p3_recv.at[t - 1], plane[t - 1])
                for t in range(1, rows)
            ]
            for copy in p_three:
                copy.start()

    outs = []
    for r in range(batch):
        tails[r].wait()
        for copy in y_copies[r]:
            copy.wait()
        val = half_a[r] + got_a[r]
        for d in range(1, chips):
            val = val + y_in[r, d - 1].astype(F32)
        half_a[r] = val
        copy = pltpu.make_async_copy(half_a.at[r], ig_o.at[r], o_sem.at[r])
        copy.start()
        outs.append(copy)
    for copy in p_three:
        copy.wait()
    cols = pl.ds(col, half)
    for k, ref in enumerate((pk_o, pv_o)):
        src = p_full.at[k * P_SIZE : (k + 1) * P_SIZE]
        copy = remote(src, ref.at[:, cols], p4_send.at[k], p4_recv.at[k], partner)
        copy.start()
        outs.append(copy)
        copy = pltpu.make_async_copy(src, ref.at[:, cols], o_sem.at[batch + k])
        copy.start()
        outs.append(copy)
    for copies in b_copies:
        for copy in copies:
            copy.wait_send()
    for copy in p_one:
        copy.wait_send()
    for copy in outs:
        copy.wait()


def backward_call(rows, chips, g, mix, ra, rb, q, ka, va, kb, vb, pa, pb, wq, wk, wv, gs):
    batch, pairs, tpc, _ = q.shape
    keys_a, keys_b = ka.shape[2], kb.shape[2]
    per, width = gs.shape[1], gs.shape[2]
    half = width // 2
    size = 2 * P_SIZE // rows
    out = lambda dt, *s: jax.ShapeDtypeStruct(s, dt)
    dma = pltpu.SemaphoreType.DMA
    vm = pltpu.VMEM
    far = chips - 1
    keys = max(keys_a, keys_b)
    return pl.pallas_call(
        functools.partial(backward_kernel, rows, chips),
        out_shape=(
            out(F32, batch, per, width),
            out(F32, P_SIZE, width),
            out(F32, P_SIZE, width),
        ),
        in_specs=[ANY] * 15,
        out_specs=[ANY] * 3,
        scratch_shapes=[
            vm((batch, pairs, tpc, PAIR), BF),
            vm((batch, pairs, tpc, PAIR), BF),
            vm((batch, pairs, tpc, PAIR), F32),
            vm((batch, pairs, tpc, PAIR), F32),
            vm((batch, pairs, tpc, PAIR), BF),
            vm((batch, pairs, keys_a, PAIR), BF),
            vm((batch, pairs, keys_a, PAIR), BF),
            vm((batch, pairs, keys_b, PAIR), BF),
            vm((batch, pairs, keys_b, PAIR), BF),
            vm((3, width, half), BF),
            vm((batch, per, width), F32),
            vm((2, 2, tpc, keys_a), BF),
            vm((2, 2, tpc, keys_b), BF),
            *([vm((tpc, keys), F32)] * 4),
            *([vm((tpc, PAIR), BF)] * 2),
            vm((batch, pairs, tpc, PAIR), F32),
            vm((keys, half), BF),
            vm((keys, half), BF),
            vm((2 * P_SIZE, half), F32),
            vm((batch, far, per, width), F32),
            vm((batch, far, per, width), F32),
            vm((batch, far, per, width), F32),
            vm((batch, far, per, width), BF),
            vm((batch, far, per, width), BF),
            vm((batch, per, width), F32),
            vm((batch, per, width), F32),
            vm((batch, per, width), F32),
            vm((rows - 1, size, half), F32),
            vm((chips, size, half), F32),
            vm((2 * P_SIZE, half), F32),
            dma((13,)), dma((2,)), dma((batch + 2,)),
            dma((batch, far)), dma((batch, far)),
            dma((batch, far)), dma((batch, far)),
            dma((batch,)), dma((batch,)),
            dma((rows - 1,)), dma((rows - 1,)),
            dma((far,)), dma((far,)),
            dma((rows - 1,)), dma((rows - 1,)),
            dma((2,)), dma((2,)),
        ],
        compiler_params=pltpu.CompilerParams(
            collective_id=2, has_side_effects=True, vmem_limit_bytes=VMEM_LIMIT
        ),
        name="attention_backward",
    )(g, mix, ra, rb, q, ka, va, kb, vb, pa, pb, wq, wk, wv, gs)


def mask_lanes(segments, prefix_vis, chip, tpc):
    length = segments.shape[1]
    twice = jnp.concatenate([segments, segments], axis=1)
    turned = lax.dynamic_slice_in_dim(twice, chip * tpc, length, 1)
    lane = jnp.arange(PAIR) % E
    seg_lane = (lane < SEGS)[None, None, :]
    same = turned[:, :, None] == lane[None, None, :]
    keys = jnp.where(seg_lane & ~same, -BIG, 0.0).astype(BF)
    queries = jnp.where((seg_lane & same[:, :tpc]) | (lane == SEGS)[None, None, :], 1.0, 0.0).astype(BF)
    hidden = (prefix_vis == 0)[:, :, None] & (lane == SEGS)[None, None, :]
    prefix = jnp.where(hidden, -BIG, 0.0).astype(BF)
    return queries, keys[:, :tpc], jnp.concatenate([keys[:, tpc:], prefix], axis=1)


def on_device(
    rows, chips,
    hidden_in, segments, prefix_vis, prefix_key, prefix_value, w_query, w_key, w_value, w_out,
    norm1_gain, norm1_bias, w_up, w_down, norm2_gain, norm2_bias, out_grad,
):
    per = hidden_in.shape[0]
    chip = lax.axis_index("wide") // 2
    x = jnp.transpose(hidden_in, (1, 0, 2))
    og = jnp.transpose(out_grad, (1, 0, 2))
    qext, kext_a, kext_b = mask_lanes(segments, prefix_vis, chip, 2 * per)
    (q, ka, va, kb, vb, pa, pb, ra, rb, mix, mixtok, wup_p, wdn_p, wup_r, wdn_r) = forward_call(
        rows, chips, x, w_query, w_key, w_value, prefix_key, prefix_value, qext, kext_a, kext_b, w_up, w_down
    )
    flat = lambda v: v.reshape(1, -1)
    block, gs, g = ffn_call(
        mixtok, x, og, w_out, flat(norm1_gain), flat(norm1_bias), flat(norm2_gain), flat(norm2_bias),
        w_up, wup_p, wup_r, w_down, wdn_p, wdn_r,
    )
    input_grad, pk_grad, pv_grad = backward_call(
        rows, chips, g, mix, ra, rb, q, ka, va, kb, vb, pa, pb, w_query, w_key, w_value, gs
    )
    return (
        jnp.transpose(block, (1, 0, 2)),
        jnp.transpose(input_grad, (1, 0, 2)),
        pk_grad,
        pv_grad,
    )


def solution(mesh):
    rows, chips = mesh.shape["rows"], mesh.shape["wide"] // 2
    act = P("wide", "rows", None)
    per_row = P("rows", None)
    in_specs = (
        act, per_row, per_row, *([P()] * 8), P(None, "wide"), P("wide", None), P(), P(), act,
    )
    out_specs = (act, act, P(), P())
    return jax.shard_map(
        functools.partial(on_device, rows, chips),
        mesh=mesh,
        in_specs=in_specs,
        out_specs=out_specs,
        check_vma=False,
    )
```

```python
import functools

import jax
import jax.numpy as jnp
from jax import lax
from jax.experimental import pallas as pl
from jax.experimental.pallas import tpu as pltpu
from jax.sharding import PartitionSpec as P

E = 64
P_SIZE = 64
SEGS = 4
PAIR = 2 * E
BIG = 1e30
norm_eps = 1e-05
root_half = 0.7071067811865476
inv_root_tau = 0.3989422804014327

BF = jnp.bfloat16
F32 = jnp.float32
MESH = pl.DeviceIdType.MESH
ANY = pl.BlockSpec(memory_space=pl.ANY)
VM = pl.BlockSpec(memory_space=pltpu.VMEM)
NN = (((1,), (0,)), ((), ()))
NT = (((1,), (1,)), ((), ()))
VMEM_LIMIT = 66 * 1024 * 1000


def dot(a, b, dims=NN):
    return lax.dot_general(a, b, dims, preferred_element_type=F32)


def lanes():
    return lax.broadcasted_iota(jnp.int32, (1, PAIR), 1)


def place():
    row, wide = lax.axis_index("rows"), lax.axis_index("wide")
    return row, wide, lax.rem(wide, 2), lax.div(wide, 2)


def greet(devices):
    barrier = pltpu.get_barrier_semaphore()
    for dev in devices:
        pl.semaphore_signal(barrier, inc=1, device_id=dev, device_id_type=MESH)
    pl.semaphore_wait(barrier, len(devices))


def remote(src, dst, send, recv, dev):
    return pltpu.make_async_remote_copy(
        src_ref=src, dst_ref=dst, send_sem=send, recv_sem=recv, device_id=dev, device_id_type=MESH
    )


def ring_pos(row, rows):
    half = rows // 2
    z, x = lax.div(row, 2), lax.rem(row, 2)
    return z + x * (2 * half - 1 - 2 * z)


def ring_row(pos, rows):
    pos = lax.rem(pos + 2 * rows, rows)
    upper = lax.div(pos, rows // 2)
    return 2 * pos + upper * (2 * rows - 1 - 4 * pos)


def mean_of(value):
    return jnp.mean(value, axis=-1, keepdims=True)


def forward_kernel(
    rows, chips,
    x_own, segs, vis, wq, wk, wv, pkey, pval, w_out, w_up, w_dn, og, g1, b1, g2, b2,
    q_o, ka_o, va_o, kb_o, vb_o, pa_o, pb_o, ra_o, rb_o, mix_o, block_o, gsum_o, gatt_o,
    xbuf, up, dn, wo, mixtok, la, ma, mix_s, ogs, gst,
    load_sem, out_sem, p_sem, x_send, x_recv, y_send, y_recv, d_send, d_recv, f_sem, o_sem,
    mx_send, mx_recv, g_send, g_recv, e_send, e_recv, sh_send, sh_recv, r_send, r_recv, k_send, k_recv,
    l_send, l_recv, gm_send, gm_recv,
):
    batch, per, width = x_own.shape
    tpc = 2 * per
    rem = (chips - 1) * tpc
    keys_b = rem + P_SIZE
    half = width // 2
    pairs = half // PAIR
    hidden = up.shape[3]
    tokens = batch * per
    row, wide, core, chip = place()
    partner = (row, wide + 1 - 2 * core)
    pos = ring_pos(row, rows)
    nxt = (ring_row(pos + 1, rows), wide)
    prv = (ring_row(pos - 1, rows), wide)
    peers = [(row, 2 * lax.rem(chip - d + chips, chips) + core) for d in range(1, chips)]
    mats = ((w_up, up), (w_dn, dn))
    cw = (rows // 2, 2)
    ccw = (rows // 2 - 1, 2)

    col = pl.multiple_of(core * half, half)
    far_loads = [
        pltpu.make_async_copy(w_up, up.at[0, core], load_sem.at[0]),
        pltpu.make_async_copy(w_dn, dn.at[0, core], load_sem.at[1]),
        pltpu.make_async_copy(w_out, wo, load_sem.at[2]),
    ] + [pltpu.make_async_copy(og.at[r], ogs.at[r], load_sem.at[3 + r]) for r in range(batch)]
    x_load = pltpu.make_async_copy(x_own, xbuf.at[:, 0, core], load_sem.at[3 + batch])

    x_pair = remote(x_own, xbuf.at[:, 0, core], x_send, x_recv, partner)
    cross = [
        [
            remote(x_own.at[r], xbuf.at[r, d, core], y_send.at[r, d - 1], y_recv.at[r, d - 1], peers[d - 1])
            for d in range(1, chips)
        ]
        for r in range(batch)
    ]

    def piece(ref, row_at):
        size = ref.shape[-2] // rows
        return pl.ds(pl.multiple_of(row_at * size, size), size)

    def w_cross(m, at, send, recv):
        src, dst = mats[m]
        at = piece(src, at)
        return [
            remote(src.at[at], dst.at[d, core, at], send.at[d - 1], recv.at[d - 1], peers[d - 1])
            for d in range(1, chips)
        ]

    wcross = [w_cross(m, row, g_send.at[m], g_recv.at[m]) for m in range(2)]
    extras = [
        w_cross(1, ring_row(pos + o, rows), e_send.at[o], e_recv.at[o]) for o in range(ccw[1] + 1, rows - cw[1])
    ]
    shards = [
        remote(mats[m][0], mats[m][1].at[0, core], sh_send.at[m], sh_recv.at[m], partner) for m in range(2)
    ]

    def place_of(s, way):
        return ring_row(pos - s if way == 0 else pos + s, rows)

    def ring_copy(m, s, way):
        buf = mats[m][1]
        ref = buf.at[1:, core, piece(buf, place_of(s - 1, way))]
        return remote(ref, ref, r_send.at[m, s, way], r_recv.at[m, s, way], nxt if way == 0 else prv)

    def hand_over(m, s, way):
        buf = mats[m][1]
        ref = buf.at[1:, core, piece(buf, place_of(s, way))]
        return remote(ref, ref, k_send.at[m, s, way], k_recv.at[m, s, way], partner)

    def ways(m, s):
        return range(2 if s <= ccw[m] else 1)

    def hop(m, s):
        if s > cw[m] + 1:
            return
        if s == 1:
            for copy in wcross[m]:
                copy.wait_recv()
            hand_over(m, 0, 0).start()
        else:
            for way in ways(m, s - 1):
                ring_copy(m, s - 1, way).wait_recv()
                hand_over(m, s - 1, way).start()
        if s <= cw[m]:
            for way in ways(m, s):
                ring_copy(m, s, way).start()

    def extra_over(o):
        buf = mats[1][1]
        ref = buf.at[1:, core, piece(buf, place_of(o, 1))]
        return remote(ref, ref, l_send.at[o], l_recv.at[o], partner)

    def take_extras():
        for i, copies in enumerate(extras):
            for copy in copies:
                copy.wait_recv()
            extra_over(ccw[1] + 1 + i).start()

    def gathered(m):
        hand_over(m, 0, 0).wait_recv()
        for s in range(1, cw[m] + 1):
            for way in ways(m, s):
                hand_over(m, s, way).wait_recv()
        if m == 1:
            for i in range(len(extras)):
                extra_over(ccw[1] + 1 + i).wait_recv()

    def sent(m):
        for copy in wcross[m]:
            copy.wait_send()
        hand_over(m, 0, 0).wait_send()
        for s in range(1, cw[m] + 1):
            for way in ways(m, s):
                ring_copy(m, s, way).wait_send()
                hand_over(m, s, way).wait_send()
        if m == 1:
            for i, copies in enumerate(extras):
                for copy in copies:
                    copy.wait_send()
                extra_over(ccw[1] + 1 + i).wait_send()

    mine_at, other_at = pl.multiple_of(core * per, per), pl.multiple_of((1 - core) * per, per)

    def mix_out(r, p):
        cols = pl.ds(pl.multiple_of(core * half + p * PAIR, PAIR), PAIR)
        dst = mixtok.at[pl.ds(pl.multiple_of(r * per, per), per), cols]
        return (
            remote(mix_s.at[r, p, pl.ds(other_at, per)], dst, mx_send.at[r, p], mx_recv.at[r, p], partner),
            pltpu.make_async_copy(mix_s.at[r, p, pl.ds(mine_at, per)], dst, f_sem.at[r, p]),
        )

    def row_out(r):
        return [
            pltpu.make_async_copy(src.at[r], dst.at[r], o_sem.at[r, i])
            for i, (src, dst) in enumerate(((mix_s, mix_o), (la, ra_o), (ma, rb_o)))
        ]

    def attention(wqkv, pks, pvs, q_s, ka, va, kb, vb, s0, s1, s2, s3, oa, pst_a, pst_b, qe, kea, keb):
        loads = [
            x_load,
            pltpu.make_async_copy(wq.at[:, pl.ds(col, half)], wqkv.at[:, 0:half], load_sem.at[4 + batch]),
            pltpu.make_async_copy(wk.at[:, pl.ds(col, half)], wqkv.at[:, half : 2 * half], load_sem.at[5 + batch]),
            pltpu.make_async_copy(wv.at[:, pl.ds(col, half)], wqkv.at[:, 2 * half : 3 * half], load_sem.at[6 + batch]),
            pltpu.make_async_copy(pkey.at[:, pl.ds(col, half)], pks, load_sem.at[7 + batch]),
            pltpu.make_async_copy(pval.at[:, pl.ds(col, half)], pvs, load_sem.at[8 + batch]),
        ]
        for copy in loads:
            copy.start()
        greet([partner, nxt, prv] + peers)
        x_pair.start()
        for group in [wcross[0]] + cross + [wcross[1]] + extras:
            for copy in group:
                copy.start()
        for copy in shards + far_loads:
            copy.start()

        term = lax.broadcasted_iota(jnp.int32, (PAIR, 1), 0)
        term = jnp.where(term >= E, term - E, term)

        def key_terms(seg):
            off = jnp.where(jnp.logical_and(term < SEGS, seg != term), -BIG, 0.0)
            return off.T.astype(BF)

        for r in range(batch):
            for d in range(chips):
                at = pl.multiple_of(lax.rem(chip + d, chips) * tpc, tpc)
                seg = segs[r : r + 1, pl.ds(at, tpc)]
                if d == 0:
                    kea[r] = key_terms(seg)
                    on = jnp.logical_or(term == SEGS, jnp.logical_and(term < SEGS, seg == term))
                    qe[r] = jnp.where(on, 1.0, 0.0).T.astype(BF)
                else:
                    keb[r, (d - 1) * tpc : d * tpc] = key_terms(seg)
            unseen = jnp.logical_and(term == SEGS, vis[r : r + 1, :] == 0)
            keb[r, rem:] = jnp.where(unseen, -BIG, 0.0).T.astype(BF)

        def project(r, d, cb, with_q):
            x = xbuf[r, d, cb]
            if with_q:
                q = (dot(x, wqkv[:, 0:half]) * 0.125).astype(BF)
                for p in range(pairs):
                    q_s[r, p, pl.ds(pl.multiple_of(cb * per, per), per), :] = q[:, p * PAIR : (p + 1) * PAIR]
            for ref_a, ref_b, at in ((ka, kb, 1), (va, vb, 2)):
                y = dot(x, wqkv[:, at * half : (at + 1) * half]).astype(BF)
                for p in range(pairs):
                    val = y[:, p * PAIR : (p + 1) * PAIR]
                    if with_q:
                        ref_a[r, p, pl.ds(pl.multiple_of(cb * per, per), per), :] = val
                    else:
                        ref_b[r, p, pl.ds(pl.multiple_of((d - 1) * tpc + cb * per, per), per), :] = val

        for copy in loads:
            copy.wait()
        for r in range(batch):
            for p in range(pairs):
                kb[r, p, rem:, :] = pks[:, p * PAIR : (p + 1) * PAIR]
                vb[r, p, rem:, :] = pvs[:, p * PAIR : (p + 1) * PAIR]

        @pl.loop(0, 2 * batch)
        def _(i):
            pl.when(i == batch)(x_pair.wait_recv)
            late = lax.div(i, batch)
            project(lax.rem(i, batch), 0, core + late - 2 * core * late, True)

        outs = [
            pltpu.make_async_copy(src, dst, out_sem.at[i])
            for i, (src, dst) in enumerate(((q_s, q_o), (ka, ka_o), (va, va_o), (kb, kb_o), (vb, vb_o)))
        ]
        for copy in outs[:3]:
            copy.start()

        bufs = (s0, s1, s2, s3)

        def score(r, p, h, k_s, kext, buf):
            keys = k_s.shape[2]
            mine = lanes() < E if h == 0 else lanes() >= E
            q = jnp.where(mine, q_s[r, p], qe[r])
            k = jnp.where(mine, k_s[r, p], kext[r])
            buf[:, 0:keys] = dot(q, k, NT)

        def unit(r, p, after, u, k_s, v_s, kext, pst, p_hbm, finish, wait_slot):
            keys = k_s.shape[2]
            copy = pltpu.make_async_copy(pst.at[u], p_hbm.at[r, p], p_sem.at[u])
            pl.when(wait_slot)(copy.wait)
            tops, sums = [], []
            for h in range(2):
                score(after[0], after[1], h, k_s, kext, bufs[2 * (1 - u) + h])
                s = bufs[2 * u + h][:, 0:keys]
                top = jnp.max(s, axis=1, keepdims=True)
                prob = jnp.exp(s - top).astype(BF)
                pst[u, h] = prob
                mine = lanes() < E if h == 0 else lanes() >= E
                v = jnp.where(mine, v_s[r, p], jnp.ones((1, PAIR), BF))
                sums.append(dot(prob, v))
                tops.append(top)
            copy.start()
            low = lanes() < E
            finish(
                r,
                p,
                jnp.where(low, sums[0], sums[1]),
                pltpu.roll(jnp.where(low, sums[1], sums[0]), E, 1),
                jnp.where(low, tops[0], tops[1]),
            )

        def finish_a(r, p, o, l, m):
            oa[r, p], la[r, p], ma[r, p] = o, l, m

        def finish_b(r, p, o, l, m):
            top = jnp.maximum(ma[r, p], m)
            w_a, w_b = jnp.exp(ma[r, p] - top), jnp.exp(m - top)
            inv = 1.0 / (w_a * la[r, p] + w_b * l)
            r_a, r_b = w_a * inv, w_b * inv
            mix_s[r, p] = (oa[r, p] * r_a + o * r_b).astype(BF)
            la[r, p], ma[r, p] = r_a, r_b

        def drain(pst, p_hbm):
            for u in range(2):
                pltpu.make_async_copy(pst.at[u], p_hbm.at[0, 0], p_sem.at[u]).wait()

        args_a = (ka, va, kea, pst_a, pa_o, finish_a)
        for h in range(2):
            score(0, 0, h, ka, kea, bufs[h])
        count = batch * pairs

        @pl.loop(0, count // 2)
        def _(i):
            for u in range(2):
                j = 2 * i + u
                after = jnp.minimum(j + 1, count - 1)
                unit(
                    lax.div(j, pairs), lax.rem(j, pairs), (lax.div(after, pairs), lax.rem(after, pairs)),
                    u, *args_a, i > 0,
                )

            @pl.when(i == 1)
            def _():
                hop(0, 1)

        drain(pst_a, pa_o)
        hop(0, 2)

        args_b = (kb, vb, keb, pst_b, pb_o, finish_b)

        @pl.loop(0, batch)
        def _(r):
            for d in range(1, chips):
                remote(
                    x_own.at[r], xbuf.at[r, d, core], y_send.at[r, d - 1], y_recv.at[r, d - 1], peers[d - 1]
                ).wait_recv()
            forward = remote(
                xbuf.at[r, 1:, core], xbuf.at[r, 1:, core], d_send.at[r], d_recv.at[r], partner
            )
            forward.start()

            @pl.loop(0, 2 * (chips - 1))
            def _(i):
                pl.when(i == chips - 1)(forward.wait_recv)
                late = lax.div(i, chips - 1)
                project(r, lax.rem(i, chips - 1) + 1, core + late - 2 * core * late, False)

            for h in range(2):
                score(r, 0, h, kb, keb, bufs[h])

            @pl.loop(0, pairs // 2)
            def _(i):
                for u in range(2):
                    p = 2 * i + u
                    unit(r, p, (r, jnp.minimum(p + 1, pairs - 1)), u, *args_b, i > 0)
                for step in range(batch):

                    @pl.when(jnp.logical_and(r == step, i == 0))
                    def _(step=step):
                        hop(0, 3 + step)

            drain(pst_b, pb_o)
            for p in range(pairs):
                for copy in mix_out(r, p):
                    copy.start()
            for copy in row_out(r):
                copy.start()
            forward.wait_send()

        for copy in outs[3:]:
            copy.start()
        for s in range(3 + batch, cw[0] + 2):
            hop(0, s)
        hop(1, 1)
        x_pair.wait_send()
        for copy in outs:
            copy.wait()

    vm = pltpu.VMEM
    keys = max(tpc, keys_b)
    pl.run_scoped(
        attention,
        vm((width, 3 * half), BF),
        vm((P_SIZE, half), BF),
        vm((P_SIZE, half), BF),
        vm((batch, pairs, tpc, PAIR), BF),
        vm((batch, pairs, tpc, PAIR), BF),
        vm((batch, pairs, tpc, PAIR), BF),
        vm((batch, pairs, keys_b, PAIR), BF),
        vm((batch, pairs, keys_b, PAIR), BF),
        *([vm((tpc, keys), F32)] * 4),
        vm((batch, pairs, tpc, PAIR), F32),
        vm((2, 2, tpc, tpc), BF),
        vm((2, 2, tpc, keys_b), BF),
        vm((batch, tpc, PAIR), BF),
        vm((batch, tpc, PAIR), BF),
        vm((batch, keys_b, PAIR), BF),
    )

    tile = min(512, hidden)
    tiles = hidden // tile
    total = 2 * chips * tiles
    chunk = 64

    def feed_forward(n1, n1l, sc1, inv1, acc, slope, pre0, pre1, gt, gtl, bst):
        for copy in far_loads:
            copy.wait()
        for r in range(batch):
            for p in range(pairs):
                for copy in mix_out(r, p):
                    copy.wait()

        @pl.loop(0, width // 256)
        def _(j):
            at = pl.ds(pl.multiple_of(j * 256, 256), 256)
            acc[:, at] = dot(mixtok[...], wo[:, at])

        def by_rows(body):
            for r in range(batch):

                @pl.loop(0, per // chunk)
                def _(i, r=r):
                    inner = pl.ds(pl.multiple_of(i * chunk, chunk), chunk)
                    body(r, inner, pl.ds(pl.multiple_of(r * per + i * chunk, chunk), chunk))

        def norm_one(r, inner, at):
            z = acc[at] + xbuf[r, 0, core, inner].astype(F32)
            c = z - mean_of(z)
            inv = lax.rsqrt(mean_of(c * c) + norm_eps)
            s = c * inv
            n = s * g1[...] + b1[...]
            n1[at], n1l[at], sc1[at], inv1[at] = n, n.astype(BF), s, inv
            acc[at] = jnp.zeros_like(z)

        by_rows(norm_one)
        for copy in shards:
            copy.wait()

        def split(j):
            slot = lax.div(j, tiles)
            at = pl.ds(pl.multiple_of(lax.rem(j, tiles) * tile, tile), tile)
            return lax.div(slot, 2), lax.rem(slot, 2), at

        def up_tile(j, buf):
            d, c, at = split(j)
            buf[...] = dot(n1l[...], up[d, c, :, at])

        pres = (pre0, pre1)
        up_tile(0, pre0)

        @pl.loop(0, total // 2)
        def _(i):
            @pl.when(i == tiles - 1)
            def _():
                gathered(0)
                hop(1, 2)

            @pl.when(i == tiles)
            def _():
                take_extras()
                hop(1, 3)
                gathered(1)

            for u in range(2):
                j = 2 * i + u
                up_tile(jnp.minimum(j + 1, total - 1), pres[1 - u])
                v = pres[u][...]
                cdf = 0.5 * (1.0 + lax.erf(v * root_half))
                a = (v * cdf).astype(BF)
                d, c, at = split(j)
                slope[j] = cdf + v * jnp.exp(-0.5 * v * v) * inv_root_tau
                acc[...] += dot(a, dn[d, c, at, :])

        def norm_two(r, inner, at):
            z = n1[at] + acc[at]
            c = z - mean_of(z)
            inv = lax.rsqrt(mean_of(c * c) + norm_eps)
            s = c * inv
            bst[at] = (s * g2[...] + b2[...]).astype(BF)
            t = ogs[r, inner] * g2[...]
            g = inv * (t - mean_of(t) - s * mean_of(t * s))
            gt[at], gtl[at] = g, g.astype(BF)
            acc[at] = jnp.zeros_like(z)

        by_rows(norm_two)
        outs = [
            pltpu.make_async_copy(bst.at[r * per : (r + 1) * per], block_o.at[r], out_sem.at[r])
            for r in range(batch)
        ]
        for copy in outs:
            copy.start()

        def down_back(j, buf):
            d, c, at = split(j)
            buf[...] = dot(gtl[...], dn[d, c, at, :], NT)

        down_back(0, pre0)

        @pl.loop(0, total // 2)
        def _(i):
            for u in range(2):
                j = 2 * i + u
                down_back(jnp.minimum(j + 1, total - 1), pres[1 - u])
                g = (pres[u][...] * slope[j]).astype(BF)
                d, c, at = split(j)
                acc[...] += dot(g, up[d, c, :, at], NT)

        def norm_back(r, inner, at):
            t = (gt[at] + acc[at]) * g1[...]
            s = sc1[at]
            g = inv1[at] * (t - mean_of(t) - s * mean_of(t * s))
            gt[at], gtl[at] = g, g.astype(BF)

        by_rows(norm_back)
        for r in range(batch):
            copy = pltpu.make_async_copy(gt.at[r * per : (r + 1) * per], gsum_o.at[r], out_sem.at[batch + r])
            copy.start()
            outs.append(copy)

        mine = pl.ds(mine_at, per)
        for side in range(2):
            base = (1 - core) * half if side == 0 else core * half
            g = dot(gtl[...], wo[pl.ds(pl.multiple_of(base, half), half), :], NT).astype(BF)
            for p in range(pairs):
                gst[side, p] = g[:, p * PAIR : (p + 1) * PAIR]
            for p in range(pairs):
                for r in range(batch):
                    src, dst = gst.at[side, p, r * per : (r + 1) * per], gatt_o.at[r, p, mine]
                    if side == 0:
                        copy = remote(src, dst, gm_send.at[r, p], gm_recv.at[r, p], partner)
                    else:
                        copy = pltpu.make_async_copy(src, dst, f_sem.at[r, p])
                    copy.start()
                    outs.append(copy)
        for r in range(batch):
            for copy in cross[r]:
                copy.wait_send()
            for copy in row_out(r):
                copy.wait()
        for m in range(2):
            sent(m)
        for copy in outs:
            copy.wait()

    pl.run_scoped(
        feed_forward,
        vm((tokens, width), F32),
        vm((tokens, width), BF),
        vm((tokens, width), F32),
        vm((tokens, 1), F32),
        vm((tokens, width), F32),
        vm((total, tokens, tile), F32),
        vm((tokens, tile), F32),
        vm((tokens, tile), F32),
        vm((tokens, width), F32),
        vm((tokens, width), BF),
        vm((tokens, width), BF),
    )


def forward_call(rows, chips, x, segs, vis, wq, wk, wv, pkey, pval, w_out, w_up, w_dn, og, g1, b1, g2, b2):
    batch, per, width = x.shape
    tpc, half = 2 * per, width // 2
    keys_b = (chips - 1) * tpc + P_SIZE
    pairs = half // PAIR
    tokens = batch * per
    steps = rows // 2
    out = lambda dt, *s: jax.ShapeDtypeStruct(s, dt)
    shapes = (
        out(BF, batch, pairs, tpc, PAIR),
        out(BF, batch, pairs, tpc, PAIR),
        out(BF, batch, pairs, tpc, PAIR),
        out(BF, batch, pairs, keys_b, PAIR),
        out(BF, batch, pairs, keys_b, PAIR),
        out(BF, batch, pairs, 2, tpc, tpc),
        out(BF, batch, pairs, 2, tpc, keys_b),
        out(F32, batch, pairs, tpc, PAIR),
        out(F32, batch, pairs, tpc, PAIR),
        out(BF, batch, pairs, tpc, PAIR),
        out(BF, batch, per, width),
        out(F32, batch, per, width),
        out(BF, batch, pairs, tpc, PAIR),
    )
    dma = pltpu.SemaphoreType.DMA
    vm = pltpu.VMEM
    scratch = [
        vm((batch, chips, 2, per, width), BF),
        vm((chips, 2, *w_up.shape), BF),
        vm((chips, 2, *w_dn.shape), BF),
        vm((width, width), BF),
        vm((tokens, width), BF),
        vm((batch, pairs, tpc, PAIR), F32),
        vm((batch, pairs, tpc, PAIR), F32),
        vm((batch, pairs, tpc, PAIR), BF),
        vm((batch, per, width), F32),
        vm((2, pairs, tokens, PAIR), BF),
        dma((9 + batch,)), dma((5,)), dma((2,)), dma, dma,
        dma((batch, chips - 1)), dma((batch, chips - 1)),
        dma((batch,)), dma((batch,)),
        dma((batch, pairs)), dma((batch, 3)),
        dma((batch, pairs)), dma((batch, pairs)),
        dma((2, chips - 1)), dma((2, chips - 1)),
        dma((rows, chips - 1)), dma((rows, chips - 1)),
        dma((2,)), dma((2,)),
        dma((2, steps + 1, 2)), dma((2, steps + 1, 2)),
        dma((2, steps + 1, 2)), dma((2, steps + 1, 2)),
        dma((rows,)), dma((rows,)),
        dma((batch, pairs)), dma((batch, pairs)),
    ]
    return pl.pallas_call(
        functools.partial(forward_kernel, rows, chips),
        out_shape=shapes,
        in_specs=[ANY] + [VM] * 2 + [ANY] * 9 + [VM] * 4,
        out_specs=[ANY] * len(shapes),
        scratch_shapes=scratch,
        compiler_params=pltpu.CompilerParams(
            collective_id=0, has_side_effects=True, vmem_limit_bytes=VMEM_LIMIT
        ),
        name="forward_and_ffn",
    )(x, segs, vis, wq, wk, wv, pkey, pval, w_out, w_up, w_dn, og, g1, b1, g2, b2)


def backward_kernel(
    rows, chips,
    g_i, mix_i, ra_i, rb_i, q_i, ka_i, va_i, kb_i, vb_i, pa_i, pb_i, wq, wk, wv, gs_i,
    ig_o, pk_o, pv_o,
    g_s, mix_s, ra, rb, q_s, ka, va, kb, vb, w_s, gs, pin_a, pin_b, s0, s1, s2, s3, do0, do1,
    dq, dks, dvs, psum, half_b, send_b, got_b, y_out, y_in, half_a, send_a, got_a,
    pr_in, pr_y, p_full,
    load_sem, p_sem, o_sem, db_send, db_recv, y_send, y_recv, da_send, da_recv,
    p1_send, p1_recv, p2_send, p2_recv, p3_send, p3_recv, p4_send, p4_recv,
):
    batch, pairs, tpc = q_s.shape[0], q_s.shape[1], q_s.shape[2]
    per = tpc // 2
    rem = (chips - 1) * tpc
    width, half = w_s.shape[1], w_s.shape[2]
    row, wide, core, chip = place()
    partner = (row, wide + 1 - 2 * core)
    peers = [(row, 2 * lax.rem(chip - d + chips, chips) + core) for d in range(1, chips)]
    back = [(row, 2 * lax.rem(chip + d, chips) + core) for d in range(1, chips)]
    plane = [(lax.rem(row + t, rows), wide) for t in range(1, rows)]

    col = pl.multiple_of(core * half, half)
    pairs_of = (
        (g_i, g_s), (mix_i, mix_s), (rb_i, rb), (kb_i, kb), (vb_i, vb), (q_i, q_s),
        (wk.at[:, pl.ds(col, half)], w_s.at[1]), (wv.at[:, pl.ds(col, half)], w_s.at[2]),
        (ra_i, ra), (ka_i, ka), (va_i, va), (wq.at[:, pl.ds(col, half)], w_s.at[0]), (gs_i, gs),
    )
    loads = [pltpu.make_async_copy(src, dst, load_sem.at[i]) for i, (src, dst) in enumerate(pairs_of)]

    def fetch(pin, p_hbm, r, p, u):
        return pltpu.make_async_copy(p_hbm.at[r, p], pin.at[u], p_sem.at[u])

    for copy in loads[:6]:
        copy.start()
    for u in range(2):
        fetch(pin_b, pb_i, 0, u, u).start()
    for copy in loads[6:]:
        copy.start()
    greet([partner] + peers + plane)
    for copy in loads[:6]:
        copy.wait()

    bufs, dos = (s0, s1, s2, s3), (do0, do1)

    def first(r, p, u, v_s, scale):
        keys = v_s.shape[2]
        g = g_s[r, p].astype(F32) * scale[r, p]
        do = g.astype(BF)
        dos[u][...] = do
        t = g * mix_s[r, p].astype(F32)
        lane = lanes()
        for h in range(2):
            mine = lane < E if h == 0 else lane >= E
            delta = jnp.sum(jnp.where(mine, t, 0.0), axis=1, keepdims=True)
            hi = delta.astype(BF)
            left = delta - hi.astype(F32)
            mid = left.astype(BF)
            low = (left - mid.astype(F32)).astype(BF)
            at = E if h == 0 else 0
            ext = jnp.where(
                lane == at, -hi, jnp.where(lane == at + 1, -mid, jnp.where(lane == at + 2, -low, jnp.zeros((1, PAIR), BF)))
            )
            one = jnp.where(jnp.logical_and(lane >= at, lane < at + 3), 1.0, 0.0).astype(BF)
            bufs[2 * u + h][:, 0:keys] = dot(
                jnp.where(mine, do, ext), jnp.where(mine, v_s[r, p], one), NT
            )

    def second(r, p, u, k_s, pin, start_dq, prefix):
        keys = k_s.shape[2]
        q2, k2, do = q_s[r, p], k_s[r, p], dos[u][...]
        do_t, q_t = do.T, q2.T
        gq, gk, gv = [], [], []
        for h in range(2):
            prob = pin[u, h]
            ds = (prob.astype(F32) * bufs[2 * u + h][:, 0:keys]).astype(BF)
            at = slice(h * E, (h + 1) * E)
            gv.append(dot(do_t[at], prob))
            gk.append(dot(q_t[at], ds))
            gq.append(dot(ds, k2))
        low = lanes() < E
        grad = jnp.where(low, gq[0], gq[1])
        dq[r, p] = grad if start_dq else dq[r, p] + grad
        cols = pl.ds(pl.multiple_of(p * PAIR, PAIR), PAIR)
        for ref, parts, k in ((dks, gk, 0), (dvs, gv, 1)):
            val = jnp.concatenate(parts, axis=0).T
            if prefix:
                ref[0:rem, cols] = val[:rem].astype(BF)
                psum[k * P_SIZE : (k + 1) * P_SIZE, cols] += val[rem:]
            else:
                ref[0:tpc, cols] = val.astype(BF)

    def group(r, k_s, v_s, scale, pin, p_hbm, start_dq, prefix):
        first(r, 0, 0, v_s, scale)

        @pl.loop(0, pairs // 2)
        def _(i):
            for u in range(2):
                p = 2 * i + u
                fetch(pin, p_hbm, r, p, u).wait()
                first(r, jnp.minimum(p + 1, pairs - 1), 1 - u, v_s, scale)
                second(r, p, u, k_s, pin, start_dq, prefix)

                @pl.when(i < pairs // 2 - 1)
                def _():
                    fetch(pin, p_hbm, r, p + 2, u).start()

    def to_inputs(at):
        keys = dot(dks[at], w_s[1], NT)
        return keys + dot(dvs[at], w_s[2], NT)

    psum[...] = jnp.zeros_like(psum)
    tails = []
    y_copies = []
    b_copies = []

    def chip_sum(r):
        for copy in b_copies[r]:
            copy.wait_recv()
        for d in range(1, chips):
            y_out[r, d - 1] = (half_b[r, d - 1] + got_b[r, d - 1]).astype(BF)
        copies = [
            remote(
                y_out.at[r, d - 1], y_in.at[r, d - 1], y_send.at[r, d - 1], y_recv.at[r, d - 1], back[d - 1]
            )
            for d in range(1, chips)
        ]
        for copy in copies:
            copy.start()
        y_copies.append(copies)

    for r in range(batch):
        group(r, kb, vb, rb, pin_b, pb_i, True, True)
        if r + 1 < batch:
            for u in range(2):
                fetch(pin_b, pb_i, r + 1, u, u).start()
        else:
            for u in range(2):
                fetch(pin_a, pa_i, 0, u, u).start()
        if r == 0:
            for copy in loads[6:]:
                copy.wait()
        copies = []
        for d in range(1, chips):
            at = pl.ds(pl.multiple_of((d - 1) * tpc + (1 - core) * per, per), per)
            send_b[r, d - 1] = to_inputs(at)
            copy = remote(
                send_b.at[r, d - 1], got_b.at[r, d - 1], db_send.at[r, d - 1], db_recv.at[r, d - 1], partner
            )
            copy.start()
            copies.append(copy)
        b_copies.append(copies)
        for d in range(1, chips):
            at = pl.ds(pl.multiple_of((d - 1) * tpc + core * per, per), per)
            half_b[r, d - 1] = to_inputs(at)
        chip_sum(r)

    size = 2 * P_SIZE // rows

    def part(at):
        return pl.ds(pl.multiple_of(at * size, size), size)

    p_one = [
        remote(psum.at[part(plane[t - 1][0])], pr_in.at[t - 1], p1_send.at[t - 1], p1_recv.at[t - 1], plane[t - 1])
        for t in range(1, rows)
    ]
    for copy in p_one:
        copy.start()

    for r in range(batch):
        group(r, ka, va, ra, pin_a, pa_i, False, False)
        if r + 1 < batch:
            for u in range(2):
                fetch(pin_a, pa_i, r + 1, u, u).start()
        for side in range(2):
            block = pl.multiple_of(((1 - core) if side == 0 else core) * per, per)
            at = pl.ds(block, per)
            part_in = to_inputs(at)
            for p in range(pairs):
                dvs[at, p * PAIR : (p + 1) * PAIR] = (dq[r, p, at, :]).astype(BF)
            val = part_in + 0.125 * dot(dvs[at], w_s[0], NT)
            if side == 0:
                send_a[r] = val
                copy = remote(send_a.at[r], got_a.at[r], da_send.at[r], da_recv.at[r], partner)
                copy.start()
                tails.append(copy)
            else:
                half_a[r] = gs[r] + val
        if r == 0:
            for copy in p_one:
                copy.wait_recv()
            total = psum[part(row)]
            for t in range(1, rows):
                total = total + pr_in[t - 1]
            pr_y[0] = total
            p_two = [
                remote(pr_y.at[0], pr_y.at[d], p2_send.at[d - 1], p2_recv.at[d - 1], peers[d - 1])
                for d in range(1, chips)
            ]
            for copy in p_two:
                copy.start()
        if r == batch - 1:
            for copy in p_two:
                copy.wait()
            whole = jnp.zeros((size, half), F32)
            for c in range(chips):
                whole = whole + pr_y[lax.rem(c - chip + chips, chips)]
            p_full[part(row)] = whole
            p_three = [
                remote(p_full.at[part(row)], p_full.at[part(row)], p3_send.at[t - 1], p3_recv.at[t - 1], plane[t - 1])
                for t in range(1, rows)
            ]
            for copy in p_three:
                copy.start()

    outs = []
    for r in range(batch):
        tails[r].wait()
        for copy in y_copies[r]:
            copy.wait()
        val = half_a[r] + got_a[r]
        for d in range(1, chips):
            val = val + y_in[r, d - 1].astype(F32)
        half_a[r] = val
        copy = pltpu.make_async_copy(half_a.at[r], ig_o.at[r], o_sem.at[r])
        copy.start()
        outs.append(copy)
    for copy in p_three:
        copy.wait()
    cols = pl.ds(col, half)
    for k, ref in enumerate((pk_o, pv_o)):
        src = p_full.at[k * P_SIZE : (k + 1) * P_SIZE]
        copy = remote(src, ref.at[:, cols], p4_send.at[k], p4_recv.at[k], partner)
        copy.start()
        outs.append(copy)
        copy = pltpu.make_async_copy(src, ref.at[:, cols], o_sem.at[batch + k])
        copy.start()
        outs.append(copy)
    for copies in b_copies:
        for copy in copies:
            copy.wait_send()
    for copy in p_one:
        copy.wait_send()
    for copy in outs:
        copy.wait()


def backward_call(rows, chips, g, mix, ra, rb, q, ka, va, kb, vb, pa, pb, wq, wk, wv, gs):
    batch, pairs, tpc, _ = q.shape
    keys_a, keys_b = ka.shape[2], kb.shape[2]
    per, width = gs.shape[1], gs.shape[2]
    half = width // 2
    size = 2 * P_SIZE // rows
    out = lambda dt, *s: jax.ShapeDtypeStruct(s, dt)
    dma = pltpu.SemaphoreType.DMA
    vm = pltpu.VMEM
    far = chips - 1
    keys = max(keys_a, keys_b)
    return pl.pallas_call(
        functools.partial(backward_kernel, rows, chips),
        out_shape=(
            out(F32, batch, per, width),
            out(F32, P_SIZE, width),
            out(F32, P_SIZE, width),
        ),
        in_specs=[ANY] * 15,
        out_specs=[ANY] * 3,
        scratch_shapes=[
            vm((batch, pairs, tpc, PAIR), BF),
            vm((batch, pairs, tpc, PAIR), BF),
            vm((batch, pairs, tpc, PAIR), F32),
            vm((batch, pairs, tpc, PAIR), F32),
            vm((batch, pairs, tpc, PAIR), BF),
            vm((batch, pairs, keys_a, PAIR), BF),
            vm((batch, pairs, keys_a, PAIR), BF),
            vm((batch, pairs, keys_b, PAIR), BF),
            vm((batch, pairs, keys_b, PAIR), BF),
            vm((3, width, half), BF),
            vm((batch, per, width), F32),
            vm((2, 2, tpc, keys_a), BF),
            vm((2, 2, tpc, keys_b), BF),
            *([vm((tpc, keys), F32)] * 4),
            *([vm((tpc, PAIR), BF)] * 2),
            vm((batch, pairs, tpc, PAIR), F32),
            vm((keys, half), BF),
            vm((keys, half), BF),
            vm((2 * P_SIZE, half), F32),
            vm((batch, far, per, width), F32),
            vm((batch, far, per, width), F32),
            vm((batch, far, per, width), F32),
            vm((batch, far, per, width), BF),
            vm((batch, far, per, width), BF),
            vm((batch, per, width), F32),
            vm((batch, per, width), F32),
            vm((batch, per, width), F32),
            vm((rows - 1, size, half), F32),
            vm((chips, size, half), F32),
            vm((2 * P_SIZE, half), F32),
            dma((13,)), dma((2,)), dma((batch + 2,)),
            dma((batch, far)), dma((batch, far)),
            dma((batch, far)), dma((batch, far)),
            dma((batch,)), dma((batch,)),
            dma((rows - 1,)), dma((rows - 1,)),
            dma((far,)), dma((far,)),
            dma((rows - 1,)), dma((rows - 1,)),
            dma((2,)), dma((2,)),
        ],
        compiler_params=pltpu.CompilerParams(
            collective_id=2, has_side_effects=True, vmem_limit_bytes=VMEM_LIMIT
        ),
        name="attention_backward",
    )(g, mix, ra, rb, q, ka, va, kb, vb, pa, pb, wq, wk, wv, gs)


def on_device(
    rows, chips,
    hidden_in, segments, prefix_vis, prefix_key, prefix_value, w_query, w_key, w_value, w_out,
    norm1_gain, norm1_bias, w_up, w_down, norm2_gain, norm2_bias, out_grad,
):
    x = jnp.transpose(hidden_in, (1, 0, 2))
    og = jnp.transpose(out_grad, (1, 0, 2))
    flat = lambda v: v.reshape(1, -1)
    q, ka, va, kb, vb, pa, pb, ra, rb, mix, block, gs, g = forward_call(
        rows, chips, x, segments, prefix_vis, w_query, w_key, w_value, prefix_key, prefix_value,
        w_out, w_up, w_down, og, flat(norm1_gain), flat(norm1_bias), flat(norm2_gain), flat(norm2_bias),
    )
    input_grad, pk_grad, pv_grad = backward_call(
        rows, chips, g, mix, ra, rb, q, ka, va, kb, vb, pa, pb, w_query, w_key, w_value, gs
    )
    return (
        jnp.transpose(block, (1, 0, 2)),
        jnp.transpose(input_grad, (1, 0, 2)),
        pk_grad,
        pv_grad,
    )


def solution(mesh):
    rows, chips = mesh.shape["rows"], mesh.shape["wide"] // 2
    act = P("wide", "rows", None)
    per_row = P("rows", None)
    in_specs = (
        act, per_row, per_row, *([P()] * 8), P(None, "wide"), P("wide", None), P(), P(), act,
    )
    out_specs = (act, act, P(), P())
    return jax.shard_map(
        functools.partial(on_device, rows, chips),
        mesh=mesh,
        in_specs=in_specs,
        out_specs=out_specs,
        check_vma=False,
    )
```

```python
import functools

import jax
import jax.numpy as jnp
from jax import lax
from jax.experimental import pallas as pl
from jax.experimental.pallas import tpu as pltpu
from jax.sharding import PartitionSpec as P

E = 64
P_SIZE = 64
SEGS = 4
PAIR = 2 * E
BIG = 1e30
norm_eps = 1e-05
root_half = 0.7071067811865476
inv_root_tau = 0.3989422804014327

BF = jnp.bfloat16
F32 = jnp.float32
MESH = pl.DeviceIdType.MESH
ANY = pl.BlockSpec(memory_space=pl.ANY)
VM = pl.BlockSpec(memory_space=pltpu.VMEM)
NN = (((1,), (0,)), ((), ()))
NT = (((1,), (1,)), ((), ()))
VMEM_LIMIT = 66 * 1024 * 1000


def dot(a, b, dims=NN):
    return lax.dot_general(a, b, dims, preferred_element_type=F32)


def lanes():
    return lax.broadcasted_iota(jnp.int32, (1, PAIR), 1)


def place():
    row, wide = lax.axis_index("rows"), lax.axis_index("wide")
    return row, wide, lax.rem(wide, 2), lax.div(wide, 2)


def greet(devices):
    barrier = pltpu.get_barrier_semaphore()
    for dev in devices:
        pl.semaphore_signal(barrier, inc=1, device_id=dev, device_id_type=MESH)
    pl.semaphore_wait(barrier, len(devices))


def remote(src, dst, send, recv, dev):
    return pltpu.make_async_remote_copy(
        src_ref=src, dst_ref=dst, send_sem=send, recv_sem=recv, device_id=dev, device_id_type=MESH
    )


def ring_pos(row, rows):
    half = rows // 2
    z, x = lax.div(row, 2), lax.rem(row, 2)
    return z + x * (2 * half - 1 - 2 * z)


def ring_row(pos, rows):
    pos = lax.rem(pos + 2 * rows, rows)
    upper = lax.div(pos, rows // 2)
    return 2 * pos + upper * (2 * rows - 1 - 4 * pos)


def mean_of(value):
    return jnp.mean(value, axis=-1, keepdims=True)


def forward_kernel(
    rows, chips,
    x_own, segs, vis, wq, wk, wv, pkey, pval, w_out, w_up, w_dn, og, g1, b1, g2, b2,
    q_o, ka_o, va_o, kb_o, vb_o, pa_o, pb_o, ra_o, rb_o, mix_o, block_o, gsum_o, gatt_o,
    xbuf, up, dn, wo, mixtok, la, ma, mix_s, ogs, gst,
    load_sem, out_sem, p_sem, x_send, x_recv, y_send, y_recv, d_send, d_recv, f_sem, o_sem,
    mx_send, mx_recv, g_send, g_recv, e_send, e_recv, sh_send, sh_recv, r_send, r_recv, k_send, k_recv,
    l_send, l_recv, gm_send, gm_recv,
):
    per, batch, width = x_own.shape
    tpc = 2 * per
    rem = (chips - 1) * tpc
    keys_b = rem + P_SIZE
    half = width // 2
    pairs = half // PAIR
    hidden = up.shape[3]
    tokens = batch * per
    row, wide, core, chip = place()
    partner = (row, wide + 1 - 2 * core)
    pos = ring_pos(row, rows)
    nxt = (ring_row(pos + 1, rows), wide)
    prv = (ring_row(pos - 1, rows), wide)
    peers = [(row, 2 * lax.rem(chip - d + chips, chips) + core) for d in range(1, chips)]
    mats = ((w_up, up), (w_dn, dn))
    cw = (rows // 2, 3)
    ccw = (rows // 2 - 1, 3)
    cuts = (1, 2 if hidden // rows >= 64 else 1)

    col = pl.multiple_of(core * half, half)
    far_loads = [
        pltpu.make_async_copy(w_up, up.at[0, core], load_sem.at[0]),
        pltpu.make_async_copy(w_dn, dn.at[0, core], load_sem.at[1]),
        pltpu.make_async_copy(w_out, wo, load_sem.at[2]),
    ] + [pltpu.make_async_copy(og.at[:, r], ogs.at[r], load_sem.at[3 + r]) for r in range(batch)]

    x_pair = remote(xbuf.at[:, 0, core], xbuf.at[:, 0, core], x_send, x_recv, partner)
    cross = [
        [
            remote(xbuf.at[r, 0, core], xbuf.at[r, d, core], y_send.at[r, d - 1], y_recv.at[r, d - 1], peers[d - 1])
            for d in range(1, chips)
        ]
        for r in range(batch)
    ]

    def piece(ref, row_at, cut=0, cuts_of=1):
        size = ref.shape[-2] // rows
        sub = size // cuts_of
        return pl.ds(pl.multiple_of(row_at * size + cut * sub, sub), sub)

    def w_cross(m, row_at, cut, cuts_of, send, recv):
        src, dst = mats[m]
        at = piece(src, row_at, cut, cuts_of)
        return [
            remote(src.at[at], dst.at[d, core, at], send.at[d - 1], recv.at[d - 1], peers[d - 1])
            for d in range(1, chips)
        ]

    split_cross = [
        [w_cross(m, row, h, cuts[m], g_send.at[m, h], g_recv.at[m, h]) for h in range(cuts[m])] for m in range(2)
    ]
    wcross = [sum(group, []) for group in split_cross]
    far_off = range(ccw[1] + 1, rows - cw[1])
    extras = sum([w_cross(1, ring_row(pos + o, rows), 0, 1, e_send.at[o], e_recv.at[o]) for o in far_off], [])
    shards = [
        remote(mats[m][0], mats[m][1].at[0, core], sh_send.at[m], sh_recv.at[m], partner) for m in range(2)
    ]

    def place_of(s, way):
        return ring_row(pos - s if way == 0 else pos + s, rows)

    def ring_copy(m, s, way, h):
        buf = mats[m][1]
        ref = buf.at[1:, core, piece(buf, place_of(s - 1, way), h, cuts[m])]
        return remote(ref, ref, r_send.at[m, s, way, h], r_recv.at[m, s, way, h], nxt if way == 0 else prv)

    def hand_over(m, s, way, h):
        buf = mats[m][1]
        ref = buf.at[1:, core, piece(buf, place_of(s, way), h, cuts[m])]
        return remote(ref, ref, k_send.at[m, s, way, h], k_recv.at[m, s, way, h], partner)

    def ways(m, s):
        return range(2 if s <= ccw[m] else 1)

    def hop(m, s, h=0):
        if s > cw[m] + 1 or h >= cuts[m]:
            return
        if s == 1:
            for copy in split_cross[m][h]:
                copy.wait_recv()
        else:
            for way in ways(m, s - 1):
                ring_copy(m, s - 1, way, h).wait_recv()
        if s <= cw[m]:
            for way in ways(m, s):
                ring_copy(m, s, way, h).start()
        for way in ways(m, s - 1) if s > 1 else range(1):
            hand_over(m, s - 1, way, h).start()

    def extra_over(o):
        buf = mats[1][1]
        ref = buf.at[1:, core, piece(buf, place_of(o, 1))]
        return remote(ref, ref, l_send.at[o], l_recv.at[o], partner)

    def take_extras():
        for copy in extras:
            copy.wait_recv()
        for o in far_off:
            extra_over(o).start()

    def all_over(m):
        copies = [hand_over(m, 0, 0, h) for h in range(cuts[m])]
        for s in range(1, cw[m] + 1):
            copies += [hand_over(m, s, way, h) for way in ways(m, s) for h in range(cuts[m])]
        if m == 1:
            copies += [extra_over(o) for o in far_off]
        return copies

    def gathered(m):
        for copy in all_over(m):
            copy.wait_recv()

    def sent(m):
        for copy in wcross[m] + all_over(m) + (extras if m == 1 else []):
            copy.wait_send()
        for s in range(1, cw[m] + 1):
            for way in ways(m, s):
                for h in range(cuts[m]):
                    ring_copy(m, s, way, h).wait_send()

    mine_at, other_at = pl.multiple_of(core * per, per), pl.multiple_of((1 - core) * per, per)

    def mix_out(r, p):
        cols = pl.ds(pl.multiple_of(core * half + p * PAIR, PAIR), PAIR)
        dst = mixtok.at[pl.ds(pl.multiple_of(r * per, per), per), cols]
        return (
            remote(mix_s.at[r, p, pl.ds(other_at, per)], dst, mx_send.at[r, p], mx_recv.at[r, p], partner),
            pltpu.make_async_copy(mix_s.at[r, p, pl.ds(mine_at, per)], dst, f_sem.at[r, p]),
        )

    def row_out(r):
        return [
            pltpu.make_async_copy(src.at[r], dst.at[r], o_sem.at[r, i])
            for i, (src, dst) in enumerate(((mix_s, mix_o), (la, ra_o), (ma, rb_o)))
        ]

    def attention(wqkv, pks, pvs, q_s, ka, va, kb, vb, s0, s1, s2, s3, oa, pst_a, pst_b, qe, kea, keb, xraw):
        x_load = pltpu.make_async_copy(x_own, xraw, load_sem.at[3 + batch])
        loads = [
            pltpu.make_async_copy(wq.at[:, pl.ds(col, half)], wqkv.at[:, 0:half], load_sem.at[4 + batch]),
            pltpu.make_async_copy(wk.at[:, pl.ds(col, half)], wqkv.at[:, half : 2 * half], load_sem.at[5 + batch]),
            pltpu.make_async_copy(wv.at[:, pl.ds(col, half)], wqkv.at[:, 2 * half : 3 * half], load_sem.at[6 + batch]),
            pltpu.make_async_copy(pkey.at[:, pl.ds(col, half)], pks, load_sem.at[7 + batch]),
            pltpu.make_async_copy(pval.at[:, pl.ds(col, half)], pvs, load_sem.at[8 + batch]),
        ]
        barrier = pltpu.get_barrier_semaphore()
        friends = [partner, nxt, prv] + peers
        for dev in friends:
            pl.semaphore_signal(barrier, inc=1, device_id=dev, device_id_type=MESH)
        x_load.start()
        for copy in loads:
            copy.start()
        x_load.wait()
        for r in range(batch):
            xbuf[r, 0, core] = xraw[:, r, :]
        pl.semaphore_wait(barrier, len(friends))
        x_pair.start()
        for group in [wcross[0]] + cross + [wcross[1]] + [extras]:
            for copy in group:
                copy.start()
        for copy in shards + far_loads:
            copy.start()

        term = lax.broadcasted_iota(jnp.int32, (PAIR, 1), 0)
        term = jnp.where(term >= E, term - E, term)

        def key_terms(seg):
            off = jnp.where(jnp.logical_and(term < SEGS, seg != term), -BIG, 0.0)
            return off.T.astype(BF)

        for r in range(batch):
            for d in range(chips):
                at = pl.multiple_of(lax.rem(chip + d, chips) * tpc, tpc)
                seg = segs[r : r + 1, pl.ds(at, tpc)]
                if d == 0:
                    kea[r] = key_terms(seg)
                    on = jnp.logical_or(term == SEGS, jnp.logical_and(term < SEGS, seg == term))
                    qe[r] = jnp.where(on, 1.0, 0.0).T.astype(BF)
                else:
                    keb[r, (d - 1) * tpc : d * tpc] = key_terms(seg)
            unseen = jnp.logical_and(term == SEGS, vis[r : r + 1, :] == 0)
            keb[r, rem:] = jnp.where(unseen, -BIG, 0.0).T.astype(BF)

        def project(r, d, cb, with_q):
            x = xbuf[r, d, cb]
            if with_q:
                q = (dot(x, wqkv[:, 0:half]) * 0.125).astype(BF)
                for p in range(pairs):
                    q_s[r, p, pl.ds(pl.multiple_of(cb * per, per), per), :] = q[:, p * PAIR : (p + 1) * PAIR]
            for ref_a, ref_b, at in ((ka, kb, 1), (va, vb, 2)):
                y = dot(x, wqkv[:, at * half : (at + 1) * half]).astype(BF)
                for p in range(pairs):
                    val = y[:, p * PAIR : (p + 1) * PAIR]
                    if with_q:
                        ref_a[r, p, pl.ds(pl.multiple_of(cb * per, per), per), :] = val
                    else:
                        ref_b[r, p, pl.ds(pl.multiple_of((d - 1) * tpc + cb * per, per), per), :] = val

        for copy in loads:
            copy.wait()
        for r in range(batch):
            for p in range(pairs):
                kb[r, p, rem:, :] = pks[:, p * PAIR : (p + 1) * PAIR]
                vb[r, p, rem:, :] = pvs[:, p * PAIR : (p + 1) * PAIR]

        @pl.loop(0, 2 * batch)
        def _(i):
            pl.when(i == batch)(x_pair.wait_recv)
            late = lax.div(i, batch)
            project(lax.rem(i, batch), 0, core + late - 2 * core * late, True)

        outs = [
            pltpu.make_async_copy(src, dst, out_sem.at[i])
            for i, (src, dst) in enumerate(((q_s, q_o), (ka, ka_o), (va, va_o), (kb, kb_o), (vb, vb_o)))
        ]
        for copy in outs[:3]:
            copy.start()

        bufs = (s0, s1, s2, s3)

        def score(r, p, h, k_s, kext, buf):
            keys = k_s.shape[2]
            mine = lanes() < E if h == 0 else lanes() >= E
            q = jnp.where(mine, q_s[r, p], qe[r])
            k = jnp.where(mine, k_s[r, p], kext[r])
            buf[:, 0:keys] = dot(q, k, NT)

        def unit(r, p, after, u, k_s, v_s, kext, pst, p_hbm, finish, wait_slot):
            keys = k_s.shape[2]
            copy = pltpu.make_async_copy(pst.at[u], p_hbm.at[r, p], p_sem.at[u])
            pl.when(wait_slot)(copy.wait)
            tops, sums = [], []
            for h in range(2):
                score(after[0], after[1], h, k_s, kext, bufs[2 * (1 - u) + h])
                s = bufs[2 * u + h][:, 0:keys]
                top = jnp.max(s, axis=1, keepdims=True)
                prob = jnp.exp(s - top).astype(BF)
                pst[u, h] = prob
                mine = lanes() < E if h == 0 else lanes() >= E
                v = jnp.where(mine, v_s[r, p], jnp.ones((1, PAIR), BF))
                sums.append(dot(prob, v))
                tops.append(top)
            copy.start()
            low = lanes() < E
            finish(
                r,
                p,
                jnp.where(low, sums[0], sums[1]),
                pltpu.roll(jnp.where(low, sums[1], sums[0]), E, 1),
                jnp.where(low, tops[0], tops[1]),
            )

        def finish_a(r, p, o, l, m):
            oa[r, p], la[r, p], ma[r, p] = o, l, m

        def finish_b(r, p, o, l, m):
            top = jnp.maximum(ma[r, p], m)
            w_a, w_b = jnp.exp(ma[r, p] - top), jnp.exp(m - top)
            inv = 1.0 / (w_a * la[r, p] + w_b * l)
            r_a, r_b = w_a * inv, w_b * inv
            mix_s[r, p] = (oa[r, p] * r_a + o * r_b).astype(BF)
            la[r, p], ma[r, p] = r_a, r_b

        def drain(pst, p_hbm):
            for u in range(2):
                pltpu.make_async_copy(pst.at[u], p_hbm.at[0, 0], p_sem.at[u]).wait()

        args_a = (ka, va, kea, pst_a, pa_o, finish_a)
        for h in range(2):
            score(0, 0, h, ka, kea, bufs[h])
        count = batch * pairs

        @pl.loop(0, count // 2)
        def _(i):
            for u in range(2):
                j = 2 * i + u
                after = jnp.minimum(j + 1, count - 1)
                unit(
                    lax.div(j, pairs), lax.rem(j, pairs), (lax.div(after, pairs), lax.rem(after, pairs)),
                    u, *args_a, i > 0,
                )

            @pl.when(i == 0)
            def _():
                hop(0, 1)

        drain(pst_a, pa_o)
        hop(0, 2)

        args_b = (kb, vb, keb, pst_b, pb_o, finish_b)

        @pl.loop(0, batch)
        def _(r):
            for d in range(1, chips):
                remote(
                    xbuf.at[r, 0, core], xbuf.at[r, d, core], y_send.at[r, d - 1], y_recv.at[r, d - 1], peers[d - 1]
                ).wait_recv()
            forward = remote(
                xbuf.at[r, 1:, core], xbuf.at[r, 1:, core], d_send.at[r], d_recv.at[r], partner
            )
            forward.start()

            @pl.loop(0, 2 * (chips - 1))
            def _(i):
                pl.when(i == chips - 1)(forward.wait_recv)
                late = lax.div(i, chips - 1)
                project(r, lax.rem(i, chips - 1) + 1, core + late - 2 * core * late, False)

            @pl.when(r == 0)
            def _():
                hop(0, 3)

            @pl.when(r == 1)
            def _():
                hop(1, 1, 0)

            for h in range(2):
                score(r, 0, h, kb, keb, bufs[h])

            @pl.loop(0, pairs // 2)
            def _(i):
                for u in range(2):
                    p = 2 * i + u
                    unit(r, p, (r, jnp.minimum(p + 1, pairs - 1)), u, *args_b, i > 0)
                @pl.when(jnp.logical_and(r == 1, i == 0))
                def _():
                    hop(0, 5)
                    hop(1, 1, 1)

                @pl.when(jnp.logical_and(r == 1, i == 1))
                def _():
                    hop(1, 2, 0)

            drain(pst_b, pb_o)
            for p in range(pairs):
                for copy in mix_out(r, p):
                    copy.start()
            for copy in row_out(r):
                copy.start()
            forward.wait_send()

            @pl.when(r == 0)
            def _():
                hop(0, 4)

        for copy in outs[3:]:
            copy.start()
        for s in range(6, cw[0] + 2):
            hop(0, s)
        x_pair.wait_send()
        for copy in outs:
            copy.wait()

    vm = pltpu.VMEM
    keys = max(tpc, keys_b)
    pl.run_scoped(
        attention,
        vm((width, 3 * half), BF),
        vm((P_SIZE, half), BF),
        vm((P_SIZE, half), BF),
        vm((batch, pairs, tpc, PAIR), BF),
        vm((batch, pairs, tpc, PAIR), BF),
        vm((batch, pairs, tpc, PAIR), BF),
        vm((batch, pairs, keys_b, PAIR), BF),
        vm((batch, pairs, keys_b, PAIR), BF),
        *([vm((tpc, keys), F32)] * 4),
        vm((batch, pairs, tpc, PAIR), F32),
        vm((2, 2, tpc, tpc), BF),
        vm((2, 2, tpc, keys_b), BF),
        vm((batch, tpc, PAIR), BF),
        vm((batch, tpc, PAIR), BF),
        vm((batch, keys_b, PAIR), BF),
        vm((per, batch, width), BF),
    )

    tile = min(512, hidden)
    tiles = hidden // tile
    total = 2 * chips * tiles
    chunk = 64

    def feed_forward(n1, n1l, sc1, inv1, acc, slope, pre0, pre1, gt, gtl, bst):
        for copy in far_loads:
            copy.wait()
        for r in range(batch):
            for p in range(pairs):
                for copy in mix_out(r, p):
                    copy.wait()

        @pl.loop(0, width // 256)
        def _(j):
            at = pl.ds(pl.multiple_of(j * 256, 256), 256)
            acc[:, at] = dot(mixtok[...], wo[:, at])

        hop(1, 2, 1)

        def by_rows(body):
            for r in range(batch):

                @pl.loop(0, per // chunk)
                def _(i, r=r):
                    inner = pl.ds(pl.multiple_of(i * chunk, chunk), chunk)
                    body(r, inner, pl.ds(pl.multiple_of(r * per + i * chunk, chunk), chunk))

        def norm_one(r, inner, at):
            z = acc[at] + xbuf[r, 0, core, inner].astype(F32)
            c = z - mean_of(z)
            inv = lax.rsqrt(mean_of(c * c) + norm_eps)
            s = c * inv
            n = s * g1[...] + b1[...]
            n1[at], n1l[at], sc1[at], inv1[at] = n, n.astype(BF), s, inv
            acc[at] = jnp.zeros_like(z)

        by_rows(norm_one)
        hop(1, 3, 0)
        take_extras()
        for copy in shards:
            copy.wait()

        def split(j):
            slot = lax.div(j, tiles)
            at = pl.ds(pl.multiple_of(lax.rem(j, tiles) * tile, tile), tile)
            return lax.div(slot, 2), lax.rem(slot, 2), at

        def up_tile(j, buf):
            d, c, at = split(j)
            buf[...] = dot(n1l[...], up[d, c, :, at])

        pres = (pre0, pre1)
        up_tile(0, pre0)

        @pl.loop(0, total // 2)
        def _(i):
            @pl.when(i == max(tiles - 1, 0))
            def _():
                gathered(0)
                hop(1, 3, 1)

            @pl.when(i == tiles)
            def _():
                hop(1, 4, 0)
                hop(1, 4, 1)
                gathered(1)

            for u in range(2):
                j = 2 * i + u
                up_tile(jnp.minimum(j + 1, total - 1), pres[1 - u])
                v = pres[u][...]
                cdf = 0.5 * (1.0 + lax.erf(v * root_half))
                a = (v * cdf).astype(BF)
                d, c, at = split(j)
                slope[j] = cdf + v * jnp.exp(-0.5 * v * v) * inv_root_tau
                acc[...] += dot(a, dn[d, c, at, :])

        def norm_two(r, inner, at):
            z = n1[at] + acc[at]
            c = z - mean_of(z)
            inv = lax.rsqrt(mean_of(c * c) + norm_eps)
            s = c * inv
            bst[inner, r, :] = (s * g2[...] + b2[...]).astype(BF)
            t = ogs[r, inner] * g2[...]
            g = inv * (t - mean_of(t) - s * mean_of(t * s))
            gt[at], gtl[at] = g, g.astype(BF)
            acc[at] = jnp.zeros_like(z)

        by_rows(norm_two)
        outs = [pltpu.make_async_copy(bst, block_o, out_sem.at[0])]
        outs[0].start()

        def down_back(j, buf):
            d, c, at = split(j)
            buf[...] = dot(gtl[...], dn[d, c, at, :], NT)

        down_back(0, pre0)

        @pl.loop(0, total // 2)
        def _(i):
            for u in range(2):
                j = 2 * i + u
                down_back(jnp.minimum(j + 1, total - 1), pres[1 - u])
                g = (pres[u][...] * slope[j]).astype(BF)
                d, c, at = split(j)
                acc[...] += dot(g, up[d, c, :, at], NT)

        def norm_back(r, inner, at):
            t = (gt[at] + acc[at]) * g1[...]
            s = sc1[at]
            g = inv1[at] * (t - mean_of(t) - s * mean_of(t * s))
            gt[at], gtl[at] = g, g.astype(BF)

        by_rows(norm_back)
        for r in range(batch):
            copy = pltpu.make_async_copy(gt.at[r * per : (r + 1) * per], gsum_o.at[r], out_sem.at[batch + r])
            copy.start()
            outs.append(copy)

        mine = pl.ds(mine_at, per)
        for side in range(2):
            base = (1 - core) * half if side == 0 else core * half
            g = dot(gtl[...], wo[pl.ds(pl.multiple_of(base, half), half), :], NT).astype(BF)
            for p in range(pairs):
                gst[side, p] = g[:, p * PAIR : (p + 1) * PAIR]
            for p in range(pairs):
                for r in range(batch):
                    src, dst = gst.at[side, p, r * per : (r + 1) * per], gatt_o.at[r, p, mine]
                    if side == 0:
                        copy = remote(src, dst, gm_send.at[r, p], gm_recv.at[r, p], partner)
                    else:
                        copy = pltpu.make_async_copy(src, dst, f_sem.at[r, p])
                    copy.start()
                    outs.append(copy)
        for r in range(batch):
            for copy in cross[r]:
                copy.wait_send()
            for copy in row_out(r):
                copy.wait()
        for m in range(2):
            sent(m)
        for copy in outs:
            copy.wait()

    pl.run_scoped(
        feed_forward,
        vm((tokens, width), F32),
        vm((tokens, width), BF),
        vm((tokens, width), F32),
        vm((tokens, 1), F32),
        vm((tokens, width), F32),
        vm((total, tokens, tile), F32),
        vm((tokens, tile), F32),
        vm((tokens, tile), F32),
        vm((tokens, width), F32),
        vm((tokens, width), BF),
        vm((per, batch, width), BF),
    )


def forward_call(rows, chips, x, segs, vis, wq, wk, wv, pkey, pval, w_out, w_up, w_dn, og, g1, b1, g2, b2):
    per, batch, width = x.shape
    tpc, half = 2 * per, width // 2
    keys_b = (chips - 1) * tpc + P_SIZE
    pairs = half // PAIR
    tokens = batch * per
    steps = rows // 2
    out = lambda dt, *s: jax.ShapeDtypeStruct(s, dt)
    shapes = (
        out(BF, batch, pairs, tpc, PAIR),
        out(BF, batch, pairs, tpc, PAIR),
        out(BF, batch, pairs, tpc, PAIR),
        out(BF, batch, pairs, keys_b, PAIR),
        out(BF, batch, pairs, keys_b, PAIR),
        out(BF, batch, pairs, 2, tpc, tpc),
        out(BF, batch, pairs, 2, tpc, keys_b),
        out(F32, batch, pairs, tpc, PAIR),
        out(F32, batch, pairs, tpc, PAIR),
        out(BF, batch, pairs, tpc, PAIR),
        out(BF, per, batch, width),
        out(F32, batch, per, width),
        out(BF, batch, pairs, tpc, PAIR),
    )
    dma = pltpu.SemaphoreType.DMA
    vm = pltpu.VMEM
    scratch = [
        vm((batch, chips, 2, per, width), BF),
        vm((chips, 2, *w_up.shape), BF),
        vm((chips, 2, *w_dn.shape), BF),
        vm((width, width), BF),
        vm((tokens, width), BF),
        vm((batch, pairs, tpc, PAIR), F32),
        vm((batch, pairs, tpc, PAIR), F32),
        vm((batch, pairs, tpc, PAIR), BF),
        vm((batch, per, width), F32),
        vm((2, pairs, tokens, PAIR), BF),
        dma((9 + batch,)), dma((5,)), dma((2,)), dma, dma,
        dma((batch, chips - 1)), dma((batch, chips - 1)),
        dma((batch,)), dma((batch,)),
        dma((batch, pairs)), dma((batch, 3)),
        dma((batch, pairs)), dma((batch, pairs)),
        dma((2, 2, chips - 1)), dma((2, 2, chips - 1)),
        dma((rows, chips - 1)), dma((rows, chips - 1)),
        dma((2,)), dma((2,)),
        dma((2, steps + 1, 2, 2)), dma((2, steps + 1, 2, 2)),
        dma((2, steps + 1, 2, 2)), dma((2, steps + 1, 2, 2)),
        dma((rows,)), dma((rows,)),
        dma((batch, pairs)), dma((batch, pairs)),
    ]
    return pl.pallas_call(
        functools.partial(forward_kernel, rows, chips),
        out_shape=shapes,
        in_specs=[ANY] + [VM] * 2 + [ANY] * 9 + [VM] * 4,
        out_specs=[ANY] * len(shapes),
        scratch_shapes=scratch,
        compiler_params=pltpu.CompilerParams(
            collective_id=0, has_side_effects=True, vmem_limit_bytes=VMEM_LIMIT
        ),
        name="forward_and_ffn",
    )(x, segs, vis, wq, wk, wv, pkey, pval, w_out, w_up, w_dn, og, g1, b1, g2, b2)


def backward_kernel(
    rows, chips,
    g_i, mix_i, ra_i, rb_i, q_i, ka_i, va_i, kb_i, vb_i, pa_i, pb_i, wq, wk, wv, gs_i,
    ig_o, pk_o, pv_o,
    g_s, mix_s, ra, rb, q_s, ka, va, kb, vb, w_s, gs, pin_a, pin_b, s0, s1, s2, s3, do0, do1,
    dq, dks, dvs, psum, half_b, send_b, got_b, y_out, y_in, half_a, send_a, got_a,
    pr_in, pr_y, p_full,
    load_sem, p_sem, o_sem, db_send, db_recv, y_send, y_recv, da_send, da_recv,
    p1_send, p1_recv, p2_send, p2_recv, p3_send, p3_recv, p4_send, p4_recv,
):
    batch, pairs, tpc = q_s.shape[0], q_s.shape[1], q_s.shape[2]
    per = tpc // 2
    rem = (chips - 1) * tpc
    width, half = w_s.shape[1], w_s.shape[2]
    row, wide, core, chip = place()
    partner = (row, wide + 1 - 2 * core)
    peers = [(row, 2 * lax.rem(chip - d + chips, chips) + core) for d in range(1, chips)]
    back = [(row, 2 * lax.rem(chip + d, chips) + core) for d in range(1, chips)]
    plane = [(lax.rem(row + t, rows), wide) for t in range(1, rows)]

    col = pl.multiple_of(core * half, half)
    pairs_of = (
        (g_i, g_s), (mix_i, mix_s), (rb_i, rb), (kb_i, kb), (vb_i, vb), (q_i, q_s),
        (wk.at[:, pl.ds(col, half)], w_s.at[1]), (wv.at[:, pl.ds(col, half)], w_s.at[2]),
        (ra_i, ra), (ka_i, ka), (va_i, va), (wq.at[:, pl.ds(col, half)], w_s.at[0]), (gs_i, gs),
    )
    loads = [pltpu.make_async_copy(src, dst, load_sem.at[i]) for i, (src, dst) in enumerate(pairs_of)]

    def fetch(pin, p_hbm, r, p, u):
        return pltpu.make_async_copy(p_hbm.at[r, p], pin.at[u], p_sem.at[u])

    for copy in loads[:6]:
        copy.start()
    for u in range(2):
        fetch(pin_b, pb_i, 0, u, u).start()
    for copy in loads[6:]:
        copy.start()
    greet([partner] + peers + plane)
    for copy in loads[:6]:
        copy.wait()

    bufs, dos = (s0, s1, s2, s3), (do0, do1)

    def first(r, p, u, v_s, scale):
        keys = v_s.shape[2]
        g = g_s[r, p].astype(F32) * scale[r, p]
        do = g.astype(BF)
        dos[u][...] = do
        t = g * mix_s[r, p].astype(F32)
        lane = lanes()
        for h in range(2):
            mine = lane < E if h == 0 else lane >= E
            delta = jnp.sum(jnp.where(mine, t, 0.0), axis=1, keepdims=True)
            hi = delta.astype(BF)
            left = delta - hi.astype(F32)
            mid = left.astype(BF)
            low = (left - mid.astype(F32)).astype(BF)
            at = E if h == 0 else 0
            ext = jnp.where(
                lane == at, -hi, jnp.where(lane == at + 1, -mid, jnp.where(lane == at + 2, -low, jnp.zeros((1, PAIR), BF)))
            )
            one = jnp.where(jnp.logical_and(lane >= at, lane < at + 3), 1.0, 0.0).astype(BF)
            bufs[2 * u + h][:, 0:keys] = dot(
                jnp.where(mine, do, ext), jnp.where(mine, v_s[r, p], one), NT
            )

    def second(r, p, u, k_s, pin, start_dq, prefix):
        keys = k_s.shape[2]
        q2, k2, do = q_s[r, p], k_s[r, p], dos[u][...]
        do_t, q_t = do.T, q2.T
        gq, gk, gv = [], [], []
        for h in range(2):
            prob = pin[u, h]
            ds = (prob.astype(F32) * bufs[2 * u + h][:, 0:keys]).astype(BF)
            at = slice(h * E, (h + 1) * E)
            gv.append(dot(do_t[at], prob))
            gk.append(dot(q_t[at], ds))
            gq.append(dot(ds, k2))
        low = lanes() < E
        grad = jnp.where(low, gq[0], gq[1])
        dq[r, p] = grad if start_dq else dq[r, p] + grad
        cols = pl.ds(pl.multiple_of(p * PAIR, PAIR), PAIR)
        for ref, parts, k in ((dks, gk, 0), (dvs, gv, 1)):
            val = jnp.concatenate(parts, axis=0).T
            if prefix:
                ref[0:rem, cols] = val[:rem].astype(BF)
                psum[k * P_SIZE : (k + 1) * P_SIZE, cols] += val[rem:]
            else:
                ref[0:tpc, cols] = val.astype(BF)

    def group(r, k_s, v_s, scale, pin, p_hbm, start_dq, prefix, between=None):
        first(r, 0, 0, v_s, scale)

        @pl.loop(0, pairs // 2)
        def _(i):
            for u in range(2):
                p = 2 * i + u
                fetch(pin, p_hbm, r, p, u).wait()
                first(r, jnp.minimum(p + 1, pairs - 1), 1 - u, v_s, scale)
                second(r, p, u, k_s, pin, start_dq, prefix)

                @pl.when(i < pairs // 2 - 1)
                def _():
                    fetch(pin, p_hbm, r, p + 2, u).start()
            if between is not None:
                between(r, i)

    def to_inputs(at):
        keys = dot(dks[at], w_s[1], NT)
        return keys + dot(dvs[at], w_s[2], NT)

    psum[...] = jnp.zeros_like(psum)
    far = range(1, chips)

    def b_copy(r, d):
        return remote(
            send_b.at[r, d - 1], got_b.at[r, d - 1], db_send.at[r, d - 1], db_recv.at[r, d - 1], partner
        )

    def y_copy(r, d):
        return remote(
            y_out.at[r, d - 1], y_in.at[r, d - 1], y_send.at[r, d - 1], y_recv.at[r, d - 1], back[d - 1]
        )

    def a_copy(r):
        return remote(send_a.at[r], got_a.at[r], da_send.at[r], da_recv.at[r], partner)

    def out_copy(r):
        return pltpu.make_async_copy(half_a.at[r], ig_o.at[:, r], o_sem.at[r])

    @pl.loop(0, batch)
    def _(r):
        group(r, kb, vb, rb, pin_b, pb_i, True, True)

        @pl.when(r + 1 < batch)
        def _():
            for u in range(2):
                fetch(pin_b, pb_i, r + 1, u, u).start()

        @pl.when(r + 1 == batch)
        def _():
            for u in range(2):
                fetch(pin_a, pa_i, 0, u, u).start()

        @pl.when(r == 0)
        def _():
            for copy in loads[6:]:
                copy.wait()

        for d in far:
            at = pl.ds(pl.multiple_of((d - 1) * tpc + (1 - core) * per, per), per)
            send_b[r, d - 1] = to_inputs(at).astype(BF)
            b_copy(r, d).start()
        for d in far:
            at = pl.ds(pl.multiple_of((d - 1) * tpc + core * per, per), per)
            half_b[d - 1] = to_inputs(at)
        for d in far:
            b_copy(r, d).wait_recv()
            y_out[r, d - 1] = (half_b[d - 1] + got_b[r, d - 1].astype(F32)).astype(BF)
            y_copy(r, d).start()

    size = 2 * P_SIZE // rows

    def part(at):
        return pl.ds(pl.multiple_of(at * size, size), size)

    p_one = [
        remote(psum.at[part(plane[t - 1][0])], pr_in.at[t - 1], p1_send.at[t - 1], p1_recv.at[t - 1], plane[t - 1])
        for t in range(1, rows)
    ]
    p_two = [remote(pr_y.at[0], pr_y.at[d], p2_send.at[d - 1], p2_recv.at[d - 1], peers[d - 1]) for d in far]
    p_three = [
        remote(p_full.at[part(row)], p_full.at[part(row)], p3_send.at[t - 1], p3_recv.at[t - 1], plane[t - 1])
        for t in range(1, rows)
    ]
    cols = pl.ds(col, half)
    p_four = [
        remote(
            p_full.at[k * P_SIZE : (k + 1) * P_SIZE], ref.at[:, cols], p4_send.at[k], p4_recv.at[k], partner
        )
        for k, ref in enumerate((pk_o, pv_o))
    ]
    p_five = [
        pltpu.make_async_copy(p_full.at[k * P_SIZE : (k + 1) * P_SIZE], ref.at[:, cols], o_sem.at[batch + k])
        for k, ref in enumerate((pk_o, pv_o))
    ]
    for copy in p_one:
        copy.start()

    def over_rows():
        for copy in p_one:
            copy.wait_recv()
        total = psum[part(row)]
        for t in range(1, rows):
            total = total + pr_in[t - 1]
        pr_y[0] = total
        for copy in p_two:
            copy.start()

    def over_chips():
        for copy in p_two:
            copy.wait_recv()
        whole = jnp.zeros((size, half), F32)
        for c in range(chips):
            whole = whole + pr_y[lax.rem(c - chip + chips, chips)]
        p_full[part(row)] = whole
        for copy in p_three:
            copy.start()

    def to_all():
        for copy in p_three:
            copy.wait_recv()
        for copy in p_four + p_five:
            copy.start()

    def finish(r):
        a_copy(r).wait_recv()
        val = half_a[r] + got_a[r].astype(F32)
        for d in far:
            y_copy(r, d).wait_recv()
            val = val + y_in[r, d - 1].astype(F32)
        half_a[r] = val
        out_copy(r).start()

    def between(r, i):
        @pl.when(jnp.logical_and(r == 0, i == 0))
        def _():
            over_rows()

        @pl.when(jnp.logical_and(r == 1, i == 0))
        def _():
            over_chips()

    @pl.loop(0, batch)
    def _(r):
        group(r, ka, va, ra, pin_a, pa_i, False, False, between)

        @pl.when(r + 1 < batch)
        def _():
            for u in range(2):
                fetch(pin_a, pa_i, r + 1, u, u).start()

        for side in range(2):
            block = pl.multiple_of(((1 - core) if side == 0 else core) * per, per)
            at = pl.ds(block, per)
            part_in = to_inputs(at)
            for p in range(pairs):
                dvs[at, p * PAIR : (p + 1) * PAIR] = (dq[r, p, at, :]).astype(BF)
            val = part_in + 0.125 * dot(dvs[at], w_s[0], NT)
            if side == 0:
                send_a[r] = val.astype(BF)
                a_copy(r).start()
            else:
                half_a[r] = gs[r] + val

        @pl.when(r == 1)
        def _():
            to_all()
            finish(0)

    for r in range(1, batch):
        finish(r)
    for r in range(batch):
        a_copy(r).wait_send()
        for d in far:
            b_copy(r, d).wait_send()
            y_copy(r, d).wait_send()
        out_copy(r).wait()
    for copy in p_one + p_two + p_three:
        copy.wait_send()
    for copy in p_four + p_five:
        copy.wait()


def backward_call(rows, chips, g, mix, ra, rb, q, ka, va, kb, vb, pa, pb, wq, wk, wv, gs):
    batch, pairs, tpc, _ = q.shape
    keys_a, keys_b = ka.shape[2], kb.shape[2]
    per, width = gs.shape[1], gs.shape[2]
    half = width // 2
    size = 2 * P_SIZE // rows
    out = lambda dt, *s: jax.ShapeDtypeStruct(s, dt)
    dma = pltpu.SemaphoreType.DMA
    vm = pltpu.VMEM
    far = chips - 1
    keys = max(keys_a, keys_b)
    return pl.pallas_call(
        functools.partial(backward_kernel, rows, chips),
        out_shape=(
            out(F32, per, batch, width),
            out(F32, P_SIZE, width),
            out(F32, P_SIZE, width),
        ),
        in_specs=[ANY] * 15,
        out_specs=[ANY] * 3,
        scratch_shapes=[
            vm((batch, pairs, tpc, PAIR), BF),
            vm((batch, pairs, tpc, PAIR), BF),
            vm((batch, pairs, tpc, PAIR), F32),
            vm((batch, pairs, tpc, PAIR), F32),
            vm((batch, pairs, tpc, PAIR), BF),
            vm((batch, pairs, keys_a, PAIR), BF),
            vm((batch, pairs, keys_a, PAIR), BF),
            vm((batch, pairs, keys_b, PAIR), BF),
            vm((batch, pairs, keys_b, PAIR), BF),
            vm((3, width, half), BF),
            vm((batch, per, width), F32),
            vm((2, 2, tpc, keys_a), BF),
            vm((2, 2, tpc, keys_b), BF),
            *([vm((tpc, keys), F32)] * 4),
            *([vm((tpc, PAIR), BF)] * 2),
            vm((batch, pairs, tpc, PAIR), F32),
            vm((keys, half), BF),
            vm((keys, half), BF),
            vm((2 * P_SIZE, half), F32),
            vm((far, per, width), F32),
            *([vm((batch, far, per, width), BF)] * 4),
            vm((batch, per, width), F32),
            vm((batch, per, width), BF),
            vm((batch, per, width), BF),
            vm((rows - 1, size, half), F32),
            vm((chips, size, half), F32),
            vm((2 * P_SIZE, half), F32),
            dma((13,)), dma((2,)), dma((batch + 2,)),
            dma((batch, far)), dma((batch, far)),
            dma((batch, far)), dma((batch, far)),
            dma((batch,)), dma((batch,)),
            dma((rows - 1,)), dma((rows - 1,)),
            dma((far,)), dma((far,)),
            dma((rows - 1,)), dma((rows - 1,)),
            dma((2,)), dma((2,)),
        ],
        compiler_params=pltpu.CompilerParams(
            collective_id=2, has_side_effects=True, vmem_limit_bytes=VMEM_LIMIT
        ),
        name="attention_backward",
    )(g, mix, ra, rb, q, ka, va, kb, vb, pa, pb, wq, wk, wv, gs)


def outputs_kernel(pieces, *refs):
    count = len(refs) // 3
    srcs, dsts, bufs, sem = refs[:count], refs[count : 2 * count], refs[2 * count : 3 * count], refs[-1]
    steps = []
    for k in range(count):
        size = srcs[k].shape[0] // pieces[k]
        for i in range(pieces[k]):
            at = slice(i * size, (i + 1) * size)
            steps.append(
                (
                    pltpu.make_async_copy(srcs[k].at[at], bufs[k].at[at], sem.at[0, k, i]),
                    pltpu.make_async_copy(bufs[k].at[at], dsts[k].at[at], sem.at[1, k, i]),
                )
            )
    for read, _ in steps:
        read.start()
    for read, write in steps:
        read.wait()
        write.start()
    for _, write in steps:
        write.wait()


def outputs_call(*arrays):
    pieces = [4 if v.ndim == 3 else 1 for v in arrays]
    return pl.pallas_call(
        functools.partial(outputs_kernel, pieces),
        out_shape=tuple(jax.ShapeDtypeStruct(v.shape, v.dtype) for v in arrays),
        in_specs=[ANY] * len(arrays),
        out_specs=[ANY] * len(arrays),
        scratch_shapes=[pltpu.VMEM(v.shape, v.dtype) for v in arrays]
        + [pltpu.SemaphoreType.DMA((2, len(arrays), 4))],
        name="outputs",
    )(*arrays)


def on_device(
    rows, chips,
    hidden_in, segments, prefix_vis, prefix_key, prefix_value, w_query, w_key, w_value, w_out,
    norm1_gain, norm1_bias, w_up, w_down, norm2_gain, norm2_bias, out_grad,
):
    flat = lambda v: v.reshape(1, -1)
    q, ka, va, kb, vb, pa, pb, ra, rb, mix, block, gs, g = forward_call(
        rows, chips, hidden_in, segments, prefix_vis, w_query, w_key, w_value, prefix_key, prefix_value,
        w_out, w_up, w_down, out_grad, flat(norm1_gain), flat(norm1_bias), flat(norm2_gain), flat(norm2_bias),
    )
    input_grad, pk_grad, pv_grad = backward_call(
        rows, chips, g, mix, ra, rb, q, ka, va, kb, vb, pa, pb, w_query, w_key, w_value, gs
    )
    return outputs_call(block, input_grad, pk_grad, pv_grad)


def solution(mesh):
    rows, chips = mesh.shape["rows"], mesh.shape["wide"] // 2
    act = P("wide", "rows", None)
    per_row = P("rows", None)
    in_specs = (
        act, per_row, per_row, *([P()] * 8), P(None, "wide"), P("wide", None), P(), P(), act,
    )
    out_specs = (act, act, P(), P())
    return jax.shard_map(
        functools.partial(on_device, rows, chips),
        mesh=mesh,
        in_specs=in_specs,
        out_specs=out_specs,
        check_vma=False,
    )
```

```python
import functools

import jax
import jax.numpy as jnp
from jax import lax
from jax.experimental import pallas as pl
from jax.experimental.pallas import tpu as pltpu
from jax.sharding import PartitionSpec as P

E = 64
P_SIZE = 64
SEGS = 4
PAIR = 2 * E
BIG = 1e30
norm_eps = 1e-05
root_half = 0.7071067811865476
inv_root_tau = 0.3989422804014327

BF = jnp.bfloat16
F32 = jnp.float32
MESH = pl.DeviceIdType.MESH
ANY = pl.BlockSpec(memory_space=pl.ANY)
VM = pl.BlockSpec(memory_space=pltpu.VMEM)
NN = (((1,), (0,)), ((), ()))
NT = (((1,), (1,)), ((), ()))
VMEM_LIMIT = 67043328


def dot(a, b, dims=NN):
    return lax.dot_general(a, b, dims, preferred_element_type=F32)


def lanes():
    return lax.broadcasted_iota(jnp.int32, (1, PAIR), 1)


def place():
    row, wide = lax.axis_index("rows"), lax.axis_index("wide")
    return row, wide, lax.rem(wide, 2), lax.div(wide, 2)


def remote(src, dst, send, recv, dev):
    return pltpu.make_async_remote_copy(
        src_ref=src, dst_ref=dst, send_sem=send, recv_sem=recv, device_id=dev, device_id_type=MESH
    )


def ring_pos(row, rows):
    half = rows // 2
    z, x = lax.div(row, 2), lax.rem(row, 2)
    return z + x * (2 * half - 1 - 2 * z)


def ring_row(pos, rows):
    pos = lax.rem(pos + 2 * rows, rows)
    upper = lax.div(pos, rows // 2)
    return 2 * pos + upper * (2 * rows - 1 - 4 * pos)


def mean_of(value):
    return jnp.mean(value, axis=-1, keepdims=True)


def layer_kernel(
    rows, chips,
    x_own, segs, vis, wq, wk, wv, pkey, pval, w_out, w_up, w_dn, og, g1, b1, g2, b2,
    pa_o, pb_o, block_o, ig_o, pk_o, pv_o,
    xbuf, up, dn, wo, mixtok, la, ma, mix_s, g_s, gs, wqkv, q_s, ka, va, kb, vb,
    got_b, y_in, got_a, psum, pr_in, pr_y, p_full, pin_b,
    load_sem, out_sem, p_sem, x_send, x_recv, y_send, y_recv, d_send, d_recv, f_sem, g_sem,
    mx_send, mx_recv, g_send, g_recv, e_send, e_recv, sh_send, sh_recv, r_send, r_recv, k_send, k_recv,
    l_send, l_recv, gm_send, gm_recv,
    db_send, db_recv, yb_send, yb_recv, da_send, da_recv,
    p1_send, p1_recv, p2_send, p2_recv, p3_send, p3_recv, p4_send, p4_recv,
):
    per, batch, width = x_own.shape
    tpc = 2 * per
    rem = (chips - 1) * tpc
    keys_b = rem + P_SIZE
    half = width // 2
    pairs = half // PAIR
    hidden = up.shape[3]
    tokens = batch * per
    row, wide, core, chip = place()
    partner = (row, wide + 1 - 2 * core)
    pos = ring_pos(row, rows)
    nxt = (ring_row(pos + 1, rows), wide)
    prv = (ring_row(pos - 1, rows), wide)
    peers = [(row, 2 * lax.rem(chip - d + chips, chips) + core) for d in range(1, chips)]
    mats = ((w_up, up), (w_dn, dn))
    cw = (rows // 2, 3)
    ccw = (rows // 2 - 1, 3)
    cuts = (1, 1)
    plane = [(lax.rem(row + t, rows), wide) for t in range(1, rows)]
    back = [(row, 2 * lax.rem(chip + d, chips) + core) for d in range(1, chips)]

    col = pl.multiple_of(core * half, half)
    far_loads = [
        pltpu.make_async_copy(w_up, up.at[0, core], load_sem.at[0]),
        pltpu.make_async_copy(w_dn, dn.at[0, core], load_sem.at[1]),
        pltpu.make_async_copy(w_out, wo, load_sem.at[2]),
    ]

    x_pair = remote(xbuf.at[:, 0, core], xbuf.at[:, 0, core], x_send, x_recv, partner)
    cross = [
        [
            remote(xbuf.at[r, 0, core], xbuf.at[r, d, core], y_send.at[r, d - 1], y_recv.at[r, d - 1], peers[d - 1])
            for d in range(1, chips)
        ]
        for r in range(batch)
    ]

    def piece(ref, row_at, cut=0, cuts_of=1):
        size = ref.shape[-2] // rows
        sub = size // cuts_of
        return pl.ds(pl.multiple_of(row_at * size + cut * sub, sub), sub)

    def w_cross(m, row_at, cut, cuts_of, send, recv):
        src, dst = mats[m]
        at = piece(src, row_at, cut, cuts_of)
        return [
            remote(src.at[at], dst.at[d, core, at], send.at[d - 1], recv.at[d - 1], peers[d - 1])
            for d in range(1, chips)
        ]

    split_cross = [
        [w_cross(m, row, h, cuts[m], g_send.at[m, h], g_recv.at[m, h]) for h in range(cuts[m])] for m in range(2)
    ]
    wcross = [sum(group, []) for group in split_cross]
    far_off = range(ccw[1] + 1, rows - cw[1])
    extras = sum([w_cross(1, ring_row(pos + o, rows), 0, 1, e_send.at[o], e_recv.at[o]) for o in far_off], [])
    shards = [
        remote(mats[m][0], mats[m][1].at[0, core], sh_send.at[m], sh_recv.at[m], partner) for m in range(2)
    ]

    def place_of(s, way):
        return ring_row(pos - s if way == 0 else pos + s, rows)

    def ring_copy(m, s, way, h):
        buf = mats[m][1]
        ref = buf.at[1:, core, piece(buf, place_of(s - 1, way), h, cuts[m])]
        return remote(ref, ref, r_send.at[m, s, way, h], r_recv.at[m, s, way, h], nxt if way == 0 else prv)

    def hand_over(m, s, way, h):
        buf = mats[m][1]
        ref = buf.at[1:, core, piece(buf, place_of(s, way), h, cuts[m])]
        return remote(ref, ref, k_send.at[m, s, way, h], k_recv.at[m, s, way, h], partner)

    def ways(m, s):
        return range(2 if s <= ccw[m] else 1)

    def hop(m, s, h=0):
        if s > cw[m] + 1 or h >= cuts[m]:
            return
        if s == 1:
            for copy in split_cross[m][h]:
                copy.wait_recv()
        else:
            for way in ways(m, s - 1):
                ring_copy(m, s - 1, way, h).wait_recv()
        if s <= cw[m]:
            for way in ways(m, s):
                ring_copy(m, s, way, h).start()
        for way in ways(m, s - 1) if s > 1 else range(1):
            hand_over(m, s - 1, way, h).start()

    def extra_over(o):
        buf = mats[1][1]
        ref = buf.at[1:, core, piece(buf, place_of(o, 1))]
        return remote(ref, ref, l_send.at[o], l_recv.at[o], partner)

    def take_extras():
        for copy in extras:
            copy.wait_recv()
        for o in far_off:
            extra_over(o).start()

    def all_over(m):
        copies = [hand_over(m, 0, 0, h) for h in range(cuts[m])]
        for s in range(1, cw[m] + 1):
            copies += [hand_over(m, s, way, h) for way in ways(m, s) for h in range(cuts[m])]
        if m == 1:
            copies += [extra_over(o) for o in far_off]
        return copies

    def gathered(m):
        for copy in all_over(m):
            copy.wait_recv()

    def sent(m):
        for copy in wcross[m] + all_over(m) + (extras if m == 1 else []):
            copy.wait_send()
        for s in range(1, cw[m] + 1):
            for way in ways(m, s):
                for h in range(cuts[m]):
                    ring_copy(m, s, way, h).wait_send()

    mine_at, other_at = pl.multiple_of(core * per, per), pl.multiple_of((1 - core) * per, per)

    def mix_out(r, p):
        cols = pl.ds(pl.multiple_of(core * half + p * PAIR, PAIR), PAIR)
        dst = mixtok.at[pl.ds(pl.multiple_of(r * per, per), per), cols]
        return (
            remote(mix_s.at[r, p, pl.ds(other_at, per)], dst, mx_send.at[r, p], mx_recv.at[r, p], partner),
            pltpu.make_async_copy(mix_s.at[r, p, pl.ds(mine_at, per)], dst, f_sem.at[r, p]),
        )

    def attention(pks, pvs, s0, s1, s2, s3, oa, pst_a, pst_b, qe, kea, keb, xraw):
        x_load = pltpu.make_async_copy(x_own, xraw, load_sem.at[3 + batch])
        loads = [
            pltpu.make_async_copy(wq.at[:, pl.ds(col, half)], wqkv.at[:, 0:half], load_sem.at[4 + batch]),
            pltpu.make_async_copy(wk.at[:, pl.ds(col, half)], wqkv.at[:, half : 2 * half], load_sem.at[5 + batch]),
            pltpu.make_async_copy(wv.at[:, pl.ds(col, half)], wqkv.at[:, 2 * half : 3 * half], load_sem.at[6 + batch]),
            pltpu.make_async_copy(pkey.at[:, pl.ds(col, half)], pks, load_sem.at[7 + batch]),
            pltpu.make_async_copy(pval.at[:, pl.ds(col, half)], pvs, load_sem.at[8 + batch]),
        ]
        barrier = pltpu.get_barrier_semaphore()
        friends = [partner] + plane + peers
        for dev in friends:
            pl.semaphore_signal(barrier, inc=1, device_id=dev, device_id_type=MESH)
        x_load.start()
        for copy in loads:
            copy.start()
        x_load.wait()
        for r in range(batch):
            xbuf[r, 0, core] = xraw[:, r, :]
        pl.semaphore_wait(barrier, len(friends))
        x_pair.start()
        for group in wcross + cross + [extras]:
            for copy in group:
                copy.start()
        for copy in shards + far_loads:
            copy.start()

        term = lax.broadcasted_iota(jnp.int32, (PAIR, 1), 0)
        term = jnp.where(term >= E, term - E, term)

        def key_terms(seg):
            off = jnp.where(jnp.logical_and(term < SEGS, seg != term), -BIG, 0.0)
            return off.T.astype(BF)

        for r in range(batch):
            for d in range(chips):
                at = pl.multiple_of(lax.rem(chip + d, chips) * tpc, tpc)
                seg = segs[r : r + 1, pl.ds(at, tpc)]
                if d == 0:
                    kea[r] = key_terms(seg)
                    on = jnp.logical_or(term == SEGS, jnp.logical_and(term < SEGS, seg == term))
                    qe[r] = jnp.where(on, 1.0, 0.0).T.astype(BF)
                else:
                    keb[r, (d - 1) * tpc : d * tpc] = key_terms(seg)
            unseen = jnp.logical_and(term == SEGS, vis[r : r + 1, :] == 0)
            keb[r, rem:] = jnp.where(unseen, -BIG, 0.0).T.astype(BF)

        def project(r, d, cb, with_q):
            x = xbuf[r, d, cb]
            if with_q:
                q = (dot(x, wqkv[:, 0:half]) * 0.125).astype(BF)
                for p in range(pairs):
                    q_s[r, p, pl.ds(pl.multiple_of(cb * per, per), per), :] = q[:, p * PAIR : (p + 1) * PAIR]
            for ref_a, ref_b, at in ((ka, kb, 1), (va, vb, 2)):
                y = dot(x, wqkv[:, at * half : (at + 1) * half]).astype(BF)
                for p in range(pairs):
                    val = y[:, p * PAIR : (p + 1) * PAIR]
                    if with_q:
                        ref_a[r, p, pl.ds(pl.multiple_of(cb * per, per), per), :] = val
                    else:
                        ref_b[r, p, pl.ds(pl.multiple_of((d - 1) * tpc + cb * per, per), per), :] = val

        for copy in loads:
            copy.wait()
        for r in range(batch):
            for p in range(pairs):
                kb[r, p, rem:, :] = pks[:, p * PAIR : (p + 1) * PAIR]
                vb[r, p, rem:, :] = pvs[:, p * PAIR : (p + 1) * PAIR]

        @pl.loop(0, 2 * batch)
        def _(i):
            pl.when(i == batch)(x_pair.wait_recv)
            late = lax.div(i, batch)
            project(lax.rem(i, batch), 0, core + late - 2 * core * late, True)

        hop(0, 1)
        bufs = (s0, s1, s2, s3)

        def score(r, p, h, k_s, kext, buf):
            keys = k_s.shape[2]
            mine = lanes() < E if h == 0 else lanes() >= E
            q = jnp.where(mine, q_s[r, p], qe[r])
            k = jnp.where(mine, k_s[r, p], kext[r])
            buf[:, 0:keys] = dot(q, k, NT)

        def unit(r, p, after, u, k_s, v_s, kext, pst, p_hbm, finish, wait_slot):
            keys = k_s.shape[2]
            copy = pltpu.make_async_copy(pst.at[u], p_hbm.at[r, p], p_sem.at[u])
            pl.when(wait_slot)(copy.wait)
            tops, sums = [], []
            for h in range(2):
                score(after[0], after[1], h, k_s, kext, bufs[2 * (1 - u) + h])
                s = bufs[2 * u + h][:, 0:keys]
                top = jnp.max(s, axis=1, keepdims=True)
                prob = jnp.exp(s - top).astype(BF)
                pst[u, h] = prob
                mine = lanes() < E if h == 0 else lanes() >= E
                v = jnp.where(mine, v_s[r, p], jnp.ones((1, PAIR), BF))
                sums.append(dot(prob, v))
                tops.append(top)
            copy.start()
            low = lanes() < E
            finish(
                r,
                p,
                jnp.where(low, sums[0], sums[1]),
                pltpu.roll(jnp.where(low, sums[1], sums[0]), E, 1),
                jnp.where(low, tops[0], tops[1]),
            )

        def finish_a(r, p, o, l, m):
            oa[r, p], la[r, p], ma[r, p] = o, l, m

        def finish_b(r, p, o, l, m):
            top = jnp.maximum(ma[r, p], m)
            w_a, w_b = jnp.exp(ma[r, p] - top), jnp.exp(m - top)
            inv = 1.0 / (w_a * la[r, p] + w_b * l)
            r_a, r_b = w_a * inv, w_b * inv
            mix_s[r, p] = (oa[r, p] * r_a + o * r_b).astype(BF)
            la[r, p], ma[r, p] = r_a, r_b

        def drain(pst, p_hbm):
            for u in range(2):
                pltpu.make_async_copy(pst.at[u], p_hbm.at[0, 0], p_sem.at[u]).wait()

        args_a = (ka, va, kea, pst_a, pa_o, finish_a)
        for h in range(2):
            score(0, 0, h, ka, kea, bufs[h])
        count = batch * pairs

        @pl.loop(0, count // 2)
        def _(i):
            for u in range(2):
                j = 2 * i + u
                after = jnp.minimum(j + 1, count - 1)
                unit(
                    lax.div(j, pairs), lax.rem(j, pairs), (lax.div(after, pairs), lax.rem(after, pairs)),
                    u, *args_a, i > 0,
                )

            @pl.when(i == 2)
            def _():
                hop(1, 1)

        drain(pst_a, pa_o)
        hop(0, 2)
        hop(1, 2)

        args_b = (kb, vb, keb, pst_b, pb_o, finish_b)

        @pl.loop(0, batch)
        def _(r):
            for d in range(1, chips):
                remote(
                    xbuf.at[r, 0, core], xbuf.at[r, d, core], y_send.at[r, d - 1], y_recv.at[r, d - 1], peers[d - 1]
                ).wait_recv()
            forward = remote(
                xbuf.at[r, 1:, core], xbuf.at[r, 1:, core], d_send.at[r], d_recv.at[r], partner
            )
            forward.start()

            @pl.loop(0, 2 * (chips - 1))
            def _(i):
                pl.when(i == chips - 1)(forward.wait_recv)
                late = lax.div(i, chips - 1)
                project(r, lax.rem(i, chips - 1) + 1, core + late - 2 * core * late, False)

            @pl.when(r == 0)
            def _():
                hop(0, 3)

            @pl.when(r == 1)
            def _():
                hop(0, 4)

            for h in range(2):
                score(r, 0, h, kb, keb, bufs[h])

            @pl.loop(0, pairs // 2)
            def _(i):
                for u in range(2):
                    p = 2 * i + u
                    unit(r, p, (r, jnp.minimum(p + 1, pairs - 1)), u, *args_b, i > 0)

            drain(pst_b, pb_o)
            for p in range(pairs):
                for copy in mix_out(r, p):
                    copy.start()
            forward.wait_send()

            @pl.when(r == 0)
            def _():
                hop(1, 3)

        for s in range(5, cw[0] + 1):
            hop(0, s)
        hop(1, 4)
        take_extras()
        x_pair.wait_send()

    vm = pltpu.VMEM
    keys = max(tpc, keys_b)
    pl.run_scoped(
        attention,
        vm((P_SIZE, half), BF),
        vm((P_SIZE, half), BF),
        *([vm((tpc, keys), F32)] * 4),
        vm((batch, pairs, tpc, PAIR), F32),
        vm((2, 2, tpc, tpc), BF),
        vm((2, 2, tpc, keys_b), BF),
        vm((batch, tpc, PAIR), BF),
        vm((batch, tpc, PAIR), BF),
        vm((batch, keys_b, PAIR), BF),
        vm((per, batch, width), BF),
    )

    tile = min(512, hidden)
    tiles = hidden // tile
    total = 2 * chips * tiles
    chunk = 64

    def fetch(pin, p_hbm, r, p, u):
        return pltpu.make_async_copy(p_hbm.at[r, p], pin.at[u], p_sem.at[u])

    def feed_forward(ogs, gst, sc1, inv1, acc, slope, pre0, pre1, bst):
        nl = mixtok
        og_loads = [pltpu.make_async_copy(og.at[:, r], ogs.at[r], load_sem.at[3 + r]) for r in range(batch)]
        for copy in og_loads:
            copy.start()
        for u in range(2):
            fetch(pin_b, pb_o, 0, u, u).start()
        for copy in far_loads:
            copy.wait()
        for r in range(batch):
            for p in range(pairs):
                for copy in mix_out(r, p):
                    copy.wait()

        @pl.loop(0, width // 256)
        def _(j):
            at = pl.ds(pl.multiple_of(j * 256, 256), 256)
            acc[:, at] = dot(mixtok[...], wo[:, at])

        def by_rows(body):
            for r in range(batch):

                @pl.loop(0, per // chunk, unroll=min(2, per // chunk))
                def _(i, r=r):
                    inner = pl.ds(pl.multiple_of(i * chunk, chunk), chunk)
                    body(r, inner, pl.ds(pl.multiple_of(r * per + i * chunk, chunk), chunk))

        def norm_one(r, inner, at):
            z = acc[at] + xbuf[r, 0, core, inner].astype(F32)
            c = z - mean_of(z)
            inv = lax.rsqrt(mean_of(c * c) + norm_eps)
            s = c * inv
            n = s * g1[...] + b1[...]
            nl[at], sc1[at], inv1[at] = n.astype(BF), s, inv
            acc[at] = jnp.zeros_like(z)

        by_rows(norm_one)
        for copy in shards + og_loads:
            copy.wait()

        def split(j):
            slot = lax.div(j, tiles)
            at = pl.ds(pl.multiple_of(lax.rem(j, tiles) * tile, tile), tile)
            return lax.div(slot, 2), lax.rem(slot, 2), at

        def up_tile(j, buf):
            d, c, at = split(j)
            buf[...] = dot(nl[...], up[d, c, :, at])

        pres = (pre0, pre1)
        up_tile(0, pre0)

        @pl.loop(0, total // 2)
        def _(i):
            @pl.when(i == max(tiles - 1, 0))
            def _():
                hop(0, cw[0] + 1)
                gathered(0)

            @pl.when(i == tiles)
            def _():
                gathered(1)

            for u in range(2):
                j = 2 * i + u
                up_tile(jnp.minimum(j + 1, total - 1), pres[1 - u])
                v = pres[u][...]
                cdf = 0.5 * (1.0 + lax.erf(v * root_half))
                a = (v * cdf).astype(BF)
                d, c, at = split(j)
                slope[j] = (cdf + v * jnp.exp(-0.5 * v * v) * inv_root_tau).astype(BF)
                acc[...] += dot(a, dn[d, c, at, :])

        def norm_two(r, inner, at):
            z = sc1[at] * g1[...] + b1[...] + acc[at]
            c = z - mean_of(z)
            inv = lax.rsqrt(mean_of(c * c) + norm_eps)
            s = c * inv
            bst[inner, r, :] = (s * g2[...] + b2[...]).astype(BF)
            t = ogs[r, inner] * g2[...]
            g = inv * (t - mean_of(t) - s * mean_of(t * s))
            gs[at], nl[at] = g, g.astype(BF)
            acc[at] = jnp.zeros_like(z)

        by_rows(norm_two)
        outs = [pltpu.make_async_copy(bst, block_o, out_sem.at[0])]
        outs[0].start()

        def down_back(j, buf):
            d, c, at = split(j)
            buf[...] = dot(nl[...], dn[d, c, at, :], NT)

        down_back(0, pre0)

        @pl.loop(0, total // 2)
        def _(i):
            for u in range(2):
                j = 2 * i + u
                down_back(jnp.minimum(j + 1, total - 1), pres[1 - u])
                g = (pres[u][...] * slope[j].astype(F32)).astype(BF)
                d, c, at = split(j)
                acc[...] += dot(g, up[d, c, :, at], NT)

        def norm_back(r, inner, at):
            t = (gs[at] + acc[at]) * g1[...]
            s = sc1[at]
            g = inv1[at] * (t - mean_of(t) - s * mean_of(t * s))
            gs[at], nl[at] = g, g.astype(BF)

        by_rows(norm_back)
        mine = pl.ds(mine_at, per)
        for side in range(2):
            base = (1 - core) * half if side == 0 else core * half
            g = dot(nl[...], wo[pl.ds(pl.multiple_of(base, half), half), :], NT).astype(BF)
            for p in range(pairs):
                for r in range(batch):
                    val = g[r * per : (r + 1) * per, p * PAIR : (p + 1) * PAIR]
                    if side == 0:
                        gst[r, p] = val
                    else:
                        g_s[r, p, mine, :] = val
            if side == 0:
                sends = [
                    remote(gst.at[r, p], g_s.at[r, p, mine], gm_send.at[r, p], gm_recv.at[r, p], partner)
                    for r in range(batch)
                    for p in range(pairs)
                ]
                for copy in sends:
                    copy.start()
        for copy in sends + outs:
            copy.wait()

    pl.run_scoped(
        feed_forward,
        vm((batch, per, width), F32),
        vm((batch, pairs, per, PAIR), BF),
        vm((tokens, width), F32),
        vm((tokens, 1), F32),
        vm((tokens, width), F32),
        vm((total, tokens, tile), BF),
        vm((tokens, tile), F32),
        vm((tokens, tile), F32),
        vm((per, batch, width), BF),
    )

    def attention_back(pin_a, s0, s1, s2, s3, do0, do1, dq, dks, dvs, half_b, send_b, y_out, send_a):
        bufs, dos = (s0, s1, s2, s3), (do0, do1)

        def first(r, p, u, v_s, scale):
            keys = v_s.shape[2]
            g = g_s[r, p].astype(F32) * scale[r, p]
            do = g.astype(BF)
            dos[u][...] = do
            t = g * mix_s[r, p].astype(F32)
            lane = lanes()
            for h in range(2):
                mine = lane < E if h == 0 else lane >= E
                delta = jnp.sum(jnp.where(mine, t, 0.0), axis=1, keepdims=True)
                hi = delta.astype(BF)
                left = delta - hi.astype(F32)
                mid = left.astype(BF)
                low = (left - mid.astype(F32)).astype(BF)
                at = E if h == 0 else 0
                ext = jnp.where(
                    lane == at, -hi, jnp.where(lane == at + 1, -mid, jnp.where(lane == at + 2, -low, jnp.zeros((1, PAIR), BF)))
                )
                one = jnp.where(jnp.logical_and(lane >= at, lane < at + 3), 1.0, 0.0).astype(BF)
                bufs[2 * u + h][:, 0:keys] = dot(
                    jnp.where(mine, do, ext), jnp.where(mine, v_s[r, p], one), NT
                )

        def second(r, p, u, k_s, pin, start_dq, prefix):
            keys = k_s.shape[2]
            q2, k2, do = q_s[r, p], k_s[r, p], dos[u][...]
            do_t, q_t = do.T, q2.T
            gq, gk, gv = [], [], []
            for h in range(2):
                prob = pin[u, h]
                ds = (prob.astype(F32) * bufs[2 * u + h][:, 0:keys]).astype(BF)
                at = slice(h * E, (h + 1) * E)
                gv.append(dot(do_t[at], prob))
                gk.append(dot(q_t[at], ds))
                gq.append(dot(ds, k2))
            low = lanes() < E
            grad = jnp.where(low, gq[0], gq[1])
            dq[r, p] = grad if start_dq else dq[r, p] + grad
            cols = pl.ds(pl.multiple_of(p * PAIR, PAIR), PAIR)
            for ref, parts, k in ((dks, gk, 0), (dvs, gv, 1)):
                val = jnp.concatenate(parts, axis=0).T
                if prefix:
                    ref[0:rem, cols] = val[:rem].astype(BF)
                    psum[k * P_SIZE : (k + 1) * P_SIZE, cols] += val[rem:]
                else:
                    ref[0:tpc, cols] = val.astype(BF)

        def group(r, k_s, v_s, scale, pin, p_hbm, start_dq, prefix, between=None):
            first(r, 0, 0, v_s, scale)

            @pl.loop(0, pairs // 2)
            def _(i):
                for u in range(2):
                    p = 2 * i + u
                    fetch(pin, p_hbm, r, p, u).wait()
                    first(r, jnp.minimum(p + 1, pairs - 1), 1 - u, v_s, scale)
                    second(r, p, u, k_s, pin, start_dq, prefix)

                    @pl.when(i < pairs // 2 - 1)
                    def _():
                        fetch(pin, p_hbm, r, p + 2, u).start()
                if between is not None:
                    between(r, i)

        def to_inputs(at):
            keys = dot(dks[at], wqkv[:, half : 2 * half], NT)
            return keys + dot(dvs[at], wqkv[:, 2 * half : 3 * half], NT)

        psum[...] = jnp.zeros_like(psum)
        far = range(1, chips)

        def b_copy(r, d):
            return remote(
                send_b.at[r, d - 1], got_b.at[r, d - 1], db_send.at[r, d - 1], db_recv.at[r, d - 1], partner
            )

        def y_copy(r, d):
            return remote(
                y_out.at[r, d - 1], y_in.at[r, d - 1], yb_send.at[r, d - 1], yb_recv.at[r, d - 1], back[d - 1]
            )

        def a_copy(r):
            return remote(send_a.at[r], got_a.at[r], da_send.at[r], da_recv.at[r], partner)

        def token_rows(r):
            return pl.ds(pl.multiple_of(r * per, per), per)

        def out_copy(r):
            return pltpu.make_async_copy(gs.at[token_rows(r)], ig_o.at[:, r], out_sem.at[r])

        @pl.loop(0, batch)
        def _(r):
            group(r, kb, vb, ma, pin_b, pb_o, True, True)

            @pl.when(r + 1 < batch)
            def _():
                for u in range(2):
                    fetch(pin_b, pb_o, r + 1, u, u).start()

            @pl.when(r + 1 == batch)
            def _():
                for u in range(2):
                    fetch(pin_a, pa_o, 0, u, u).start()

            for d in far:
                at = pl.ds(pl.multiple_of((d - 1) * tpc + (1 - core) * per, per), per)
                send_b[r, d - 1] = to_inputs(at).astype(BF)
                b_copy(r, d).start()
            for d in far:
                at = pl.ds(pl.multiple_of((d - 1) * tpc + core * per, per), per)
                half_b[d - 1] = to_inputs(at)
            for d in far:
                b_copy(r, d).wait_recv()
                y_out[r, d - 1] = (half_b[d - 1] + got_b[r, d - 1].astype(F32)).astype(BF)
                y_copy(r, d).start()

        size = 2 * P_SIZE // rows

        def part(at):
            return pl.ds(pl.multiple_of(at * size, size), size)

        p_one = [
            remote(psum.at[part(plane[t - 1][0])], pr_in.at[t - 1], p1_send.at[t - 1], p1_recv.at[t - 1], plane[t - 1])
            for t in range(1, rows)
        ]
        p_two = [remote(pr_y.at[0], pr_y.at[d], p2_send.at[d - 1], p2_recv.at[d - 1], peers[d - 1]) for d in far]
        p_three = [
            remote(p_full.at[part(row)], p_full.at[part(row)], p3_send.at[t - 1], p3_recv.at[t - 1], plane[t - 1])
            for t in range(1, rows)
        ]
        cols = pl.ds(col, half)
        p_four = [
            remote(
                p_full.at[k * P_SIZE : (k + 1) * P_SIZE], ref.at[:, cols], p4_send.at[k], p4_recv.at[k], partner
            )
            for k, ref in enumerate((pk_o, pv_o))
        ]
        p_five = [
            pltpu.make_async_copy(p_full.at[k * P_SIZE : (k + 1) * P_SIZE], ref.at[:, cols], out_sem.at[batch + k])
            for k, ref in enumerate((pk_o, pv_o))
        ]
        for copy in p_one:
            copy.start()

        def over_rows():
            for copy in p_one:
                copy.wait_recv()
            total = psum[part(row)]
            for t in range(1, rows):
                total = total + pr_in[t - 1]
            pr_y[0] = total
            for copy in p_two:
                copy.start()

        def over_chips():
            for copy in p_two:
                copy.wait_recv()
            whole = jnp.zeros((size, half), F32)
            for c in range(chips):
                whole = whole + pr_y[lax.rem(c - chip + chips, chips)]
            p_full[part(row)] = whole
            for copy in p_three:
                copy.start()

        def to_all():
            for copy in p_three:
                copy.wait_recv()
            for copy in p_four + p_five:
                copy.start()

        def finish(r):
            a_copy(r).wait_recv()
            val = gs[token_rows(r)] + got_a[r].astype(F32)
            for d in far:
                y_copy(r, d).wait_recv()
                val = val + y_in[r, d - 1].astype(F32)
            gs[token_rows(r)] = val
            out_copy(r).start()

        def between(r, i):
            @pl.when(jnp.logical_and(r == 0, i == 0))
            def _():
                over_rows()

            @pl.when(jnp.logical_and(r == 1, i == 0))
            def _():
                over_chips()

        @pl.loop(0, batch)
        def _(r):
            group(r, ka, va, la, pin_a, pa_o, False, False, between)

            @pl.when(r + 1 < batch)
            def _():
                for u in range(2):
                    fetch(pin_a, pa_o, r + 1, u, u).start()

            for side in range(2):
                block = pl.multiple_of(((1 - core) if side == 0 else core) * per, per)
                at = pl.ds(block, per)
                part_in = to_inputs(at)
                for p in range(pairs):
                    dvs[at, p * PAIR : (p + 1) * PAIR] = (dq[r, p, at, :]).astype(BF)
                val = part_in + 0.125 * dot(dvs[at], wqkv[:, 0:half], NT)
                if side == 0:
                    send_a[r] = val.astype(BF)
                    a_copy(r).start()
                else:
                    gs[token_rows(r)] += val

            @pl.when(r == 1)
            def _():
                to_all()
                finish(0)

        for r in range(1, batch):
            finish(r)
        for r in range(batch):
            a_copy(r).wait_send()
            for d in far:
                b_copy(r, d).wait_send()
                y_copy(r, d).wait_send()
            out_copy(r).wait()
        for copy in p_one + p_two + p_three:
            copy.wait_send()
        for copy in p_four + p_five:
            copy.wait()

    pl.run_scoped(
        attention_back,
        vm((2, 2, tpc, tpc), BF),
        *([vm((tpc, keys), F32)] * 4),
        *([vm((tpc, PAIR), BF)] * 2),
        vm((batch, pairs, tpc, PAIR), F32),
        vm((keys, half), BF),
        vm((keys, half), BF),
        vm((chips - 1, per, width), F32),
        *([vm((batch, chips - 1, per, width), BF)] * 2),
        vm((batch, per, width), BF),
    )
    for r in range(batch):
        for copy in cross[r]:
            copy.wait_send()
    for m in range(2):
        sent(m)


def layer_call(rows, chips, x, segs, vis, wq, wk, wv, pkey, pval, w_out, w_up, w_dn, og, g1, b1, g2, b2):
    per, batch, width = x.shape
    tpc, half = 2 * per, width // 2
    far = chips - 1
    keys_b = far * tpc + P_SIZE
    pairs = half // PAIR
    tokens = batch * per
    steps = rows // 2
    size = 2 * P_SIZE // rows
    out = lambda dt, *s: jax.ShapeDtypeStruct(s, dt)
    shapes = (
        out(BF, batch, pairs, 2, tpc, tpc),
        out(BF, batch, pairs, 2, tpc, keys_b),
        out(BF, per, batch, width),
        out(F32, per, batch, width),
        out(F32, P_SIZE, width),
        out(F32, P_SIZE, width),
    )
    dma = pltpu.SemaphoreType.DMA
    vm = pltpu.VMEM
    scratch = [
        vm((batch, chips, 2, per, width), BF),
        vm((chips, 2, *w_up.shape), BF),
        vm((chips, 2, *w_dn.shape), BF),
        vm((width, width), BF),
        vm((tokens, width), BF),
        vm((batch, pairs, tpc, PAIR), F32),
        vm((batch, pairs, tpc, PAIR), F32),
        vm((batch, pairs, tpc, PAIR), BF),
        vm((batch, pairs, tpc, PAIR), BF),
        vm((tokens, width), F32),
        vm((width, 3 * half), BF),
        vm((batch, pairs, tpc, PAIR), BF),
        vm((batch, pairs, tpc, PAIR), BF),
        vm((batch, pairs, tpc, PAIR), BF),
        vm((batch, pairs, keys_b, PAIR), BF),
        vm((batch, pairs, keys_b, PAIR), BF),
        vm((batch, far, per, width), BF),
        vm((batch, far, per, width), BF),
        vm((batch, per, width), BF),
        vm((2 * P_SIZE, half), F32),
        vm((rows - 1, size, half), F32),
        vm((chips, size, half), F32),
        vm((2 * P_SIZE, half), F32),
        vm((2, 2, tpc, keys_b), BF),
        dma((9 + batch,)), dma((5,)), dma((2,)), dma, dma,
        dma((batch, far)), dma((batch, far)),
        dma((batch,)), dma((batch,)),
        dma((batch, pairs)), dma((batch, pairs)),
        dma((batch, pairs)), dma((batch, pairs)),
        dma((2, 2, far)), dma((2, 2, far)),
        dma((rows, far)), dma((rows, far)),
        dma((2,)), dma((2,)),
        dma((2, steps + 1, 2, 2)), dma((2, steps + 1, 2, 2)),
        dma((2, steps + 1, 2, 2)), dma((2, steps + 1, 2, 2)),
        dma((rows,)), dma((rows,)),
        dma((batch, pairs)), dma((batch, pairs)),
        dma((batch, far)), dma((batch, far)),
        dma((batch, far)), dma((batch, far)),
        dma((batch,)), dma((batch,)),
        dma((rows - 1,)), dma((rows - 1,)),
        dma((far,)), dma((far,)),
        dma((rows - 1,)), dma((rows - 1,)),
        dma((2,)), dma((2,)),
    ]
    return pl.pallas_call(
        functools.partial(layer_kernel, rows, chips),
        out_shape=shapes,
        in_specs=[ANY] + [VM] * 2 + [ANY] * 9 + [VM] * 4,
        out_specs=[ANY] * len(shapes),
        scratch_shapes=scratch,
        compiler_params=pltpu.CompilerParams(
            collective_id=0, has_side_effects=True, vmem_limit_bytes=VMEM_LIMIT
        ),
        name="layer",
    )(x, segs, vis, wq, wk, wv, pkey, pval, w_out, w_up, w_dn, og, g1, b1, g2, b2)


def outputs_kernel(pieces, *refs):
    count = len(refs) // 3
    srcs, dsts, bufs, sem = refs[:count], refs[count : 2 * count], refs[2 * count : 3 * count], refs[-1]
    steps = []
    for k in range(count):
        size = srcs[k].shape[0] // pieces[k]
        for i in range(pieces[k]):
            at = slice(i * size, (i + 1) * size)
            steps.append(
                (
                    pltpu.make_async_copy(srcs[k].at[at], bufs[k].at[at], sem.at[0, k, i]),
                    pltpu.make_async_copy(bufs[k].at[at], dsts[k].at[at], sem.at[1, k, i]),
                )
            )
    for read, _ in steps:
        read.start()
    for read, write in steps:
        read.wait()
        write.start()
    for _, write in steps:
        write.wait()


def outputs_call(*arrays):
    pieces = [4 if v.ndim == 3 else 1 for v in arrays]
    return pl.pallas_call(
        functools.partial(outputs_kernel, pieces),
        out_shape=tuple(jax.ShapeDtypeStruct(v.shape, v.dtype) for v in arrays),
        in_specs=[ANY] * len(arrays),
        out_specs=[ANY] * len(arrays),
        scratch_shapes=[pltpu.VMEM(v.shape, v.dtype) for v in arrays]
        + [pltpu.SemaphoreType.DMA((2, len(arrays), 4))],
        name="outputs",
    )(*arrays)


def on_device(
    rows, chips,
    hidden_in, segments, prefix_vis, prefix_key, prefix_value, w_query, w_key, w_value, w_out,
    norm1_gain, norm1_bias, w_up, w_down, norm2_gain, norm2_bias, out_grad,
):
    flat = lambda v: v.reshape(1, -1)
    _, _, block, input_grad, pk_grad, pv_grad = layer_call(
        rows, chips, hidden_in, segments, prefix_vis, w_query, w_key, w_value, prefix_key, prefix_value,
        w_out, w_up, w_down, out_grad, flat(norm1_gain), flat(norm1_bias), flat(norm2_gain), flat(norm2_bias),
    )
    return outputs_call(block, input_grad, pk_grad, pv_grad)


def solution(mesh):
    rows, chips = mesh.shape["rows"], mesh.shape["wide"] // 2
    act = P("wide", "rows", None)
    per_row = P("rows", None)
    in_specs = (
        act, per_row, per_row, *([P()] * 8), P(None, "wide"), P("wide", None), P(), P(), act,
    )
    out_specs = (act, act, P(), P())
    return jax.shard_map(
        functools.partial(on_device, rows, chips),
        mesh=mesh,
        in_specs=in_specs,
        out_specs=out_specs,
        check_vma=False,
    )
```

```python
import functools

import jax
import jax.numpy as jnp
from jax import lax
from jax.experimental import pallas as pl
from jax.experimental.pallas import tpu as pltpu
from jax.sharding import PartitionSpec as P

E = 64
P_SIZE = 64
SEGS = 4
PAIR = 2 * E
BIG = 1e30
norm_eps = 1e-05
root_half = 0.7071067811865476
inv_root_tau = 0.3989422804014327

BF = jnp.bfloat16
F32 = jnp.float32
MESH = pl.DeviceIdType.MESH
ANY = pl.BlockSpec(memory_space=pl.ANY)
VM = pl.BlockSpec(memory_space=pltpu.VMEM)
NN = (((1,), (0,)), ((), ()))
NT = (((1,), (1,)), ((), ()))
VMEM_LIMIT = 67043328


def dot(a, b, dims=NN):
    return lax.dot_general(a, b, dims, preferred_element_type=F32)


def lanes():
    return lax.broadcasted_iota(jnp.int32, (1, PAIR), 1)


def place():
    row, wide = lax.axis_index("rows"), lax.axis_index("wide")
    return row, wide, lax.rem(wide, 2), lax.div(wide, 2)


def remote(src, dst, send, recv, dev):
    return pltpu.make_async_remote_copy(
        src_ref=src, dst_ref=dst, send_sem=send, recv_sem=recv, device_id=dev, device_id_type=MESH
    )


def ring_pos(row, rows):
    half = rows // 2
    z, x = lax.div(row, 2), lax.rem(row, 2)
    return z + x * (2 * half - 1 - 2 * z)


def ring_row(pos, rows):
    pos = lax.rem(pos + 2 * rows, rows)
    upper = lax.div(pos, rows // 2)
    return 2 * pos + upper * (2 * rows - 1 - 4 * pos)


def mean_of(value):
    return jnp.mean(value, axis=-1, keepdims=True)


def layer_kernel(
    rows, chips,
    x_own, segs, vis, wq, wk, wv, pkey, pval, w_out, w_up, w_dn, og, g1, b1, g2, b2,
    pa_o, pb_o, block_o, ig_o, pk_o, pv_o,
    xbuf, up, dn, wo, mixtok, la, ma, mix_s, g_s, gs, wqkv, q_s, ka, va, kb, vb,
    got_b, y_in, got_a, psum, pr_in, pr_y, p_full, pin_b,
    load_sem, out_sem, p_sem, x_send, x_recv, y_send, y_recv, d_send, d_recv, f_sem, g_sem,
    mx_send, mx_recv, g_send, g_recv, e_send, e_recv, sh_send, sh_recv, r_send, r_recv, k_send, k_recv,
    l_send, l_recv, gm_send, gm_recv,
    db_send, db_recv, yb_send, yb_recv, da_send, da_recv,
    p1_send, p1_recv, p2_send, p2_recv, p3_send, p3_recv, p4_send, p4_recv,
):
    per, batch, width = x_own.shape
    tpc = 2 * per
    rem = (chips - 1) * tpc
    keys_b = rem + P_SIZE
    half = width // 2
    pairs = half // PAIR
    hidden = up.shape[3]
    tokens = batch * per
    row, wide, core, chip = place()
    partner = (row, wide + 1 - 2 * core)
    pos = ring_pos(row, rows)
    nxt = (ring_row(pos + 1, rows), wide)
    prv = (ring_row(pos - 1, rows), wide)
    peers = [(row, 2 * lax.rem(chip - d + chips, chips) + core) for d in range(1, chips)]
    mats = ((w_up, up), (w_dn, dn))
    cw = (rows // 2, 3)
    ccw = (rows // 2 - 1, 3)
    cuts = (1, 1)
    plane = [(lax.rem(row + t, rows), wide) for t in range(1, rows)]
    back = [(row, 2 * lax.rem(chip + d, chips) + core) for d in range(1, chips)]

    col = pl.multiple_of(core * half, half)
    far_loads = [
        pltpu.make_async_copy(w_up, up.at[0, core], load_sem.at[0]),
        pltpu.make_async_copy(w_dn, dn.at[0, core], load_sem.at[1]),
        pltpu.make_async_copy(w_out, wo, load_sem.at[2]),
    ]

    x_pair = remote(xbuf.at[:, 0, core], xbuf.at[:, 0, core], x_send, x_recv, partner)
    cross = [
        [
            remote(xbuf.at[r, 0, core], xbuf.at[r, d, core], y_send.at[r, d - 1], y_recv.at[r, d - 1], peers[d - 1])
            for d in range(1, chips)
        ]
        for r in range(batch)
    ]

    def piece(ref, row_at, cut=0, cuts_of=1):
        size = ref.shape[-2] // rows
        sub = size // cuts_of
        return pl.ds(pl.multiple_of(row_at * size + cut * sub, sub), sub)

    def w_cross(m, row_at, cut, cuts_of, send, recv):
        src, dst = mats[m]
        at = piece(src, row_at, cut, cuts_of)
        return [
            remote(src.at[at], dst.at[d, core, at], send.at[d - 1], recv.at[d - 1], peers[d - 1])
            for d in range(1, chips)
        ]

    split_cross = [
        [w_cross(m, row, h, cuts[m], g_send.at[m, h], g_recv.at[m, h]) for h in range(cuts[m])] for m in range(2)
    ]
    wcross = [sum(group, []) for group in split_cross]
    far_off = range(ccw[1] + 1, rows - cw[1])
    extras = sum([w_cross(1, ring_row(pos + o, rows), 0, 1, e_send.at[o], e_recv.at[o]) for o in far_off], [])
    shards = [
        remote(mats[m][0], mats[m][1].at[0, core], sh_send.at[m], sh_recv.at[m], partner) for m in range(2)
    ]

    def place_of(s, way):
        return ring_row(pos - s if way == 0 else pos + s, rows)

    def ring_copy(m, s, way, h):
        buf = mats[m][1]
        ref = buf.at[1:, core, piece(buf, place_of(s - 1, way), h, cuts[m])]
        return remote(ref, ref, r_send.at[m, s, way, h], r_recv.at[m, s, way, h], nxt if way == 0 else prv)

    def hand_over(m, s, way, h):
        buf = mats[m][1]
        ref = buf.at[1:, core, piece(buf, place_of(s, way), h, cuts[m])]
        return remote(ref, ref, k_send.at[m, s, way, h], k_recv.at[m, s, way, h], partner)

    def ways(m, s):
        return range(2 if s <= ccw[m] else 1)

    def hop(m, s, h=0):
        if s > cw[m] + 1 or h >= cuts[m]:
            return
        if s == 1:
            for copy in split_cross[m][h]:
                copy.wait_recv()
        else:
            for way in ways(m, s - 1):
                ring_copy(m, s - 1, way, h).wait_recv()
        if s <= cw[m]:
            for way in ways(m, s):
                ring_copy(m, s, way, h).start()
        for way in ways(m, s - 1) if s > 1 else range(1):
            hand_over(m, s - 1, way, h).start()

    def extra_over(o):
        buf = mats[1][1]
        ref = buf.at[1:, core, piece(buf, place_of(o, 1))]
        return remote(ref, ref, l_send.at[o], l_recv.at[o], partner)

    def take_extras():
        for copy in extras:
            copy.wait_recv()
        for o in far_off:
            extra_over(o).start()

    def all_over(m):
        copies = [hand_over(m, 0, 0, h) for h in range(cuts[m])]
        for s in range(1, cw[m] + 1):
            copies += [hand_over(m, s, way, h) for way in ways(m, s) for h in range(cuts[m])]
        if m == 1:
            copies += [extra_over(o) for o in far_off]
        return copies

    def gathered(m):
        for copy in all_over(m):
            copy.wait_recv()

    def sent(m):
        for copy in wcross[m] + all_over(m) + (extras if m == 1 else []):
            copy.wait_send()
        for s in range(1, cw[m] + 1):
            for way in ways(m, s):
                for h in range(cuts[m]):
                    ring_copy(m, s, way, h).wait_send()

    mine_at, other_at = pl.multiple_of(core * per, per), pl.multiple_of((1 - core) * per, per)

    def mix_out(r, p):
        cols = pl.ds(pl.multiple_of(core * half + p * PAIR, PAIR), PAIR)
        dst = mixtok.at[pl.ds(pl.multiple_of(r * per, per), per), cols]
        return (
            remote(mix_s.at[r, p, pl.ds(other_at, per)], dst, mx_send.at[r, p], mx_recv.at[r, p], partner),
            pltpu.make_async_copy(mix_s.at[r, p, pl.ds(mine_at, per)], dst, f_sem.at[r, p]),
        )

    def attention(pks, pvs, s0, s1, s2, s3, oa, pst_a, pst_b, qe, kea, keb, xraw):
        x_load = pltpu.make_async_copy(x_own, xraw, load_sem.at[3 + batch])
        loads = [
            pltpu.make_async_copy(wq.at[:, pl.ds(col, half)], wqkv.at[:, 0:half], load_sem.at[4 + batch]),
            pltpu.make_async_copy(wk.at[:, pl.ds(col, half)], wqkv.at[:, half : 2 * half], load_sem.at[5 + batch]),
            pltpu.make_async_copy(wv.at[:, pl.ds(col, half)], wqkv.at[:, 2 * half : 3 * half], load_sem.at[6 + batch]),
            pltpu.make_async_copy(pkey.at[:, pl.ds(col, half)], pks, load_sem.at[7 + batch]),
            pltpu.make_async_copy(pval.at[:, pl.ds(col, half)], pvs, load_sem.at[8 + batch]),
        ]
        barrier = pltpu.get_barrier_semaphore()
        friends = [partner] + plane + peers
        for dev in friends:
            pl.semaphore_signal(barrier, inc=1, device_id=dev, device_id_type=MESH)
        x_load.start()
        for copy in loads:
            copy.start()
        pl.semaphore_wait(barrier, len(friends))
        for group in wcross:
            for copy in group:
                copy.start()
        x_load.wait()
        for r in range(batch):
            xbuf[r, 0, core] = xraw[:, r, :]
        x_pair.start()
        for group in cross + [extras]:
            for copy in group:
                copy.start()
        for copy in shards + far_loads:
            copy.start()

        term = lax.broadcasted_iota(jnp.int32, (PAIR, 1), 0)
        term = jnp.where(term >= E, term - E, term)

        def key_terms(seg):
            off = jnp.where(jnp.logical_and(term < SEGS, seg != term), -BIG, 0.0)
            return off.T.astype(BF)

        for r in range(batch):
            for d in range(chips):
                at = pl.multiple_of(lax.rem(chip + d, chips) * tpc, tpc)
                seg = segs[r : r + 1, pl.ds(at, tpc)]
                if d == 0:
                    kea[r] = key_terms(seg)
                    on = jnp.logical_or(term == SEGS, jnp.logical_and(term < SEGS, seg == term))
                    qe[r] = jnp.where(on, 1.0, 0.0).T.astype(BF)
                else:
                    keb[r, (d - 1) * tpc : d * tpc] = key_terms(seg)
            unseen = jnp.logical_and(term == SEGS, vis[r : r + 1, :] == 0)
            keb[r, rem:] = jnp.where(unseen, -BIG, 0.0).T.astype(BF)

        def project(r, d, cb, with_q):
            x = xbuf[r, d, cb]
            if with_q:
                q = (dot(x, wqkv[:, 0:half]) * 0.125).astype(BF)
                for p in range(pairs):
                    q_s[r, p, pl.ds(pl.multiple_of(cb * per, per), per), :] = q[:, p * PAIR : (p + 1) * PAIR]
            for ref_a, ref_b, at in ((ka, kb, 1), (va, vb, 2)):
                y = dot(x, wqkv[:, at * half : (at + 1) * half]).astype(BF)
                for p in range(pairs):
                    val = y[:, p * PAIR : (p + 1) * PAIR]
                    if with_q:
                        ref_a[r, p, pl.ds(pl.multiple_of(cb * per, per), per), :] = val
                    else:
                        ref_b[r, p, pl.ds(pl.multiple_of((d - 1) * tpc + cb * per, per), per), :] = val

        for copy in loads:
            copy.wait()
        for r in range(batch):
            for p in range(pairs):
                kb[r, p, rem:, :] = pks[:, p * PAIR : (p + 1) * PAIR]
                vb[r, p, rem:, :] = pvs[:, p * PAIR : (p + 1) * PAIR]

        @pl.loop(0, 2 * batch)
        def _(i):
            pl.when(i == batch)(x_pair.wait_recv)
            late = lax.div(i, batch)
            project(lax.rem(i, batch), 0, core + late - 2 * core * late, True)

        hop(0, 1)
        bufs = (s0, s1, s2, s3)

        def score(r, p, h, k_s, kext, buf):
            keys = k_s.shape[2]
            mine = lanes() < E if h == 0 else lanes() >= E
            q = jnp.where(mine, q_s[r, p], qe[r])
            k = jnp.where(mine, k_s[r, p], kext[r])
            buf[:, 0:keys] = dot(q, k, NT)

        def unit(r, p, after, u, k_s, v_s, kext, pst, p_hbm, finish, wait_slot):
            keys = k_s.shape[2]
            copy = pltpu.make_async_copy(pst.at[u], p_hbm.at[r, p], p_sem.at[u])
            pl.when(wait_slot)(copy.wait)
            tops, sums = [], []
            for h in range(2):
                score(after[0], after[1], h, k_s, kext, bufs[2 * (1 - u) + h])
                s = bufs[2 * u + h][:, 0:keys]
                top = jnp.max(s, axis=1, keepdims=True)
                prob = jnp.exp(s - top).astype(BF)
                pst[u, h] = prob
                mine = lanes() < E if h == 0 else lanes() >= E
                v = jnp.where(mine, v_s[r, p], jnp.ones((1, PAIR), BF))
                sums.append(dot(prob, v))
                tops.append(top)
            copy.start()
            low = lanes() < E
            finish(
                r,
                p,
                jnp.where(low, sums[0], sums[1]),
                pltpu.roll(jnp.where(low, sums[1], sums[0]), E, 1),
                jnp.where(low, tops[0], tops[1]),
            )

        def finish_a(r, p, o, l, m):
            oa[r, p], la[r, p], ma[r, p] = o, l, m

        def finish_b(r, p, o, l, m):
            top = jnp.maximum(ma[r, p], m)
            w_a, w_b = jnp.exp(ma[r, p] - top), jnp.exp(m - top)
            inv = 1.0 / (w_a * la[r, p] + w_b * l)
            r_a, r_b = w_a * inv, w_b * inv
            mix_s[r, p] = (oa[r, p] * r_a + o * r_b).astype(BF)
            la[r, p], ma[r, p] = r_a, r_b

        def drain(pst, p_hbm):
            for u in range(2):
                pltpu.make_async_copy(pst.at[u], p_hbm.at[0, 0], p_sem.at[u]).wait()

        args_a = (ka, va, kea, pst_a, pa_o, finish_a)
        for h in range(2):
            score(0, 0, h, ka, kea, bufs[h])
        count = batch * pairs

        @pl.loop(0, count // 2)
        def _(i):
            for u in range(2):
                j = 2 * i + u
                after = jnp.minimum(j + 1, count - 1)
                unit(
                    lax.div(j, pairs), lax.rem(j, pairs), (lax.div(after, pairs), lax.rem(after, pairs)),
                    u, *args_a, i > 0,
                )

            @pl.when(i == 2)
            def _():
                hop(1, 1)

        drain(pst_a, pa_o)
        hop(0, 2)
        hop(1, 2)

        args_b = (kb, vb, keb, pst_b, pb_o, finish_b)

        @pl.loop(0, batch)
        def _(r):
            for d in range(1, chips):
                remote(
                    xbuf.at[r, 0, core], xbuf.at[r, d, core], y_send.at[r, d - 1], y_recv.at[r, d - 1], peers[d - 1]
                ).wait_recv()
            forward = remote(
                xbuf.at[r, 1:, core], xbuf.at[r, 1:, core], d_send.at[r], d_recv.at[r], partner
            )
            forward.start()

            @pl.loop(0, 2 * (chips - 1))
            def _(i):
                pl.when(i == chips - 1)(forward.wait_recv)
                late = lax.div(i, chips - 1)
                project(r, lax.rem(i, chips - 1) + 1, core + late - 2 * core * late, False)

            @pl.when(r == 0)
            def _():
                hop(0, 3)

            @pl.when(r == 1)
            def _():
                hop(0, 4)

            for h in range(2):
                score(r, 0, h, kb, keb, bufs[h])

            @pl.loop(0, pairs // 2)
            def _(i):
                for u in range(2):
                    p = 2 * i + u
                    unit(r, p, (r, jnp.minimum(p + 1, pairs - 1)), u, *args_b, i > 0)

            drain(pst_b, pb_o)
            for p in range(pairs):
                for copy in mix_out(r, p):
                    copy.start()
            forward.wait_send()

            @pl.when(r == 0)
            def _():
                hop(1, 3)

        for s in range(5, cw[0] + 1):
            hop(0, s)
        hop(1, 4)
        take_extras()
        x_pair.wait_send()

    vm = pltpu.VMEM
    keys = max(tpc, keys_b)
    pl.run_scoped(
        attention,
        vm((P_SIZE, half), BF),
        vm((P_SIZE, half), BF),
        *([vm((tpc, keys), F32)] * 4),
        vm((batch, pairs, tpc, PAIR), F32),
        vm((2, 2, tpc, tpc), BF),
        vm((2, 2, tpc, keys_b), BF),
        vm((batch, tpc, PAIR), BF),
        vm((batch, tpc, PAIR), BF),
        vm((batch, keys_b, PAIR), BF),
        vm((per, batch, width), BF),
    )

    tile = min(512, hidden)
    tiles = hidden // tile
    total = 2 * chips * tiles
    chunk = 64

    def fetch(pin, p_hbm, r, p, u):
        return pltpu.make_async_copy(p_hbm.at[r, p], pin.at[u], p_sem.at[u])

    def feed_forward(ogs, gst, sc1, inv1, acc, slope, pre0, pre1, bst):
        nl = mixtok
        og_loads = [pltpu.make_async_copy(og.at[:, r], ogs.at[r], load_sem.at[3 + r]) for r in range(batch)]
        for copy in og_loads:
            copy.start()
        for u in range(2):
            fetch(pin_b, pb_o, 0, u, u).start()
        for copy in far_loads:
            copy.wait()
        for r in range(batch):
            for p in range(pairs):
                for copy in mix_out(r, p):
                    copy.wait()

        @pl.loop(0, width // 256)
        def _(j):
            at = pl.ds(pl.multiple_of(j * 256, 256), 256)
            acc[:, at] = dot(mixtok[...], wo[:, at])

        def by_rows(body):
            for r in range(batch):

                @pl.loop(0, per // chunk, unroll=min(2, per // chunk))
                def _(i, r=r):
                    inner = pl.ds(pl.multiple_of(i * chunk, chunk), chunk)
                    body(r, inner, pl.ds(pl.multiple_of(r * per + i * chunk, chunk), chunk))

        def norm_one(r, inner, at):
            z = acc[at] + xbuf[r, 0, core, inner].astype(F32)
            c = z - mean_of(z)
            inv = lax.rsqrt(mean_of(c * c) + norm_eps)
            s = c * inv
            n = s * g1[...] + b1[...]
            nl[at], sc1[at], inv1[at] = n.astype(BF), s, inv
            acc[at] = jnp.zeros_like(z)

        by_rows(norm_one)
        for copy in shards + og_loads:
            copy.wait()

        def split(j):
            slot = lax.div(j, tiles)
            at = pl.ds(pl.multiple_of(lax.rem(j, tiles) * tile, tile), tile)
            return lax.div(slot, 2), lax.rem(slot, 2), at

        def up_tile(j, buf):
            d, c, at = split(j)
            buf[...] = dot(nl[...], up[d, c, :, at])

        pres = (pre0, pre1)
        up_tile(0, pre0)

        @pl.loop(0, total // 2)
        def _(i):
            @pl.when(i == max(tiles - 1, 0))
            def _():
                hop(0, cw[0] + 1)
                gathered(0)

            @pl.when(i == tiles)
            def _():
                gathered(1)

            for u in range(2):
                j = 2 * i + u
                up_tile(jnp.minimum(j + 1, total - 1), pres[1 - u])
                v = pres[u][...]
                cdf = 0.5 * (1.0 + lax.erf(v * root_half))
                a = (v * cdf).astype(BF)
                d, c, at = split(j)
                slope[j] = (cdf + v * jnp.exp(-0.5 * v * v) * inv_root_tau).astype(BF)
                acc[...] += dot(a, dn[d, c, at, :])

        def norm_two(r, inner, at):
            z = sc1[at] * g1[...] + b1[...] + acc[at]
            c = z - mean_of(z)
            inv = lax.rsqrt(mean_of(c * c) + norm_eps)
            s = c * inv
            bst[inner, r, :] = (s * g2[...] + b2[...]).astype(BF)
            t = ogs[r, inner] * g2[...]
            g = inv * (t - mean_of(t) - s * mean_of(t * s))
            gs[at], nl[at] = g, g.astype(BF)
            acc[at] = jnp.zeros_like(z)

        by_rows(norm_two)
        outs = [pltpu.make_async_copy(bst, block_o, out_sem.at[0])]
        outs[0].start()

        def down_back(j, buf):
            d, c, at = split(j)
            buf[...] = dot(nl[...], dn[d, c, at, :], NT)

        down_back(0, pre0)

        @pl.loop(0, total // 2)
        def _(i):
            for u in range(2):
                j = 2 * i + u
                down_back(jnp.minimum(j + 1, total - 1), pres[1 - u])
                g = (pres[u][...] * slope[j].astype(F32)).astype(BF)
                d, c, at = split(j)
                acc[...] += dot(g, up[d, c, :, at], NT)

        def norm_back(r, inner, at):
            t = (gs[at] + acc[at]) * g1[...]
            s = sc1[at]
            g = inv1[at] * (t - mean_of(t) - s * mean_of(t * s))
            gs[at], nl[at] = g, g.astype(BF)

        by_rows(norm_back)
        mine = pl.ds(mine_at, per)
        for side in range(2):
            base = (1 - core) * half if side == 0 else core * half
            g = dot(nl[...], wo[pl.ds(pl.multiple_of(base, half), half), :], NT).astype(BF)
            for p in range(pairs):
                for r in range(batch):
                    val = g[r * per : (r + 1) * per, p * PAIR : (p + 1) * PAIR]
                    if side == 0:
                        gst[r, p] = val
                    else:
                        g_s[r, p, mine, :] = val
            if side == 0:
                sends = [
                    remote(gst.at[r, p], g_s.at[r, p, mine], gm_send.at[r, p], gm_recv.at[r, p], partner)
                    for r in range(batch)
                    for p in range(pairs)
                ]
                for copy in sends:
                    copy.start()
        for copy in sends + outs:
            copy.wait()

    pl.run_scoped(
        feed_forward,
        vm((batch, per, width), F32),
        vm((batch, pairs, per, PAIR), BF),
        vm((tokens, width), F32),
        vm((tokens, 1), F32),
        vm((tokens, width), F32),
        vm((total, tokens, tile), BF),
        vm((tokens, tile), F32),
        vm((tokens, tile), F32),
        vm((per, batch, width), BF),
    )

    def attention_back(pin_a, s0, s1, s2, s3, do0, do1, dq, dks, dvs, half_b, send_b, y_out, send_a):
        bufs, dos = (s0, s1, s2, s3), (do0, do1)

        def first(r, p, u, v_s, scale):
            keys = v_s.shape[2]
            g = g_s[r, p].astype(F32) * scale[r, p]
            do = g.astype(BF)
            dos[u][...] = do
            t = g * mix_s[r, p].astype(F32)
            lane = lanes()
            for h in range(2):
                mine = lane < E if h == 0 else lane >= E
                delta = jnp.sum(jnp.where(mine, t, 0.0), axis=1, keepdims=True)
                hi = delta.astype(BF)
                left = delta - hi.astype(F32)
                mid = left.astype(BF)
                low = (left - mid.astype(F32)).astype(BF)
                at = E if h == 0 else 0
                ext = jnp.where(
                    lane == at, -hi, jnp.where(lane == at + 1, -mid, jnp.where(lane == at + 2, -low, jnp.zeros((1, PAIR), BF)))
                )
                one = jnp.where(jnp.logical_and(lane >= at, lane < at + 3), 1.0, 0.0).astype(BF)
                bufs[2 * u + h][:, 0:keys] = dot(
                    jnp.where(mine, do, ext), jnp.where(mine, v_s[r, p], one), NT
                )

        def second(r, p, u, k_s, pin, start_dq, prefix):
            keys = k_s.shape[2]
            q2, k2, do = q_s[r, p], k_s[r, p], dos[u][...]
            do_t, q_t = do.T, q2.T
            gq, gk, gv = [], [], []
            for h in range(2):
                prob = pin[u, h]
                ds = (prob.astype(F32) * bufs[2 * u + h][:, 0:keys]).astype(BF)
                at = slice(h * E, (h + 1) * E)
                gv.append(dot(do_t[at], prob))
                gk.append(dot(q_t[at], ds))
                gq.append(dot(ds, k2))
            low = lanes() < E
            grad = jnp.where(low, gq[0], gq[1])
            dq[r, p] = grad if start_dq else dq[r, p] + grad
            cols = pl.ds(pl.multiple_of(p * PAIR, PAIR), PAIR)
            for ref, parts, k in ((dks, gk, 0), (dvs, gv, 1)):
                val = jnp.concatenate(parts, axis=0).T
                if prefix:
                    ref[0:rem, cols] = val[:rem].astype(BF)
                    psum[k * P_SIZE : (k + 1) * P_SIZE, cols] += val[rem:]
                else:
                    ref[0:tpc, cols] = val.astype(BF)

        def group(r, k_s, v_s, scale, pin, p_hbm, start_dq, prefix, between=None):
            first(r, 0, 0, v_s, scale)

            @pl.loop(0, pairs // 2)
            def _(i):
                for u in range(2):
                    p = 2 * i + u
                    fetch(pin, p_hbm, r, p, u).wait()
                    first(r, jnp.minimum(p + 1, pairs - 1), 1 - u, v_s, scale)
                    second(r, p, u, k_s, pin, start_dq, prefix)

                    @pl.when(i < pairs // 2 - 1)
                    def _():
                        fetch(pin, p_hbm, r, p + 2, u).start()
                if between is not None:
                    between(r, i)

        def to_inputs(at):
            keys = dot(dks[at], wqkv[:, half : 2 * half], NT)
            return keys + dot(dvs[at], wqkv[:, 2 * half : 3 * half], NT)

        psum[...] = jnp.zeros_like(psum)
        far = range(1, chips)

        def b_copy(r, d):
            return remote(
                send_b.at[r, d - 1], got_b.at[r, d - 1], db_send.at[r, d - 1], db_recv.at[r, d - 1], partner
            )

        def y_copy(r, d):
            return remote(
                y_out.at[r, d - 1], y_in.at[r, d - 1], yb_send.at[r, d - 1], yb_recv.at[r, d - 1], back[d - 1]
            )

        def a_copy(r):
            return remote(send_a.at[r], got_a.at[r], da_send.at[r], da_recv.at[r], partner)

        def token_rows(r):
            return pl.ds(pl.multiple_of(r * per, per), per)

        def out_copy(r):
            return pltpu.make_async_copy(gs.at[token_rows(r)], ig_o.at[:, r], out_sem.at[r])

        @pl.loop(0, batch)
        def _(r):
            group(r, kb, vb, ma, pin_b, pb_o, True, True)

            @pl.when(r + 1 < batch)
            def _():
                for u in range(2):
                    fetch(pin_b, pb_o, r + 1, u, u).start()

            @pl.when(r + 1 == batch)
            def _():
                for u in range(2):
                    fetch(pin_a, pa_o, 0, u, u).start()

            for d in far:
                at = pl.ds(pl.multiple_of((d - 1) * tpc + (1 - core) * per, per), per)
                send_b[r, d - 1] = to_inputs(at).astype(BF)
                b_copy(r, d).start()
            for d in far:
                at = pl.ds(pl.multiple_of((d - 1) * tpc + core * per, per), per)
                half_b[d - 1] = to_inputs(at)
            for d in far:
                b_copy(r, d).wait_recv()
                y_out[r, d - 1] = (half_b[d - 1] + got_b[r, d - 1].astype(F32)).astype(BF)
                y_copy(r, d).start()

        size = 2 * P_SIZE // rows

        def part(at):
            return pl.ds(pl.multiple_of(at * size, size), size)

        p_one = [
            remote(psum.at[part(plane[t - 1][0])], pr_in.at[t - 1], p1_send.at[t - 1], p1_recv.at[t - 1], plane[t - 1])
            for t in range(1, rows)
        ]
        p_two = [remote(pr_y.at[0], pr_y.at[d], p2_send.at[d - 1], p2_recv.at[d - 1], peers[d - 1]) for d in far]
        p_three = [
            remote(p_full.at[part(row)], p_full.at[part(row)], p3_send.at[t - 1], p3_recv.at[t - 1], plane[t - 1])
            for t in range(1, rows)
        ]
        cols = pl.ds(col, half)
        p_four = [
            remote(
                p_full.at[k * P_SIZE : (k + 1) * P_SIZE], ref.at[:, cols], p4_send.at[k], p4_recv.at[k], partner
            )
            for k, ref in enumerate((pk_o, pv_o))
        ]
        p_five = [
            pltpu.make_async_copy(p_full.at[k * P_SIZE : (k + 1) * P_SIZE], ref.at[:, cols], out_sem.at[batch + k])
            for k, ref in enumerate((pk_o, pv_o))
        ]
        for copy in p_one:
            copy.start()

        def over_rows():
            for copy in p_one:
                copy.wait_recv()
            total = psum[part(row)]
            for t in range(1, rows):
                total = total + pr_in[t - 1]
            pr_y[0] = total
            for copy in p_two:
                copy.start()

        def over_chips():
            for copy in p_two:
                copy.wait_recv()
            whole = jnp.zeros((size, half), F32)
            for c in range(chips):
                whole = whole + pr_y[lax.rem(c - chip + chips, chips)]
            p_full[part(row)] = whole
            for copy in p_three:
                copy.start()

        def to_all():
            for copy in p_three:
                copy.wait_recv()
            for copy in p_four + p_five:
                copy.start()

        def finish(r):
            a_copy(r).wait_recv()
            val = gs[token_rows(r)] + got_a[r].astype(F32)
            for d in far:
                y_copy(r, d).wait_recv()
                val = val + y_in[r, d - 1].astype(F32)
            gs[token_rows(r)] = val
            out_copy(r).start()

        def between(r, i):
            @pl.when(jnp.logical_and(r == 0, i == 0))
            def _():
                over_rows()

            @pl.when(jnp.logical_and(r == 1, i == 0))
            def _():
                over_chips()

        @pl.loop(0, batch)
        def _(r):
            group(r, ka, va, la, pin_a, pa_o, False, False, between)

            @pl.when(r + 1 < batch)
            def _():
                for u in range(2):
                    fetch(pin_a, pa_o, r + 1, u, u).start()

            for side in range(2):
                block = pl.multiple_of(((1 - core) if side == 0 else core) * per, per)
                at = pl.ds(block, per)
                part_in = to_inputs(at)
                for p in range(pairs):
                    dvs[at, p * PAIR : (p + 1) * PAIR] = (dq[r, p, at, :]).astype(BF)
                val = part_in + 0.125 * dot(dvs[at], wqkv[:, 0:half], NT)
                if side == 0:
                    send_a[r] = val.astype(BF)
                    a_copy(r).start()
                else:
                    gs[token_rows(r)] += val

            @pl.when(r == 1)
            def _():
                to_all()
                finish(0)

        for r in range(1, batch):
            finish(r)
        for r in range(batch):
            a_copy(r).wait_send()
            for d in far:
                b_copy(r, d).wait_send()
                y_copy(r, d).wait_send()
            out_copy(r).wait()
        for copy in p_one + p_two + p_three:
            copy.wait_send()
        for copy in p_four + p_five:
            copy.wait()

    pl.run_scoped(
        attention_back,
        vm((2, 2, tpc, tpc), BF),
        *([vm((tpc, keys), F32)] * 4),
        *([vm((tpc, PAIR), BF)] * 2),
        vm((batch, pairs, tpc, PAIR), F32),
        vm((keys, half), BF),
        vm((keys, half), BF),
        vm((chips - 1, per, width), F32),
        *([vm((batch, chips - 1, per, width), BF)] * 2),
        vm((batch, per, width), BF),
    )
    for r in range(batch):
        for copy in cross[r]:
            copy.wait_send()
    for m in range(2):
        sent(m)


def layer_call(rows, chips, x, segs, vis, wq, wk, wv, pkey, pval, w_out, w_up, w_dn, og, g1, b1, g2, b2):
    per, batch, width = x.shape
    tpc, half = 2 * per, width // 2
    far = chips - 1
    keys_b = far * tpc + P_SIZE
    pairs = half // PAIR
    tokens = batch * per
    steps = rows // 2
    size = 2 * P_SIZE // rows
    out = lambda dt, *s: jax.ShapeDtypeStruct(s, dt)
    shapes = (
        out(BF, batch, pairs, 2, tpc, tpc),
        out(BF, batch, pairs, 2, tpc, keys_b),
        out(BF, per, batch, width),
        out(F32, per, batch, width),
        out(F32, P_SIZE, width),
        out(F32, P_SIZE, width),
    )
    dma = pltpu.SemaphoreType.DMA
    vm = pltpu.VMEM
    scratch = [
        vm((batch, chips, 2, per, width), BF),
        vm((chips, 2, *w_up.shape), BF),
        vm((chips, 2, *w_dn.shape), BF),
        vm((width, width), BF),
        vm((tokens, width), BF),
        vm((batch, pairs, tpc, PAIR), F32),
        vm((batch, pairs, tpc, PAIR), F32),
        vm((batch, pairs, tpc, PAIR), BF),
        vm((batch, pairs, tpc, PAIR), BF),
        vm((tokens, width), F32),
        vm((width, 3 * half), BF),
        vm((batch, pairs, tpc, PAIR), BF),
        vm((batch, pairs, tpc, PAIR), BF),
        vm((batch, pairs, tpc, PAIR), BF),
        vm((batch, pairs, keys_b, PAIR), BF),
        vm((batch, pairs, keys_b, PAIR), BF),
        vm((batch, far, per, width), BF),
        vm((batch, far, per, width), BF),
        vm((batch, per, width), BF),
        vm((2 * P_SIZE, half), F32),
        vm((rows - 1, size, half), F32),
        vm((chips, size, half), F32),
        vm((2 * P_SIZE, half), F32),
        vm((2, 2, tpc, keys_b), BF),
        dma((9 + batch,)), dma((5,)), dma((2,)), dma, dma,
        dma((batch, far)), dma((batch, far)),
        dma((batch,)), dma((batch,)),
        dma((batch, pairs)), dma((batch, pairs)),
        dma((batch, pairs)), dma((batch, pairs)),
        dma((2, 2, far)), dma((2, 2, far)),
        dma((rows, far)), dma((rows, far)),
        dma((2,)), dma((2,)),
        dma((2, steps + 1, 2, 2)), dma((2, steps + 1, 2, 2)),
        dma((2, steps + 1, 2, 2)), dma((2, steps + 1, 2, 2)),
        dma((rows,)), dma((rows,)),
        dma((batch, pairs)), dma((batch, pairs)),
        dma((batch, far)), dma((batch, far)),
        dma((batch, far)), dma((batch, far)),
        dma((batch,)), dma((batch,)),
        dma((rows - 1,)), dma((rows - 1,)),
        dma((far,)), dma((far,)),
        dma((rows - 1,)), dma((rows - 1,)),
        dma((2,)), dma((2,)),
    ]
    return pl.pallas_call(
        functools.partial(layer_kernel, rows, chips),
        out_shape=shapes,
        in_specs=[ANY] + [VM] * 2 + [ANY] * 9 + [VM] * 4,
        out_specs=[ANY] * len(shapes),
        scratch_shapes=scratch,
        compiler_params=pltpu.CompilerParams(
            collective_id=0, has_side_effects=True, vmem_limit_bytes=VMEM_LIMIT
        ),
        name="layer",
    )(x, segs, vis, wq, wk, wv, pkey, pval, w_out, w_up, w_dn, og, g1, b1, g2, b2)


def outputs_kernel(pieces, *refs):
    count = len(refs) // 3
    srcs, dsts, bufs, sem = refs[:count], refs[count : 2 * count], refs[2 * count : 3 * count], refs[-1]
    steps = []
    for k in range(count):
        size = srcs[k].shape[0] // pieces[k]
        for i in range(pieces[k]):
            at = slice(i * size, (i + 1) * size)
            steps.append(
                (
                    pltpu.make_async_copy(srcs[k].at[at], bufs[k].at[at], sem.at[0, k, i]),
                    pltpu.make_async_copy(bufs[k].at[at], dsts[k].at[at], sem.at[1, k, i]),
                )
            )
    for read, _ in steps:
        read.start()
    for read, write in steps:
        read.wait()
        write.start()
    for _, write in steps:
        write.wait()


def outputs_call(*arrays):
    pieces = [4 if v.ndim == 3 else 1 for v in arrays]
    return pl.pallas_call(
        functools.partial(outputs_kernel, pieces),
        out_shape=tuple(jax.ShapeDtypeStruct(v.shape, v.dtype) for v in arrays),
        in_specs=[ANY] * len(arrays),
        out_specs=[ANY] * len(arrays),
        scratch_shapes=[pltpu.VMEM(v.shape, v.dtype) for v in arrays]
        + [pltpu.SemaphoreType.DMA((2, len(arrays), 4))],
        name="outputs",
    )(*arrays)


def on_device(
    rows, chips,
    hidden_in, segments, prefix_vis, prefix_key, prefix_value, w_query, w_key, w_value, w_out,
    norm1_gain, norm1_bias, w_up, w_down, norm2_gain, norm2_bias, out_grad,
):
    flat = lambda v: v.reshape(1, -1)
    _, _, block, input_grad, pk_grad, pv_grad = layer_call(
        rows, chips, hidden_in, segments, prefix_vis, w_query, w_key, w_value, prefix_key, prefix_value,
        w_out, w_up, w_down, out_grad, flat(norm1_gain), flat(norm1_bias), flat(norm2_gain), flat(norm2_bias),
    )
    return outputs_call(block, input_grad, pk_grad, pv_grad)


def solution(mesh):
    rows, chips = mesh.shape["rows"], mesh.shape["wide"] // 2
    act = P("wide", "rows", None)
    per_row = P("rows", None)
    in_specs = (
        act, per_row, per_row, *([P()] * 8), P(None, "wide"), P("wide", None), P(), P(), act,
    )
    out_specs = (act, act, P(), P())
    return jax.shard_map(
        functools.partial(on_device, rows, chips),
        mesh=mesh,
        in_specs=in_specs,
        out_specs=out_specs,
        check_vma=False,
    )
```

```python
import functools

import jax
import jax.numpy as jnp
from jax import lax
from jax.experimental import pallas as pl
from jax.experimental.pallas import tpu as pltpu
from jax.sharding import PartitionSpec as P

E = 64
P_SIZE = 64
SEGS = 4
PAIR = 2 * E
BIG = 1e30
norm_eps = 1e-05
root_half = 0.7071067811865476
inv_root_tau = 0.3989422804014327

BF = jnp.bfloat16
F32 = jnp.float32
MESH = pl.DeviceIdType.MESH
ANY = pl.BlockSpec(memory_space=pl.ANY)
VM = pl.BlockSpec(memory_space=pltpu.VMEM)
NN = (((1,), (0,)), ((), ()))
NT = (((1,), (1,)), ((), ()))
VMEM_LIMIT = 67043328


def dot(a, b, dims=NN):
    return lax.dot_general(a, b, dims, preferred_element_type=F32)


def lanes():
    return lax.broadcasted_iota(jnp.int32, (1, PAIR), 1)


def place():
    row, wide = lax.axis_index("rows"), lax.axis_index("wide")
    return row, wide, lax.rem(wide, 2), lax.div(wide, 2)


def remote(src, dst, send, recv, dev):
    return pltpu.make_async_remote_copy(
        src_ref=src, dst_ref=dst, send_sem=send, recv_sem=recv, device_id=dev, device_id_type=MESH
    )


def ring_pos(row, rows):
    half = rows // 2
    z, x = lax.div(row, 2), lax.rem(row, 2)
    return z + x * (2 * half - 1 - 2 * z)


def ring_row(pos, rows):
    pos = lax.rem(pos + 2 * rows, rows)
    upper = lax.div(pos, rows // 2)
    return 2 * pos + upper * (2 * rows - 1 - 4 * pos)


def mean_of(value):
    return jnp.mean(value, axis=-1, keepdims=True)


def layer_kernel(
    rows, chips,
    x_own, segs, vis, wq, wk, wv, pkey, pval, w_out, w_up, w_dn, og, g1, b1, g2, b2,
    pa_o, pb_o, block_o, ig_o, pk_o, pv_o,
    xbuf, up, dn, wo, mixtok, la, ma, mix_s, g_s, gs, wqkv, q_s, ka, va, kb, vb,
    got_b, y_in, got_a, psum, pr_in, pr_y, p_full, pin_b,
    load_sem, out_sem, p_sem, x_send, x_recv, y_send, y_recv, d_send, d_recv, f_sem, g_sem,
    mx_send, mx_recv, g_send, g_recv, e_send, e_recv, sh_send, sh_recv, r_send, r_recv, k_send, k_recv,
    l_send, l_recv, gm_send, gm_recv,
    db_send, db_recv, yb_send, yb_recv, da_send, da_recv,
    p1_send, p1_recv, p2_send, p2_recv, p3_send, p3_recv, p4_send, p4_recv,
):
    per, batch, width = x_own.shape
    tpc = 2 * per
    rem = (chips - 1) * tpc
    keys_b = rem + P_SIZE
    half = width // 2
    pairs = half // PAIR
    hidden = up.shape[3]
    tokens = batch * per
    row, wide, core, chip = place()
    partner = (row, wide + 1 - 2 * core)
    pos = ring_pos(row, rows)
    nxt = (ring_row(pos + 1, rows), wide)
    prv = (ring_row(pos - 1, rows), wide)
    peers = [(row, 2 * lax.rem(chip - d + chips, chips) + core) for d in range(1, chips)]
    mats = ((w_up, up), (w_dn, dn))
    cw = (rows // 2, 3)
    ccw = (rows // 2 - 1, 2)
    cuts = (1, 1)
    plane = [(lax.rem(row + t, rows), wide) for t in range(1, rows)]
    back = [(row, 2 * lax.rem(chip + d, chips) + core) for d in range(1, chips)]

    col = pl.multiple_of(core * half, half)
    far_loads = [
        pltpu.make_async_copy(w_up, up.at[0, core], load_sem.at[0]),
        pltpu.make_async_copy(w_dn, dn.at[0, core], load_sem.at[1]),
        pltpu.make_async_copy(w_out, wo, load_sem.at[2]),
    ]

    x_pair = remote(xbuf.at[:, 0, core], xbuf.at[:, 0, core], x_send, x_recv, partner)
    cross = [
        [
            remote(xbuf.at[r, 0, core], xbuf.at[r, d, core], y_send.at[r, d - 1], y_recv.at[r, d - 1], peers[d - 1])
            for d in range(1, chips)
        ]
        for r in range(batch)
    ]

    def piece(ref, row_at, cut=0, cuts_of=1):
        size = ref.shape[-2] // rows
        sub = size // cuts_of
        return pl.ds(pl.multiple_of(row_at * size + cut * sub, sub), sub)

    def w_cross(m, row_at, cut, cuts_of, send, recv):
        src, dst = mats[m]
        at = piece(src, row_at, cut, cuts_of)
        return [
            remote(src.at[at], dst.at[d, core, at], send.at[d - 1], recv.at[d - 1], peers[d - 1])
            for d in range(1, chips)
        ]

    split_cross = [
        [w_cross(m, row, h, cuts[m], g_send.at[m, h], g_recv.at[m, h]) for h in range(cuts[m])] for m in range(2)
    ]
    wcross = [sum(group, []) for group in split_cross]
    far_off = range(ccw[1] + 1, rows - cw[1])
    extras = sum([w_cross(1, ring_row(pos + o, rows), 0, 1, e_send.at[o], e_recv.at[o]) for o in far_off], [])
    shards = [
        remote(mats[m][0], mats[m][1].at[0, core], sh_send.at[m], sh_recv.at[m], partner) for m in range(2)
    ]

    def place_of(s, way):
        return ring_row(pos - s if way == 0 else pos + s, rows)

    def ring_copy(m, s, way, h):
        buf = mats[m][1]
        ref = buf.at[1:, core, piece(buf, place_of(s - 1, way), h, cuts[m])]
        return remote(ref, ref, r_send.at[m, s, way, h], r_recv.at[m, s, way, h], nxt if way == 0 else prv)

    def hand_over(m, s, way, h):
        buf = mats[m][1]
        ref = buf.at[1:, core, piece(buf, place_of(s, way), h, cuts[m])]
        return remote(ref, ref, k_send.at[m, s, way, h], k_recv.at[m, s, way, h], partner)

    def ways(m, s):
        return range(2 if s <= ccw[m] else 1)

    def hop(m, s, h=0):
        if s > cw[m] + 1 or h >= cuts[m]:
            return
        if s == 1:
            for copy in split_cross[m][h]:
                copy.wait_recv()
        else:
            for way in ways(m, s - 1):
                ring_copy(m, s - 1, way, h).wait_recv()
        if s <= cw[m]:
            for way in ways(m, s):
                ring_copy(m, s, way, h).start()
        for way in ways(m, s - 1) if s > 1 else range(1):
            hand_over(m, s - 1, way, h).start()

    def extra_over(o):
        buf = mats[1][1]
        ref = buf.at[1:, core, piece(buf, place_of(o, 1))]
        return remote(ref, ref, l_send.at[o], l_recv.at[o], partner)

    def take_extras():
        for copy in extras:
            copy.wait_recv()
        for o in far_off:
            extra_over(o).start()

    def all_over(m):
        copies = [hand_over(m, 0, 0, h) for h in range(cuts[m])]
        for s in range(1, cw[m] + 1):
            copies += [hand_over(m, s, way, h) for way in ways(m, s) for h in range(cuts[m])]
        if m == 1:
            copies += [extra_over(o) for o in far_off]
        return copies

    def gathered(m):
        for copy in all_over(m):
            copy.wait_recv()

    def sent(m):
        for copy in wcross[m] + all_over(m) + (extras if m == 1 else []):
            copy.wait_send()
        for s in range(1, cw[m] + 1):
            for way in ways(m, s):
                for h in range(cuts[m]):
                    ring_copy(m, s, way, h).wait_send()

    mine_at, other_at = pl.multiple_of(core * per, per), pl.multiple_of((1 - core) * per, per)

    def mix_out(r, p):
        cols = pl.ds(pl.multiple_of(core * half + p * PAIR, PAIR), PAIR)
        dst = mixtok.at[pl.ds(pl.multiple_of(r * per, per), per), cols]
        return (
            remote(mix_s.at[r, p, pl.ds(other_at, per)], dst, mx_send.at[r, p], mx_recv.at[r, p], partner),
            pltpu.make_async_copy(mix_s.at[r, p, pl.ds(mine_at, per)], dst, f_sem.at[r, p]),
        )

    def attention(pks, pvs, s0, s1, s2, s3, oa, pst_a, pst_b, qe, kea, keb, xraw):
        x_load = pltpu.make_async_copy(x_own, xraw, load_sem.at[3 + batch])
        loads = [
            pltpu.make_async_copy(wq.at[:, pl.ds(col, half)], wqkv.at[:, 0:half], load_sem.at[4 + batch]),
            pltpu.make_async_copy(wk.at[:, pl.ds(col, half)], wqkv.at[:, half : 2 * half], load_sem.at[5 + batch]),
            pltpu.make_async_copy(wv.at[:, pl.ds(col, half)], wqkv.at[:, 2 * half : 3 * half], load_sem.at[6 + batch]),
            pltpu.make_async_copy(pkey.at[:, pl.ds(col, half)], pks, load_sem.at[7 + batch]),
            pltpu.make_async_copy(pval.at[:, pl.ds(col, half)], pvs, load_sem.at[8 + batch]),
        ]
        barrier = pltpu.get_barrier_semaphore()
        friends = [partner] + plane + peers
        for dev in friends:
            pl.semaphore_signal(barrier, inc=1, device_id=dev, device_id_type=MESH)
        x_load.start()
        for copy in loads:
            copy.start()
        pl.semaphore_wait(barrier, len(friends))
        for group in wcross:
            for copy in group:
                copy.start()
        x_load.wait()
        for r in range(batch):
            xbuf[r, 0, core] = xraw[:, r, :]
        x_pair.start()
        for group in cross + [extras]:
            for copy in group:
                copy.start()
        for copy in shards + far_loads:
            copy.start()

        term = lax.broadcasted_iota(jnp.int32, (PAIR, 1), 0)
        term = jnp.where(term >= E, term - E, term)

        def key_terms(seg):
            off = jnp.where(jnp.logical_and(term < SEGS, seg != term), -BIG, 0.0)
            return off.T.astype(BF)

        for r in range(batch):
            for d in range(chips):
                at = pl.multiple_of(lax.rem(chip + d, chips) * tpc, tpc)
                seg = segs[r : r + 1, pl.ds(at, tpc)]
                if d == 0:
                    kea[r] = key_terms(seg)
                    on = jnp.logical_or(term == SEGS, jnp.logical_and(term < SEGS, seg == term))
                    qe[r] = jnp.where(on, 1.0, 0.0).T.astype(BF)
                else:
                    keb[r, (d - 1) * tpc : d * tpc] = key_terms(seg)
            unseen = jnp.logical_and(term == SEGS, vis[r : r + 1, :] == 0)
            keb[r, rem:] = jnp.where(unseen, -BIG, 0.0).T.astype(BF)

        def project(r, d, cb, with_q):
            x = xbuf[r, d, cb]
            if with_q:
                q = (dot(x, wqkv[:, 0:half]) * 0.125).astype(BF)
                for p in range(pairs):
                    q_s[r, p, pl.ds(pl.multiple_of(cb * per, per), per), :] = q[:, p * PAIR : (p + 1) * PAIR]
            for ref_a, ref_b, at in ((ka, kb, 1), (va, vb, 2)):
                y = dot(x, wqkv[:, at * half : (at + 1) * half]).astype(BF)
                for p in range(pairs):
                    val = y[:, p * PAIR : (p + 1) * PAIR]
                    if with_q:
                        ref_a[r, p, pl.ds(pl.multiple_of(cb * per, per), per), :] = val
                    else:
                        ref_b[r, p, pl.ds(pl.multiple_of((d - 1) * tpc + cb * per, per), per), :] = val

        for copy in loads:
            copy.wait()
        for r in range(batch):
            for p in range(pairs):
                kb[r, p, rem:, :] = pks[:, p * PAIR : (p + 1) * PAIR]
                vb[r, p, rem:, :] = pvs[:, p * PAIR : (p + 1) * PAIR]

        @pl.loop(0, 2 * batch)
        def _(i):
            pl.when(i == batch)(x_pair.wait_recv)
            late = lax.div(i, batch)
            project(lax.rem(i, batch), 0, core + late - 2 * core * late, True)

        hop(0, 1)
        bufs = (s0, s1, s2, s3)

        def score(r, p, h, k_s, kext, buf):
            keys = k_s.shape[2]
            mine = lanes() < E if h == 0 else lanes() >= E
            q = jnp.where(mine, q_s[r, p], qe[r])
            k = jnp.where(mine, k_s[r, p], kext[r])
            buf[:, 0:keys] = dot(q, k, NT)

        def unit(r, p, after, u, k_s, v_s, kext, pst, p_hbm, finish, wait_slot):
            keys = k_s.shape[2]
            copy = pltpu.make_async_copy(pst.at[u], p_hbm.at[r, p], p_sem.at[u])
            pl.when(wait_slot)(copy.wait)
            tops, sums = [], []
            for h in range(2):
                score(after[0], after[1], h, k_s, kext, bufs[2 * (1 - u) + h])
                s = bufs[2 * u + h][:, 0:keys]
                top = jnp.max(s, axis=1, keepdims=True)
                prob = jnp.exp(s - top).astype(BF)
                pst[u, h] = prob
                mine = lanes() < E if h == 0 else lanes() >= E
                v = jnp.where(mine, v_s[r, p], jnp.ones((1, PAIR), BF))
                sums.append(dot(prob, v))
                tops.append(top)
            copy.start()
            low = lanes() < E
            finish(
                r,
                p,
                jnp.where(low, sums[0], sums[1]),
                pltpu.roll(jnp.where(low, sums[1], sums[0]), E, 1),
                jnp.where(low, tops[0], tops[1]),
            )

        def finish_a(r, p, o, l, m):
            oa[r, p], la[r, p], ma[r, p] = o, l, m

        def finish_b(r, p, o, l, m):
            top = jnp.maximum(ma[r, p], m)
            w_a, w_b = jnp.exp(ma[r, p] - top), jnp.exp(m - top)
            inv = 1.0 / (w_a * la[r, p] + w_b * l)
            r_a, r_b = w_a * inv, w_b * inv
            mix_s[r, p] = (oa[r, p] * r_a + o * r_b).astype(BF)
            la[r, p], ma[r, p] = r_a, r_b

        def drain(pst, p_hbm):
            for u in range(2):
                pltpu.make_async_copy(pst.at[u], p_hbm.at[0, 0], p_sem.at[u]).wait()

        args_a = (ka, va, kea, pst_a, pa_o, finish_a)
        for h in range(2):
            score(0, 0, h, ka, kea, bufs[h])
        count = batch * pairs

        @pl.loop(0, count // 2)
        def _(i):
            for u in range(2):
                j = 2 * i + u
                after = jnp.minimum(j + 1, count - 1)
                unit(
                    lax.div(j, pairs), lax.rem(j, pairs), (lax.div(after, pairs), lax.rem(after, pairs)),
                    u, *args_a, i > 0,
                )

            @pl.when(i == 2)
            def _():
                hop(1, 1)

        drain(pst_a, pa_o)
        hop(0, 2)
        hop(1, 2)

        args_b = (kb, vb, keb, pst_b, pb_o, finish_b)

        @pl.loop(0, batch)
        def _(r):
            for d in range(1, chips):
                remote(
                    xbuf.at[r, 0, core], xbuf.at[r, d, core], y_send.at[r, d - 1], y_recv.at[r, d - 1], peers[d - 1]
                ).wait_recv()
            forward = remote(
                xbuf.at[r, 1:, core], xbuf.at[r, 1:, core], d_send.at[r], d_recv.at[r], partner
            )
            forward.start()

            @pl.loop(0, 2 * (chips - 1))
            def _(i):
                pl.when(i == chips - 1)(forward.wait_recv)
                late = lax.div(i, chips - 1)
                project(r, lax.rem(i, chips - 1) + 1, core + late - 2 * core * late, False)

            @pl.when(r == 0)
            def _():
                hop(0, 3)

            @pl.when(r == 1)
            def _():
                hop(0, 4)

            for h in range(2):
                score(r, 0, h, kb, keb, bufs[h])

            @pl.loop(0, pairs // 2)
            def _(i):
                for u in range(2):
                    p = 2 * i + u
                    unit(r, p, (r, jnp.minimum(p + 1, pairs - 1)), u, *args_b, i > 0)

            drain(pst_b, pb_o)
            for p in range(pairs):
                for copy in mix_out(r, p):
                    copy.start()
            forward.wait_send()

            @pl.when(r == 0)
            def _():
                hop(1, 3)

        for s in range(5, cw[0] + 1):
            hop(0, s)
        hop(1, 4)
        take_extras()
        x_pair.wait_send()

    vm = pltpu.VMEM
    keys = max(tpc, keys_b)
    pl.run_scoped(
        attention,
        vm((P_SIZE, half), BF),
        vm((P_SIZE, half), BF),
        *([vm((tpc, keys), F32)] * 4),
        vm((batch, pairs, tpc, PAIR), F32),
        vm((2, 2, tpc, tpc), BF),
        vm((2, 2, tpc, keys_b), BF),
        vm((batch, tpc, PAIR), BF),
        vm((batch, tpc, PAIR), BF),
        vm((batch, keys_b, PAIR), BF),
        vm((per, batch, width), BF),
    )

    tile = min(512, hidden)
    tiles = hidden // tile
    total = 2 * chips * tiles
    chunk = 64

    def fetch(pin, p_hbm, r, p, u):
        return pltpu.make_async_copy(p_hbm.at[r, p], pin.at[u], p_sem.at[u])

    def feed_forward(ogs, gst, sc1, inv1, acc, slope, pre0, pre1, bst):
        nl = mixtok
        og_loads = [pltpu.make_async_copy(og.at[:, r], ogs.at[r], load_sem.at[3 + r]) for r in range(batch)]
        for copy in og_loads:
            copy.start()
        for u in range(2):
            fetch(pin_b, pb_o, 0, u, u).start()
        for copy in far_loads:
            copy.wait()
        for r in range(batch):
            for p in range(pairs):
                for copy in mix_out(r, p):
                    copy.wait()

        @pl.loop(0, width // 256)
        def _(j):
            at = pl.ds(pl.multiple_of(j * 256, 256), 256)
            acc[:, at] = dot(mixtok[...], wo[:, at])

        def by_rows(body):
            for r in range(batch):

                @pl.loop(0, per // chunk, unroll=min(2, per // chunk))
                def _(i, r=r):
                    inner = pl.ds(pl.multiple_of(i * chunk, chunk), chunk)
                    body(r, inner, pl.ds(pl.multiple_of(r * per + i * chunk, chunk), chunk))

        def norm_one(r, inner, at):
            z = acc[at] + xbuf[r, 0, core, inner].astype(F32)
            c = z - mean_of(z)
            inv = lax.rsqrt(mean_of(c * c) + norm_eps)
            s = c * inv
            n = s * g1[...] + b1[...]
            nl[at], sc1[at], inv1[at] = n.astype(BF), s, inv
            acc[at] = jnp.zeros_like(z)

        by_rows(norm_one)
        hop(0, cw[0] + 1)
        for copy in shards + og_loads:
            copy.wait()

        def split(j):
            slot = lax.div(j, tiles)
            at = pl.ds(pl.multiple_of(lax.rem(j, tiles) * tile, tile), tile)
            return lax.div(slot, 2), lax.rem(slot, 2), at

        def up_tile(j, buf):
            d, c, at = split(j)
            buf[...] = dot(nl[...], up[d, c, :, at])

        pres = (pre0, pre1)
        up_tile(0, pre0)

        @pl.loop(0, total // 2)
        def _(i):
            @pl.when(i == max(tiles - 1, 0))
            def _():
                gathered(0)

            @pl.when(i == tiles)
            def _():
                gathered(1)

            for u in range(2):
                j = 2 * i + u
                up_tile(jnp.minimum(j + 1, total - 1), pres[1 - u])
                v = pres[u][...]
                cdf = 0.5 * (1.0 + lax.erf(v * root_half))
                a = (v * cdf).astype(BF)
                d, c, at = split(j)
                slope[j] = (cdf + v * jnp.exp(-0.5 * v * v) * inv_root_tau).astype(BF)
                acc[...] += dot(a, dn[d, c, at, :])

        def norm_two(r, inner, at):
            z = sc1[at] * g1[...] + b1[...] + acc[at]
            c = z - mean_of(z)
            inv = lax.rsqrt(mean_of(c * c) + norm_eps)
            s = c * inv
            bst[inner, r, :] = (s * g2[...] + b2[...]).astype(BF)
            t = ogs[r, inner] * g2[...]
            g = inv * (t - mean_of(t) - s * mean_of(t * s))
            gs[at], nl[at] = g, g.astype(BF)
            acc[at] = jnp.zeros_like(z)

        by_rows(norm_two)
        outs = [pltpu.make_async_copy(bst, block_o, out_sem.at[0])]
        outs[0].start()

        def down_back(j, buf):
            d, c, at = split(j)
            buf[...] = dot(nl[...], dn[d, c, at, :], NT)

        down_back(0, pre0)

        @pl.loop(0, total // 2)
        def _(i):
            for u in range(2):
                j = 2 * i + u
                down_back(jnp.minimum(j + 1, total - 1), pres[1 - u])
                g = (pres[u][...] * slope[j].astype(F32)).astype(BF)
                d, c, at = split(j)
                acc[...] += dot(g, up[d, c, :, at], NT)

        def norm_back(r, inner, at):
            t = (gs[at] + acc[at]) * g1[...]
            s = sc1[at]
            g = inv1[at] * (t - mean_of(t) - s * mean_of(t * s))
            gs[at], nl[at] = g, g.astype(BF)

        by_rows(norm_back)
        mine = pl.ds(mine_at, per)
        for side in range(2):
            base = (1 - core) * half if side == 0 else core * half
            g = dot(nl[...], wo[pl.ds(pl.multiple_of(base, half), half), :], NT).astype(BF)
            for p in range(pairs):
                for r in range(batch):
                    val = g[r * per : (r + 1) * per, p * PAIR : (p + 1) * PAIR]
                    if side == 0:
                        gst[r, p] = val
                    else:
                        g_s[r, p, mine, :] = val
            if side == 0:
                sends = [
                    remote(gst.at[r, p], g_s.at[r, p, mine], gm_send.at[r, p], gm_recv.at[r, p], partner)
                    for r in range(batch)
                    for p in range(pairs)
                ]
                for copy in sends:
                    copy.start()
        for copy in sends + outs:
            copy.wait()

    pl.run_scoped(
        feed_forward,
        vm((batch, per, width), F32),
        vm((batch, pairs, per, PAIR), BF),
        vm((tokens, width), F32),
        vm((tokens, 1), F32),
        vm((tokens, width), F32),
        vm((total, tokens, tile), BF),
        vm((tokens, tile), F32),
        vm((tokens, tile), F32),
        vm((per, batch, width), BF),
    )

    def attention_back(pin_a, s0, s1, s2, s3, do0, do1, dq, dks, dvs, half_b, send_b, y_out, send_a):
        bufs, dos = (s0, s1, s2, s3), (do0, do1)

        def first(r, p, u, v_s, scale):
            keys = v_s.shape[2]
            g = g_s[r, p].astype(F32) * scale[r, p]
            do = g.astype(BF)
            dos[u][...] = do
            t = g * mix_s[r, p].astype(F32)
            lane = lanes()
            for h in range(2):
                mine = lane < E if h == 0 else lane >= E
                delta = jnp.sum(jnp.where(mine, t, 0.0), axis=1, keepdims=True)
                hi = delta.astype(BF)
                left = delta - hi.astype(F32)
                mid = left.astype(BF)
                low = (left - mid.astype(F32)).astype(BF)
                at = E if h == 0 else 0
                ext = jnp.where(
                    lane == at, -hi, jnp.where(lane == at + 1, -mid, jnp.where(lane == at + 2, -low, jnp.zeros((1, PAIR), BF)))
                )
                one = jnp.where(jnp.logical_and(lane >= at, lane < at + 3), 1.0, 0.0).astype(BF)
                bufs[2 * u + h][:, 0:keys] = dot(
                    jnp.where(mine, do, ext), jnp.where(mine, v_s[r, p], one), NT
                )

        def second(r, p, u, k_s, pin, start_dq, prefix):
            keys = k_s.shape[2]
            q2, k2, do = q_s[r, p], k_s[r, p], dos[u][...]
            do_t, q_t = do.T, q2.T
            gq, gk, gv = [], [], []
            for h in range(2):
                prob = pin[u, h]
                ds = (prob.astype(F32) * bufs[2 * u + h][:, 0:keys]).astype(BF)
                at = slice(h * E, (h + 1) * E)
                gv.append(dot(do_t[at], prob))
                gk.append(dot(q_t[at], ds))
                gq.append(dot(ds, k2))
            low = lanes() < E
            grad = jnp.where(low, gq[0], gq[1])
            dq[r, p] = grad if start_dq else dq[r, p] + grad
            cols = pl.ds(pl.multiple_of(p * PAIR, PAIR), PAIR)
            for ref, parts, k in ((dks, gk, 0), (dvs, gv, 1)):
                val = jnp.concatenate(parts, axis=0).T
                if prefix:
                    ref[0:rem, cols] = val[:rem].astype(BF)
                    psum[k * P_SIZE : (k + 1) * P_SIZE, cols] += val[rem:]
                else:
                    ref[0:tpc, cols] = val.astype(BF)

        def group(r, k_s, v_s, scale, pin, p_hbm, start_dq, prefix, between=None):
            first(r, 0, 0, v_s, scale)

            @pl.loop(0, pairs // 2)
            def _(i):
                for u in range(2):
                    p = 2 * i + u
                    fetch(pin, p_hbm, r, p, u).wait()
                    first(r, jnp.minimum(p + 1, pairs - 1), 1 - u, v_s, scale)
                    second(r, p, u, k_s, pin, start_dq, prefix)

                    @pl.when(i < pairs // 2 - 1)
                    def _():
                        fetch(pin, p_hbm, r, p + 2, u).start()
                if between is not None:
                    between(r, i)

        def to_inputs(at):
            keys = dot(dks[at], wqkv[:, half : 2 * half], NT)
            return keys + dot(dvs[at], wqkv[:, 2 * half : 3 * half], NT)

        psum[...] = jnp.zeros_like(psum)
        far = range(1, chips)

        def b_copy(r, d):
            return remote(
                send_b.at[r, d - 1], got_b.at[r, d - 1], db_send.at[r, d - 1], db_recv.at[r, d - 1], partner
            )

        def y_copy(r, d):
            return remote(
                y_out.at[r, d - 1], y_in.at[r, d - 1], yb_send.at[r, d - 1], yb_recv.at[r, d - 1], back[d - 1]
            )

        def a_copy(r):
            return remote(send_a.at[r], got_a.at[r], da_send.at[r], da_recv.at[r], partner)

        def token_rows(r):
            return pl.ds(pl.multiple_of(r * per, per), per)

        def out_copy(r):
            return pltpu.make_async_copy(gs.at[token_rows(r)], ig_o.at[:, r], out_sem.at[r])

        @pl.loop(0, batch)
        def _(r):
            group(r, kb, vb, ma, pin_b, pb_o, True, True)

            @pl.when(r + 1 < batch)
            def _():
                for u in range(2):
                    fetch(pin_b, pb_o, r + 1, u, u).start()

            @pl.when(r + 1 == batch)
            def _():
                for u in range(2):
                    fetch(pin_a, pa_o, 0, u, u).start()

            for d in far:
                at = pl.ds(pl.multiple_of((d - 1) * tpc + (1 - core) * per, per), per)
                send_b[r, d - 1] = to_inputs(at).astype(BF)
                b_copy(r, d).start()
            for d in far:
                at = pl.ds(pl.multiple_of((d - 1) * tpc + core * per, per), per)
                half_b[d - 1] = to_inputs(at)
            for d in far:
                b_copy(r, d).wait_recv()
                y_out[r, d - 1] = (half_b[d - 1] + got_b[r, d - 1].astype(F32)).astype(BF)
                y_copy(r, d).start()

        size = 2 * P_SIZE // rows

        def part(at):
            return pl.ds(pl.multiple_of(at * size, size), size)

        p_one = [
            remote(psum.at[part(plane[t - 1][0])], pr_in.at[t - 1], p1_send.at[t - 1], p1_recv.at[t - 1], plane[t - 1])
            for t in range(1, rows)
        ]
        p_two = [remote(pr_y.at[0], pr_y.at[d], p2_send.at[d - 1], p2_recv.at[d - 1], peers[d - 1]) for d in far]
        p_three = [
            remote(p_full.at[part(row)], p_full.at[part(row)], p3_send.at[t - 1], p3_recv.at[t - 1], plane[t - 1])
            for t in range(1, rows)
        ]
        cols = pl.ds(col, half)
        p_four = [
            remote(
                p_full.at[k * P_SIZE : (k + 1) * P_SIZE], ref.at[:, cols], p4_send.at[k], p4_recv.at[k], partner
            )
            for k, ref in enumerate((pk_o, pv_o))
        ]
        p_five = [
            pltpu.make_async_copy(p_full.at[k * P_SIZE : (k + 1) * P_SIZE], ref.at[:, cols], out_sem.at[batch + k])
            for k, ref in enumerate((pk_o, pv_o))
        ]
        for copy in p_one:
            copy.start()

        def over_rows():
            for copy in p_one:
                copy.wait_recv()
            total = psum[part(row)]
            for t in range(1, rows):
                total = total + pr_in[t - 1]
            pr_y[0] = total
            for copy in p_two:
                copy.start()

        def over_chips():
            for copy in p_two:
                copy.wait_recv()
            whole = jnp.zeros((size, half), F32)
            for c in range(chips):
                whole = whole + pr_y[lax.rem(c - chip + chips, chips)]
            p_full[part(row)] = whole
            for copy in p_three:
                copy.start()

        def to_all():
            for copy in p_three:
                copy.wait_recv()
            for copy in p_four + p_five:
                copy.start()

        def finish(r):
            a_copy(r).wait_recv()
            val = gs[token_rows(r)] + got_a[r].astype(F32)
            for d in far:
                y_copy(r, d).wait_recv()
                val = val + y_in[r, d - 1].astype(F32)
            gs[token_rows(r)] = val
            out_copy(r).start()

        def between(r, i):
            @pl.when(jnp.logical_and(r == 0, i == 0))
            def _():
                over_rows()

            @pl.when(jnp.logical_and(r == 1, i == 0))
            def _():
                over_chips()

        @pl.loop(0, batch)
        def _(r):
            group(r, ka, va, la, pin_a, pa_o, False, False, between)

            @pl.when(r + 1 < batch)
            def _():
                for u in range(2):
                    fetch(pin_a, pa_o, r + 1, u, u).start()

            for side in range(2):
                block = pl.multiple_of(((1 - core) if side == 0 else core) * per, per)
                at = pl.ds(block, per)
                part_in = to_inputs(at)
                for p in range(pairs):
                    dvs[at, p * PAIR : (p + 1) * PAIR] = (dq[r, p, at, :]).astype(BF)
                val = part_in + 0.125 * dot(dvs[at], wqkv[:, 0:half], NT)
                if side == 0:
                    send_a[r] = val.astype(BF)
                    a_copy(r).start()
                else:
                    gs[token_rows(r)] += val

            @pl.when(r == 1)
            def _():
                to_all()
                finish(0)

        for r in range(1, batch):
            finish(r)
        for r in range(batch):
            a_copy(r).wait_send()
            for d in far:
                b_copy(r, d).wait_send()
                y_copy(r, d).wait_send()
            out_copy(r).wait()
        for copy in p_one + p_two + p_three:
            copy.wait_send()
        for copy in p_four + p_five:
            copy.wait()

    pl.run_scoped(
        attention_back,
        vm((2, 2, tpc, tpc), BF),
        *([vm((tpc, keys), F32)] * 4),
        *([vm((tpc, PAIR), BF)] * 2),
        vm((batch, pairs, tpc, PAIR), F32),
        vm((keys, half), BF),
        vm((keys, half), BF),
        vm((chips - 1, per, width), F32),
        *([vm((batch, chips - 1, per, width), BF)] * 2),
        vm((batch, per, width), BF),
    )
    for r in range(batch):
        for copy in cross[r]:
            copy.wait_send()
    for m in range(2):
        sent(m)


def layer_call(rows, chips, x, segs, vis, wq, wk, wv, pkey, pval, w_out, w_up, w_dn, og, g1, b1, g2, b2):
    per, batch, width = x.shape
    tpc, half = 2 * per, width // 2
    far = chips - 1
    keys_b = far * tpc + P_SIZE
    pairs = half // PAIR
    tokens = batch * per
    steps = rows // 2
    size = 2 * P_SIZE // rows
    out = lambda dt, *s: jax.ShapeDtypeStruct(s, dt)
    shapes = (
        out(BF, batch, pairs, 2, tpc, tpc),
        out(BF, batch, pairs, 2, tpc, keys_b),
        out(BF, per, batch, width),
        out(F32, per, batch, width),
        out(F32, P_SIZE, width),
        out(F32, P_SIZE, width),
    )
    dma = pltpu.SemaphoreType.DMA
    vm = pltpu.VMEM
    scratch = [
        vm((batch, chips, 2, per, width), BF),
        vm((chips, 2, *w_up.shape), BF),
        vm((chips, 2, *w_dn.shape), BF),
        vm((width, width), BF),
        vm((tokens, width), BF),
        vm((batch, pairs, tpc, PAIR), F32),
        vm((batch, pairs, tpc, PAIR), F32),
        vm((batch, pairs, tpc, PAIR), BF),
        vm((batch, pairs, tpc, PAIR), BF),
        vm((tokens, width), F32),
        vm((width, 3 * half), BF),
        vm((batch, pairs, tpc, PAIR), BF),
        vm((batch, pairs, tpc, PAIR), BF),
        vm((batch, pairs, tpc, PAIR), BF),
        vm((batch, pairs, keys_b, PAIR), BF),
        vm((batch, pairs, keys_b, PAIR), BF),
        vm((batch, far, per, width), BF),
        vm((batch, far, per, width), BF),
        vm((batch, per, width), BF),
        vm((2 * P_SIZE, half), F32),
        vm((rows - 1, size, half), F32),
        vm((chips, size, half), F32),
        vm((2 * P_SIZE, half), F32),
        vm((2, 2, tpc, keys_b), BF),
        dma((9 + batch,)), dma((5,)), dma((2,)), dma, dma,
        dma((batch, far)), dma((batch, far)),
        dma((batch,)), dma((batch,)),
        dma((batch, pairs)), dma((batch, pairs)),
        dma((batch, pairs)), dma((batch, pairs)),
        dma((2, 2, far)), dma((2, 2, far)),
        dma((rows, far)), dma((rows, far)),
        dma((2,)), dma((2,)),
        dma((2, steps + 1, 2, 2)), dma((2, steps + 1, 2, 2)),
        dma((2, steps + 1, 2, 2)), dma((2, steps + 1, 2, 2)),
        dma((rows,)), dma((rows,)),
        dma((batch, pairs)), dma((batch, pairs)),
        dma((batch, far)), dma((batch, far)),
        dma((batch, far)), dma((batch, far)),
        dma((batch,)), dma((batch,)),
        dma((rows - 1,)), dma((rows - 1,)),
        dma((far,)), dma((far,)),
        dma((rows - 1,)), dma((rows - 1,)),
        dma((2,)), dma((2,)),
    ]
    return pl.pallas_call(
        functools.partial(layer_kernel, rows, chips),
        out_shape=shapes,
        in_specs=[ANY] + [VM] * 2 + [ANY] * 9 + [VM] * 4,
        out_specs=[ANY] * len(shapes),
        scratch_shapes=scratch,
        compiler_params=pltpu.CompilerParams(
            collective_id=0, has_side_effects=True, vmem_limit_bytes=VMEM_LIMIT
        ),
        name="layer",
    )(x, segs, vis, wq, wk, wv, pkey, pval, w_out, w_up, w_dn, og, g1, b1, g2, b2)


def outputs_kernel(pieces, *refs):
    count = len(refs) // 3
    srcs, dsts, bufs, sem = refs[:count], refs[count : 2 * count], refs[2 * count : 3 * count], refs[-1]
    steps = []
    for k in range(count):
        size = srcs[k].shape[0] // pieces[k]
        for i in range(pieces[k]):
            at = slice(i * size, (i + 1) * size)
            steps.append(
                (
                    pltpu.make_async_copy(srcs[k].at[at], bufs[k].at[at], sem.at[0, k, i]),
                    pltpu.make_async_copy(bufs[k].at[at], dsts[k].at[at], sem.at[1, k, i]),
                )
            )
    for read, _ in steps:
        read.start()
    for read, write in steps:
        read.wait()
        write.start()
    for _, write in steps:
        write.wait()


def outputs_call(*arrays):
    pieces = [4 if v.ndim == 3 else 1 for v in arrays]
    return pl.pallas_call(
        functools.partial(outputs_kernel, pieces),
        out_shape=tuple(jax.ShapeDtypeStruct(v.shape, v.dtype) for v in arrays),
        in_specs=[ANY] * len(arrays),
        out_specs=[ANY] * len(arrays),
        scratch_shapes=[pltpu.VMEM(v.shape, v.dtype) for v in arrays]
        + [pltpu.SemaphoreType.DMA((2, len(arrays), 4))],
        name="outputs",
    )(*arrays)


def on_device(
    rows, chips,
    hidden_in, segments, prefix_vis, prefix_key, prefix_value, w_query, w_key, w_value, w_out,
    norm1_gain, norm1_bias, w_up, w_down, norm2_gain, norm2_bias, out_grad,
):
    flat = lambda v: v.reshape(1, -1)
    _, _, block, input_grad, pk_grad, pv_grad = layer_call(
        rows, chips, hidden_in, segments, prefix_vis, w_query, w_key, w_value, prefix_key, prefix_value,
        w_out, w_up, w_down, out_grad, flat(norm1_gain), flat(norm1_bias), flat(norm2_gain), flat(norm2_bias),
    )
    return outputs_call(block, input_grad, pk_grad, pv_grad)


def solution(mesh):
    rows, chips = mesh.shape["rows"], mesh.shape["wide"] // 2
    act = P("wide", "rows", None)
    per_row = P("rows", None)
    in_specs = (
        act, per_row, per_row, *([P()] * 8), P(None, "wide"), P("wide", None), P(), P(), act,
    )
    out_specs = (act, act, P(), P())
    return jax.shard_map(
        functools.partial(on_device, rows, chips),
        mesh=mesh,
        in_specs=in_specs,
        out_specs=out_specs,
        check_vma=False,
    )
```
